512 devices in a mesh: fsdp: 32 (over y, z_lo, core), head: 4 (over z_hi), seq: 4 (over x).
Axes of the slice: x: 4, y: 4, z: 16 (z_hi: 4, z_lo: 4; z = z_hi * 4 + z_lo), core: 2. Of those that a mesh axis runs over, the one named last changes fastest.
Arguments:
- latents: bfloat16 [6144, 6144], P('fsdp', ('head', 'seq')), may hold values from -100 to 100
- train_qkv: bfloat16 [3, 6144, 4096], P(None, 'fsdp', ('head', 'seq')), may hold values from -0.078125 to 0.078125
- ema_qkv: bfloat16 [3, 6144, 4096], P(None, 'fsdp', ('head', 'seq')), may hold values from -0.078125 to 0.078125
- q_gain: float32 [128], replicated, may hold values from 0.8 to 2.5
- k_gain: float32 [128], replicated, may hold values from 0.8 to 2.5
- out_weight: bfloat16 [4096, 6144], P(('head', 'seq')), may hold values from -0.125 to 0.125
- modulation: float32 [8, 3, 6144], replicated, may hold values from -4 to 4
- timestep: int32 [1], replicated, may hold values from 0 to 7
- step: int32 [1], replicated, may hold values from 0 to 7
Outputs:
- block_output: bfloat16 [6144, 6144], P('fsdp', ('head', 'seq'))
The draws below stay inside these ranges and needn't reach their ends.
All inputs are finite; a program needn't handle non-finite values.
Results may differ from the reference program's by a relative error of at most 0.025.
Values may be sent and summed in bfloat16 or wider, within the bound.
No kernel may reach another device: no remote copies, remote signals or barrier semaphores. Data moves between devices by JAX's collectives and lax.ppermute only.
A program may use at most 64 MiB of HBM per device.

```python
import math
import jax
import jax.numpy as jnp
from jax import lax

D = 6144
HD = 128
HEADS_DEV = 2
NSTEPS = 8
HEADS = 32
HC = 4096
S = 6144


def draw_latents(key, part):
    key_rough, key_offset, key_noise, key_rows = jax.random.split(key, 4)
    column = jnp.arange(D, dtype=jnp.float32) / (D - 1)
    rough = jax.random.uniform(key_rough, (D,), jnp.float32, 0.7, 1.3)
    column_scale = jnp.exp(math.log(0.04) + column * math.log(10.0)) * rough
    row_scale = jnp.exp(jax.random.uniform(key_rows, (S, 1), jnp.float32, math.log(0.3), math.log(3.0)))
    offset = jax.random.uniform(key_offset, (S, 1), jnp.float32, -1.5, 1.5)
    noise = jax.random.truncated_normal(key_noise, -4.0, 4.0, (S, D), jnp.float32)
    return (row_scale * column_scale[None, :] * (offset + noise)).astype(jnp.bfloat16)


def draw_modulation(key, part):
    key_first, key_sign, key_size = jax.random.split(key, 3)
    first = 0.7 * jax.random.truncated_normal(key_first, -4.0 / 0.7, 4.0 / 0.7, (NSTEPS, 2, D), jnp.float32)
    signs = jnp.where(jax.random.uniform(key_sign, (NSTEPS, 1, D), jnp.float32) < 0.5, -1.0, 1.0)
    sizes = jnp.exp(jax.random.uniform(key_size, (NSTEPS, 1, D), jnp.float32, math.log(0.5), math.log(4.0)))
    gates = jnp.clip(signs * sizes, -4.0, 4.0)
    return jnp.concatenate([first, gates], axis=1).astype(jnp.float32)


def raised(entries, stream_key, source, target, shards_of, factor):
    owner, partner = [(jnp.arange(entries.shape[position]) // (entries.shape[position] // shards_of)).reshape([-1 if axis == position else 1 for axis in range(entries.ndim)]) for position in (source, target)]
    chosen = jax.random.permutation(stream_key, shards_of)[partner]
    strong = (owner == chosen) | (owner == (partner + shards_of // 2) % shards_of)
    return jnp.where(strong, factor * entries, entries)


def steps_of(own_key, extent, shards, least, largest):
    def one(dim, blocks):
        draws = jax.random.uniform(jax.random.fold_in(jax.random.fold_in(own_key, 6), dim), (blocks,), jnp.float32, least / len(shards), largest / len(shards))
        return jnp.repeat(jnp.exp(draws), extent[dim] // blocks).reshape((-1,) + (1,) * (len(extent) - dim - 1))

    loudness = one(*shards[0])
    for cut in shards[1:]:
        loudness = loudness * one(*cut)
    return loudness


def scatter_about(own_key, extent, deviation, most, shards=(), kind=jnp.bfloat16):
    drawn = deviation * jax.random.normal(own_key, extent, jnp.float32)
    if shards:
        drawn = drawn * steps_of(own_key, extent, shards, -0.22, 0.18)
    return jnp.clip(drawn, -most, most).astype(kind)


def heavy_noise(stream_key, shape, deviation, most, pieces, heavy, kind=jnp.bfloat16):
    array = deviation * jax.random.normal(stream_key, shape, jnp.float32)
    if pieces:
        array = array * steps_of(stream_key, shape, pieces, -0.22, 0.18)
    return jnp.clip(raised(array, jax.random.fold_in(stream_key, 3), *heavy), -most, most).astype(kind)


def setup_inputs(seed: int = 0) -> dict:
    arg_keys = jax.random.split(jax.random.key(seed), 10)
    return {
        "latents": draw_latents(jax.random.fold_in(arg_keys[9], 71), 0),
        "train_qkv": scatter_about(arg_keys[1], (3, D, HC), D ** -0.5, 0.078125, ((1, 32), (2, 16))),
        "ema_qkv": scatter_about(arg_keys[2], (3, D, HC), D ** -0.5, 0.078125, ((1, 32), (2, 16))),
        "q_gain": jnp.clip(jax.random.uniform(arg_keys[3], (HD,), jnp.float32, 0.8, 2.5), 0.8, 2.5),
        "k_gain": jnp.clip(jax.random.uniform(arg_keys[4], (HD,), jnp.float32, 0.8, 2.5), 0.8, 2.5),
        "out_weight": heavy_noise(arg_keys[5], (HC, D), HC ** -0.5, 0.125, ((0, 16),), (0, 1, 16, 2.0)),
        "modulation": draw_modulation(jax.random.fold_in(arg_keys[9], 71), 0),
        "timestep": jax.random.randint(arg_keys[7], (1,), 0, NSTEPS).astype(jnp.int32),
        "step": jax.random.randint(arg_keys[8], (1,), 0, 8).astype(jnp.int32),
    }


def head_norm(projected_part, gain):
    shaped = projected_part.reshape(projected_part.shape[0], HEADS, HD)
    squares = lax.optimization_barrier(jnp.mean(shaped * shaped, axis=2, keepdims=True))
    return (shaped * lax.rsqrt(squares + 1e-06) * gain.astype(jnp.float32)).astype(jnp.bfloat16)

def reference(latents, train_qkv, ema_qkv, q_gain, k_gain, out_weight, modulation, timestep, step):
    stepped = step[0].astype(jnp.float32)
    decay = (1.0 + stepped) / (10.0 + stepped)
    ema_weights = (decay * ema_qkv.astype(jnp.float32) + (1.0 - decay) * train_qkv.astype(jnp.float32)).astype(jnp.bfloat16)
    mod_row = modulation[timestep[0]]
    widened = latents.astype(jnp.float32)
    average = lax.optimization_barrier(jnp.mean(widened, axis=1, keepdims=True))
    centred = widened - average
    variance = lax.optimization_barrier(jnp.mean(centred * centred, axis=1, keepdims=True))
    hidden = (centred * lax.rsqrt(variance + 1e-06) * (1.0 + mod_row[1]) + mod_row[0]).astype(jnp.bfloat16)
    query_proj = jnp.dot(hidden, ema_weights[0], preferred_element_type=jnp.float32)
    key_proj = jnp.dot(hidden, ema_weights[1], preferred_element_type=jnp.float32)
    value_proj = jnp.dot(hidden, ema_weights[2], preferred_element_type=jnp.float32)
    queries = jnp.transpose(head_norm(query_proj, q_gain), (1, 0, 2))
    keys = jnp.transpose(head_norm(key_proj, k_gain), (1, 0, 2))
    values = jnp.transpose(value_proj.astype(jnp.bfloat16).reshape(-1, HEADS, HD), (1, 0, 2))
    scaling = 1.0 / math.sqrt(HD)

    def one_head(operands):
        head_q, head_k, head_v = operands
        scores = jnp.dot(head_q, head_k.T, preferred_element_type=jnp.float32) * scaling
        expo = jnp.exp(scores)
        weights = expo.astype(jnp.bfloat16)
        totals = lax.optimization_barrier(jnp.sum(expo, axis=1))
        numer = jnp.dot(weights, head_v, preferred_element_type=jnp.float32)
        return (numer / totals[:, None]).astype(jnp.bfloat16)
    attended = lax.map(one_head, (queries, keys, values))
    attended = jnp.transpose(attended, (1, 0, 2)).reshape(-1, HC)
    groups = HEADS // HEADS_DEV
    group_width = HEADS_DEV * HD
    attended_groups = jnp.transpose(attended.reshape(S, groups, group_width), (1, 0, 2))
    weight_groups = out_weight.reshape(groups, group_width, D)

    def add_group(total, operands):
        part_rows, part_weight = operands
        term = jnp.dot(part_rows, part_weight, preferred_element_type=jnp.float32).astype(jnp.bfloat16)
        term = lax.optimization_barrier(term)
        return (total + term.astype(jnp.float32), None)
    branch, _ = lax.scan(add_group, jnp.zeros((S, D), jnp.float32), (attended_groups, weight_groups))
    return (widened + mod_row[2][None, :] * branch).astype(jnp.bfloat16)
```

```python
import math

import jax
import jax.numpy as jnp
from jax import lax
from jax.experimental import pallas as pl
from jax.experimental.pallas import tpu as pltpu
from jax.sharding import Mesh
from jax.sharding import PartitionSpec as P

D = 6144
HD = 128
GRID = 4
BF = jnp.bfloat16
F32 = jnp.float32
LOG2E = 1.4426950408889634
TOKENS = ("y", "zl", "core")


def shift(amount):
    return [(i, (i + amount) % GRID) for i in range(GRID)]


def gather_small(shard, axis_name):
    spread = jnp.broadcast_to(shard[None], (GRID,) + shard.shape)
    return lax.all_to_all(spread, axis_name, 0, 0, tiled=True)


def norm_kernel(raw_ref, mod_ref, out_ref):
    blocks = [(s, h) for s in range(GRID) for h in range(GRID)]
    rows, width = raw_ref.shape[2], raw_ref.shape[3]
    total = jnp.zeros((rows, width), F32)
    for s, h in blocks:
        total = total + raw_ref[s, h].astype(F32)
    average = jnp.sum(total, axis=1, keepdims=True) * (1.0 / D)
    squares = jnp.zeros((rows, width), F32)
    for s, h in blocks:
        centred = raw_ref[s, h].astype(F32) - average
        squares = squares + centred * centred
    variance = jnp.sum(squares, axis=1, keepdims=True) * (1.0 / D)
    inverse = lax.rsqrt(variance + 1e-06)
    for s, h in blocks:
        block = h * GRID + s
        centred = raw_ref[s, h].astype(F32) - average
        scale = mod_ref[1, block : block + 1, :]
        move = mod_ref[0, block : block + 1, :]
        out_ref[block] = (centred * inverse * (1.0 + scale) + move).astype(BF)


def project_kernel(hidden_ref, weight_ref, q_gain_ref, k_gain_ref, q_ref, kv_ref, acc_ref):
    step = pl.program_id(0)

    @pl.when(step == 0)
    def _():
        acc_ref[...] = jnp.zeros_like(acc_ref)

    for b in range(hidden_ref.shape[0]):
        width = hidden_ref.shape[2]
        for j in range(3):
            acc_ref[j] += jnp.dot(
                hidden_ref[b],
                weight_ref[j, b * width : (b + 1) * width, :],
                preferred_element_type=F32,
            )

    @pl.when(step == pl.num_programs(0) - 1)
    def _():
        for h in range(2):
            part = slice(h * HD, (h + 1) * HD)
            for j, gain_ref in ((0, q_gain_ref), (1, k_gain_ref)):
                values = acc_ref[j, :, part]
                squares = jnp.mean(values * values, axis=1, keepdims=True)
                normed = (values * lax.rsqrt(squares + 1e-06) * gain_ref[...]).astype(BF)
                if j == 0:
                    q_ref[h] = normed
                else:
                    kv_ref[h, 0] = normed
            kv_ref[h, 1] = acc_ref[2, :, part].astype(BF)


def attend_kernel(q_ref, kv_ref, out_ref, k_all, v_all):
    rows = q_ref.shape[1]
    blocks = kv_ref.shape[0]

    @pl.when(pl.program_id(0) == 0)
    def _():
        for b in range(blocks):
            k_all[b * rows : (b + 1) * rows, :] = kv_ref[b, 0]
            v_all[b * rows : (b + 1) * rows, :HD] = kv_ref[b, 1]
        v_all[:, HD:] = jnp.ones((blocks * rows, HD), BF)

    chunk = 512
    both = jnp.zeros((rows, 2 * HD), F32)
    for c in range(blocks * rows // chunk):
        part = slice(c * chunk, (c + 1) * chunk)
        scores = lax.dot_general(
            q_ref[0], k_all[part, :], (((1,), (1,)), ((), ())), preferred_element_type=F32
        )
        weights = jnp.exp2(scores * (LOG2E / math.sqrt(HD))).astype(BF)
        both = both + jnp.dot(weights, v_all[part, :], preferred_element_type=F32)
    out_ref[0, :rows, :] = both[:, :HD].astype(BF)
    totals = both[:, HD:]
    lane = lax.broadcasted_iota(jnp.int32, (HD, HD), 1)
    line = lax.broadcasted_iota(jnp.int32, (HD, HD), 0)
    first = jnp.sum(jnp.where(lane == line, totals[:HD], 0.0), axis=0, keepdims=True)
    rest = rows - HD
    second = jnp.sum(
        jnp.where(lane[:rest] == line[:rest], totals[HD:], 0.0), axis=0, keepdims=True
    )
    sub = lax.broadcasted_iota(jnp.int32, (16, HD), 0)
    first_high = first.astype(BF).astype(F32)
    second_high = second.astype(BF).astype(F32)
    packed = jnp.where(sub == 0, first_high, 0.0)
    packed = jnp.where(sub == 1, second_high, packed)
    packed = jnp.where(sub == 2, first - first_high, packed)
    packed = jnp.where(sub == 3, second - second_high, packed)
    out_ref[0, rows:, :] = packed.astype(BF)


def combine_kernel(parts_ref, out_ref):
    rows = out_ref.shape[0]
    lane = lax.broadcasted_iota(jnp.int32, (HD, HD), 1)
    line = lax.broadcasted_iota(jnp.int32, (HD, HD), 0)
    rest = rows - HD
    for h in range(2):
        numer = jnp.zeros((rows, HD), F32)
        packed = jnp.zeros((16, HD), F32)
        for g in range(GRID):
            numer = numer + parts_ref[2 * g + h, :rows, :].astype(F32)
            packed = packed + parts_ref[2 * g + h, rows:, :].astype(F32)
        first = packed[0:1] + packed[2:3]
        second = packed[1:2] + packed[3:4]
        first = jnp.sum(jnp.where(lane == line, first, 0.0), axis=1, keepdims=True)
        second = jnp.sum(
            jnp.where(lane[:rest] == line[:rest], second, 0.0), axis=1, keepdims=True
        )
        part = slice(h * HD, (h + 1) * HD)
        out_ref[:HD, part] = (numer[:HD] / first).astype(BF)
        out_ref[HD:, part] = (numer[HD:] / second).astype(BF)


def branch_kernel(a0, a1, a2, a3, w0, w1, w2, w3, out_ref):
    total = jnp.dot(a0[...], w0[0], preferred_element_type=F32)
    for a, w in ((a1, w1), (a2, w2), (a3, w3)):
        total = total + jnp.dot(a[...], w[0], preferred_element_type=F32)
    out_ref[0] = total.astype(BF)


def per_device(latents, train_qkv, ema_qkv, q_gain, k_gain, out_weight, modulation, timestep, step):
    rows, width = latents.shape
    channels = ema_qkv.shape[2]
    blocks = GRID * GRID
    stepped = step[0].astype(F32)
    decay = (1.0 + stepped) / (10.0 + stepped)
    ema_weights = (decay * ema_qkv.astype(F32) + (1.0 - decay) * train_qkv.astype(F32)).astype(BF)
    full_weights = lax.all_gather(ema_weights, TOKENS, axis=1, tiled=True)

    seq_here = lax.axis_index("seq")
    by_seq = jnp.transpose(out_weight.reshape(channels, GRID, GRID, width), (2, 1, 0, 3))
    out_parts = [
        lax.ppermute(
            lax.dynamic_index_in_dim(by_seq, (seq_here + k) % GRID, 0, keepdims=False), "seq", shift(k)
        )
        if k
        else lax.dynamic_index_in_dim(by_seq, seq_here, 0, keepdims=False)
        for k in range(GRID)
    ]

    mod_row = lax.dynamic_index_in_dim(modulation, timestep[0], 0, keepdims=False)
    raw = gather_small(latents, "head")
    raw = gather_small(raw, "seq").reshape(GRID, GRID, rows, width)
    hidden = pl.pallas_call(
        norm_kernel,
        out_shape=jax.ShapeDtypeStruct((blocks, rows, width), BF),
        name="norm",
    )(raw, mod_row.reshape(3, blocks, width))

    per_step = 2
    queries, pairs = pl.pallas_call(
        project_kernel,
        grid=(blocks // per_step,),
        in_specs=[
            pl.BlockSpec((per_step, rows, width), lambda i: (i, 0, 0)),
            pl.BlockSpec((3, per_step * width, channels), lambda i: (0, i, 0)),
            pl.BlockSpec((1, HD), lambda i: (0, 0)),
            pl.BlockSpec((1, HD), lambda i: (0, 0)),
        ],
        out_specs=[
            pl.BlockSpec((2, rows, HD), lambda i: (0, 0, 0)),
            pl.BlockSpec((2, 2, rows, HD), lambda i: (0, 0, 0, 0)),
        ],
        out_shape=[
            jax.ShapeDtypeStruct((2, rows, HD), BF),
            jax.ShapeDtypeStruct((2, 2, rows, HD), BF),
        ],
        scratch_shapes=[pltpu.VMEM((3, rows, channels), F32)],
        name="project",
    )(hidden, full_weights, q_gain.reshape(1, HD), k_gain.reshape(1, HD))

    pairs = jnp.broadcast_to(pairs[None], (GRID,) + pairs.shape).reshape(2 * GRID, 2, rows, HD)
    pairs = lax.all_to_all(pairs, ("y", "core"), 0, 0, tiled=True)
    queries = jnp.broadcast_to(queries[None], (GRID,) + queries.shape).reshape(2 * GRID, rows, HD)
    queries = lax.all_to_all(queries, ("zl", "core"), 0, 0, tiled=True)

    sent = rows + 16
    parts = pl.pallas_call(
        attend_kernel,
        grid=(2 * GRID,),
        in_specs=[
            pl.BlockSpec((1, rows, HD), lambda i: (i, 0, 0)),
            pl.BlockSpec((2 * GRID, 2, rows, HD), lambda i: (0, 0, 0, 0)),
        ],
        out_specs=pl.BlockSpec((1, sent, HD), lambda i: (i, 0, 0)),
        out_shape=jax.ShapeDtypeStruct((2 * GRID, sent, HD), BF),
        scratch_shapes=[
            pltpu.VMEM((2 * GRID * rows, HD), BF),
            pltpu.VMEM((2 * GRID * rows, 2 * HD), BF),
        ],
        name="attend",
    )(queries, pairs)
    parts = lax.all_to_all(parts, ("zl", "core"), 0, 0, tiled=True)
    attended = pl.pallas_call(
        combine_kernel,
        out_shape=jax.ShapeDtypeStruct((rows, channels), BF),
        name="combine",
    )(parts)

    around = [attended] + [lax.ppermute(attended, "seq", shift(k)) for k in (1, 2, 3)]
    branch = pl.pallas_call(
        branch_kernel,
        grid=(GRID,),
        in_specs=[pl.BlockSpec((rows, channels), lambda i: (0, 0))] * GRID
        + [pl.BlockSpec((1, channels, width), lambda i: (i, 0, 0))] * GRID,
        out_specs=pl.BlockSpec((1, rows, width), lambda i: (i, 0, 0)),
        out_shape=jax.ShapeDtypeStruct((GRID, rows, width), BF),
        name="branch",
    )(*around, *out_parts)
    branch = lax.all_to_all(branch, "head", 0, 0, tiled=True)
    summed = jnp.sum(branch.astype(F32), axis=0)
    position = lax.axis_index(("head", "seq")) * width
    gate = lax.dynamic_slice_in_dim(mod_row[2], position, width, 0)
    return (latents.astype(F32) + gate[None, :] * summed).astype(BF)


def solution(mesh):
    fine = Mesh(
        mesh.devices.reshape(GRID, GRID, 2, GRID, GRID), ("y", "zl", "core", "head", "seq")
    )
    in_specs = (
        P(TOKENS, ("head", "seq")),
        P(None, TOKENS, ("head", "seq")),
        P(None, TOKENS, ("head", "seq")),
        P(),
        P(),
        P(("head", "seq"), None),
        P(),
        P(),
        P(),
    )
    out_specs = P(TOKENS, ("head", "seq"))
    return jax.shard_map(
        per_device, mesh=fine, in_specs=in_specs, out_specs=out_specs, check_vma=False
    )
```

```python
import math

import jax
import jax.numpy as jnp
from jax import lax
from jax.experimental import pallas as pl
from jax.experimental.pallas import tpu as pltpu
from jax.sharding import Mesh
from jax.sharding import PartitionSpec as P

D = 6144
HD = 128
GRID = 4
BF = jnp.bfloat16
F32 = jnp.float32
LOG2E = 1.4426950408889634
TOKENS = ("y", "zl", "core")


def shift(amount):
    return [(i, (i + amount) % GRID) for i in range(GRID)]


def gather_small(shard, axis_name):
    spread = jnp.broadcast_to(shard[None], (GRID,) + shard.shape)
    return lax.all_to_all(spread, axis_name, 0, 0, tiled=True)


def norm_kernel(raw_ref, mod_ref, out_ref):
    blocks = [(s, h) for s in range(GRID) for h in range(GRID)]
    rows, width = raw_ref.shape[2], raw_ref.shape[3]
    total = jnp.zeros((rows, width), F32)
    for s, h in blocks:
        total = total + raw_ref[s, h].astype(F32)
    average = jnp.sum(total, axis=1, keepdims=True) * (1.0 / D)
    squares = jnp.zeros((rows, width), F32)
    for s, h in blocks:
        centred = raw_ref[s, h].astype(F32) - average
        squares = squares + centred * centred
    variance = jnp.sum(squares, axis=1, keepdims=True) * (1.0 / D)
    inverse = lax.rsqrt(variance + 1e-06)
    for s, h in blocks:
        block = h * GRID + s
        centred = raw_ref[s, h].astype(F32) - average
        scale = mod_ref[1, block : block + 1, :]
        move = mod_ref[0, block : block + 1, :]
        out_ref[block] = (centred * inverse * (1.0 + scale) + move).astype(BF)


def project_kernel(hidden_ref, weight_ref, q_gain_ref, k_gain_ref, q_ref, kv_ref, acc_ref):
    step = pl.program_id(0)

    @pl.when(step == 0)
    def _():
        acc_ref[...] = jnp.zeros_like(acc_ref)

    for b in range(hidden_ref.shape[0]):
        width = hidden_ref.shape[2]
        for j in range(3):
            acc_ref[j] += jnp.dot(
                hidden_ref[b],
                weight_ref[j, b * width : (b + 1) * width, :],
                preferred_element_type=F32,
            )

    @pl.when(step == pl.num_programs(0) - 1)
    def _():
        for h in range(2):
            part = slice(h * HD, (h + 1) * HD)
            for j, gain_ref in ((0, q_gain_ref), (1, k_gain_ref)):
                values = acc_ref[j, :, part]
                squares = jnp.mean(values * values, axis=1, keepdims=True)
                normed = (values * lax.rsqrt(squares + 1e-06) * gain_ref[...]).astype(BF)
                if j == 0:
                    q_ref[h] = normed
                else:
                    kv_ref[h, 0] = normed
            kv_ref[h, 1] = acc_ref[2, :, part].astype(BF)


def attend_kernel(line_ref, q_ref, kv_ref, out_ref, k_all, v_all):
    rows = q_ref.shape[1]
    blocks = kv_ref.shape[0]

    @pl.when(pl.program_id(0) == 0)
    def _():
        for b in range(blocks):
            k_all[b * rows : (b + 1) * rows, :] = kv_ref[b, 0]
            v_all[b * rows : (b + 1) * rows, :HD] = kv_ref[b, 1]
        v_all[:, HD:] = jnp.ones((blocks * rows, HD), BF)

    chunk = 512
    both = jnp.zeros((rows, 2 * HD), F32)
    for c in range(blocks * rows // chunk):
        part = slice(c * chunk, (c + 1) * chunk)
        scores = lax.dot_general(
            q_ref[0], k_all[part, :], (((1,), (1,)), ((), ())), preferred_element_type=F32
        )
        weights = jnp.exp2(scores * (LOG2E / math.sqrt(HD))).astype(BF)
        both = both + jnp.dot(weights, v_all[part, :], preferred_element_type=F32)
    out_ref[0, :rows, :] = both[:, :HD].astype(BF)
    totals = both[:, HD:]
    lane = lax.broadcasted_iota(jnp.int32, (HD, HD), 1)
    line = lax.broadcasted_iota(jnp.int32, (HD, HD), 0)
    first = jnp.sum(jnp.where(lane == line, totals[:HD], 0.0), axis=0, keepdims=True)
    rest = rows - HD
    second = jnp.sum(
        jnp.where(lane[:rest] == line[:rest], totals[HD:], 0.0), axis=0, keepdims=True
    )
    sub = lax.broadcasted_iota(jnp.int32, (16, HD), 0)
    first_high = first.astype(BF).astype(F32)
    second_high = second.astype(BF).astype(F32)
    packed = jnp.where(sub == 0, first_high, 0.0)
    packed = jnp.where(sub == 1, second_high, packed)
    packed = jnp.where(sub == 2, first - first_high, packed)
    packed = jnp.where(sub == 3, second - second_high, packed)
    out_ref[0, rows:, :] = packed.astype(BF)


def combine_kernel(parts_ref, out_ref):
    rows = out_ref.shape[0]
    lane = lax.broadcasted_iota(jnp.int32, (HD, HD), 1)
    line = lax.broadcasted_iota(jnp.int32, (HD, HD), 0)
    rest = rows - HD
    for h in range(2):
        numer = jnp.zeros((rows, HD), F32)
        packed = jnp.zeros((16, HD), F32)
        for g in range(GRID):
            numer = numer + parts_ref[2 * g + h, :rows, :].astype(F32)
            packed = packed + parts_ref[2 * g + h, rows:, :].astype(F32)
        first = packed[0:1] + packed[2:3]
        second = packed[1:2] + packed[3:4]
        first = jnp.sum(jnp.where(lane == line, first, 0.0), axis=1, keepdims=True)
        second = jnp.sum(
            jnp.where(lane[:rest] == line[:rest], second, 0.0), axis=1, keepdims=True
        )
        part = slice(h * HD, (h + 1) * HD)
        out_ref[:HD, part] = (numer[:HD] / first).astype(BF)
        out_ref[HD:, part] = (numer[HD:] / second).astype(BF)


def branch_kernel(a0, a1, a2, a3, w0, w1, w2, w3, out_ref):
    total = jnp.dot(a0[...], w0[0], preferred_element_type=F32)
    for a, w in ((a1, w1), (a2, w2), (a3, w3)):
        total = total + jnp.dot(a[...], w[0], preferred_element_type=F32)
    out_ref[0] = total.astype(BF)


def per_device(latents, train_qkv, ema_qkv, q_gain, k_gain, out_weight, modulation, timestep, step):
    rows, width = latents.shape
    channels = ema_qkv.shape[2]
    blocks = GRID * GRID
    stepped = step[0].astype(F32)
    decay = (1.0 + stepped) / (10.0 + stepped)
    ema_weights = (decay * ema_qkv.astype(F32) + (1.0 - decay) * train_qkv.astype(F32)).astype(BF)
    full_weights = lax.all_gather(ema_weights, TOKENS, axis=1, tiled=True)

    seq_here = lax.axis_index("seq")
    by_seq = jnp.transpose(out_weight.reshape(channels, GRID, GRID, width), (2, 1, 0, 3))
    out_parts = [
        lax.ppermute(
            lax.dynamic_index_in_dim(by_seq, (seq_here + k) % GRID, 0, keepdims=False), "seq", shift(k)
        )
        if k
        else lax.dynamic_index_in_dim(by_seq, seq_here, 0, keepdims=False)
        for k in range(GRID)
    ]

    mod_row = lax.dynamic_index_in_dim(modulation, timestep[0], 0, keepdims=False)
    raw = gather_small(latents, "head")
    raw = gather_small(raw, "seq").reshape(GRID, GRID, rows, width)
    hidden = pl.pallas_call(
        norm_kernel,
        out_shape=jax.ShapeDtypeStruct((blocks, rows, width), BF),
        name="norm",
    )(raw, mod_row.reshape(3, blocks, width))
    hidden, *out_parts = lax.optimization_barrier((hidden, *out_parts))

    per_step = 2
    queries, pairs = pl.pallas_call(
        project_kernel,
        grid=(blocks // per_step,),
        in_specs=[
            pl.BlockSpec((per_step, rows, width), lambda i: (i, 0, 0)),
            pl.BlockSpec((3, per_step * width, channels), lambda i: (0, i, 0)),
            pl.BlockSpec((1, HD), lambda i: (0, 0)),
            pl.BlockSpec((1, HD), lambda i: (0, 0)),
        ],
        out_specs=[
            pl.BlockSpec((2, rows, HD), lambda i: (0, 0, 0)),
            pl.BlockSpec((2, 2, rows, HD), lambda i: (0, 0, 0, 0)),
        ],
        out_shape=[
            jax.ShapeDtypeStruct((2, rows, HD), BF),
            jax.ShapeDtypeStruct((2, 2, rows, HD), BF),
        ],
        scratch_shapes=[pltpu.VMEM((3, rows, channels), F32)],
        name="project",
    )(hidden, full_weights, q_gain.reshape(1, HD), k_gain.reshape(1, HD))

    pairs = jnp.broadcast_to(pairs[None], (GRID,) + pairs.shape).reshape(2 * GRID, 2, rows, HD)
    pairs = lax.all_to_all(pairs, ("y", "core"), 0, 0, tiled=True)
    core = lax.axis_index("core")
    own = lax.dynamic_index_in_dim(queries, core, 0, keepdims=False)
    other = lax.dynamic_index_in_dim(queries, 1 - core, 0, keepdims=False)
    other = lax.ppermute(other, "core", [(0, 1), (1, 0)])
    own, other = jnp.where(core == 0, own, other), jnp.where(core == 0, other, own)
    queries = jnp.stack([own, other])
    queries = [queries] + [lax.ppermute(queries, "zl", shift(k)) for k in (1, 2, 3)]
    queries = jnp.concatenate(queries)
    line_here = lax.axis_index("zl").astype(jnp.int32).reshape(1)

    sent = rows + 16
    parts = pl.pallas_call(
        attend_kernel,
        grid_spec=pltpu.PrefetchScalarGridSpec(
            num_scalar_prefetch=1,
            grid=(2 * GRID,),
            in_specs=[
                pl.BlockSpec(
                    (1, rows, HD),
                    lambda i, line: (lax.rem(line[0] + GRID - i // 2, GRID) * 2 + i % 2, 0, 0),
                ),
                pl.BlockSpec((2 * GRID, 2, rows, HD), lambda i, line: (0, 0, 0, 0)),
            ],
            out_specs=pl.BlockSpec((1, sent, HD), lambda i, line: (i, 0, 0)),
            scratch_shapes=[
                pltpu.VMEM((2 * GRID * rows, HD), BF),
                pltpu.VMEM((2 * GRID * rows, 2 * HD), BF),
            ],
        ),
        out_shape=jax.ShapeDtypeStruct((2 * GRID, sent, HD), BF),
        name="attend",
    )(line_here, queries, pairs)
    parts = lax.all_to_all(parts, ("zl", "core"), 0, 0, tiled=True)
    attended = pl.pallas_call(
        combine_kernel,
        out_shape=jax.ShapeDtypeStruct((rows, channels), BF),
        name="combine",
    )(parts)

    around = [attended] + [lax.ppermute(attended, "seq", shift(k)) for k in (1, 2, 3)]
    branch = pl.pallas_call(
        branch_kernel,
        grid=(GRID,),
        in_specs=[pl.BlockSpec((rows, channels), lambda i: (0, 0))] * GRID
        + [pl.BlockSpec((1, channels, width), lambda i: (i, 0, 0))] * GRID,
        out_specs=pl.BlockSpec((1, rows, width), lambda i: (i, 0, 0)),
        out_shape=jax.ShapeDtypeStruct((GRID, rows, width), BF),
        name="branch",
    )(*around, *out_parts)
    branch = lax.all_to_all(branch, "head", 0, 0, tiled=True)
    summed = jnp.sum(branch.astype(F32), axis=0)
    position = lax.axis_index(("head", "seq")) * width
    gate = lax.dynamic_slice_in_dim(mod_row[2], position, width, 0)
    return (latents.astype(F32) + gate[None, :] * summed).astype(BF)


def solution(mesh):
    fine = Mesh(
        mesh.devices.reshape(GRID, GRID, 2, GRID, GRID), ("y", "zl", "core", "head", "seq")
    )
    in_specs = (
        P(TOKENS, ("head", "seq")),
        P(None, TOKENS, ("head", "seq")),
        P(None, TOKENS, ("head", "seq")),
        P(),
        P(),
        P(("head", "seq"), None),
        P(),
        P(),
        P(),
    )
    out_specs = P(TOKENS, ("head", "seq"))
    return jax.shard_map(
        per_device, mesh=fine, in_specs=in_specs, out_specs=out_specs, check_vma=False
    )
```

```python
import math

import jax
import jax.numpy as jnp
from jax import lax
from jax.experimental import pallas as pl
from jax.experimental.pallas import tpu as pltpu
from jax.sharding import Mesh
from jax.sharding import PartitionSpec as P

D = 6144
HD = 128
GRID = 4
BF = jnp.bfloat16
F32 = jnp.float32
LOG2E = 1.4426950408889634
TOKENS = ("y", "zl", "core")


def shift(amount):
    return [(i, (i + amount) % GRID) for i in range(GRID)]


def gather_small(shard, axis_name):
    spread = jnp.broadcast_to(shard[None], (GRID,) + shard.shape)
    return lax.all_to_all(spread, axis_name, 0, 0, tiled=True)


def norm_kernel(raw_ref, mod_ref, out_ref):
    blocks = [(s, h) for s in range(GRID) for h in range(GRID)]
    rows, width = raw_ref.shape[2], raw_ref.shape[3]
    total = jnp.zeros((rows, width), F32)
    for s, h in blocks:
        total = total + raw_ref[s, h].astype(F32)
    average = jnp.sum(total, axis=1, keepdims=True) * (1.0 / D)
    squares = jnp.zeros((rows, width), F32)
    for s, h in blocks:
        centred = raw_ref[s, h].astype(F32) - average
        squares = squares + centred * centred
    variance = jnp.sum(squares, axis=1, keepdims=True) * (1.0 / D)
    inverse = lax.rsqrt(variance + 1e-06)
    for s, h in blocks:
        block = h * GRID + s
        centred = raw_ref[s, h].astype(F32) - average
        scale = mod_ref[1, block : block + 1, :]
        move = mod_ref[0, block : block + 1, :]
        out_ref[:, block * width : (block + 1) * width] = (
            centred * inverse * (1.0 + scale) + move
        ).astype(BF)


def pick_kernel(seq_ref, *refs):
    for source, target in zip(refs[:GRID], refs[GRID:]):
        target[0] = source[...]


def project_kernel(core_ref, hidden_ref, weight_ref, q_gain_ref, k_gain_ref, own_ref, other_ref, acc_ref):
    step = pl.program_id(0)

    @pl.when(step == 0)
    def _():
        acc_ref[...] = jnp.zeros_like(acc_ref)

    for j in range(3):
        acc_ref[j] += jnp.dot(hidden_ref[...], weight_ref[j], preferred_element_type=F32)

    @pl.when(step == pl.num_programs(0) - 1)
    def _():
        for h in range(2):
            part = slice(h * HD, (h + 1) * HD)
            results = []
            for j, gain_ref in ((0, q_gain_ref), (1, k_gain_ref)):
                values = acc_ref[j, :, part]
                squares = jnp.mean(values * values, axis=1, keepdims=True)
                results.append((values * lax.rsqrt(squares + 1e-06) * gain_ref[...]).astype(BF))
            results.append(acc_ref[2, :, part].astype(BF))

            @pl.when(core_ref[0] == h)
            def _():
                for j in range(3):
                    own_ref[j] = results[j]

            @pl.when(core_ref[0] != h)
            def _():
                for j in range(3):
                    other_ref[j] = results[j]


def attend_kernel(core_ref, q_ref, kv_ref, out_ref, k_all, v_all):
    rows = q_ref.shape[2]
    blocks = kv_ref.shape[0] * 2

    @pl.when(pl.program_id(0) == 0)
    def _():
        for b in range(blocks):
            k_all[b * rows : (b + 1) * rows, :] = kv_ref[b // 2, b % 2, 0]
            v_all[b * rows : (b + 1) * rows, :HD] = kv_ref[b // 2, b % 2, 1]
        v_all[:, HD:] = jnp.ones((blocks * rows, HD), BF)

    chunk = 512
    both = jnp.zeros((rows, 2 * HD), F32)
    for c in range(blocks * rows // chunk):
        part = slice(c * chunk, (c + 1) * chunk)
        scores = lax.dot_general(
            q_ref[0, 0], k_all[part, :], (((1,), (1,)), ((), ())), preferred_element_type=F32
        )
        weights = jnp.exp2(scores * (LOG2E / math.sqrt(HD))).astype(BF)
        both = both + jnp.dot(weights, v_all[part, :], preferred_element_type=F32)
    out_ref[0, :rows, :] = both[:, :HD].astype(BF)
    totals = both[:, HD:]
    lane = lax.broadcasted_iota(jnp.int32, (HD, HD), 1)
    line = lax.broadcasted_iota(jnp.int32, (HD, HD), 0)
    first = jnp.sum(jnp.where(lane == line, totals[:HD], 0.0), axis=0, keepdims=True)
    rest = rows - HD
    second = jnp.sum(
        jnp.where(lane[:rest] == line[:rest], totals[HD:], 0.0), axis=0, keepdims=True
    )
    sub = lax.broadcasted_iota(jnp.int32, (16, HD), 0)
    first_high = first.astype(BF).astype(F32)
    second_high = second.astype(BF).astype(F32)
    packed = jnp.where(sub == 0, first_high, 0.0)
    packed = jnp.where(sub == 1, second_high, packed)
    packed = jnp.where(sub == 2, first - first_high, packed)
    packed = jnp.where(sub == 3, second - second_high, packed)
    out_ref[0, rows:, :] = packed.astype(BF)


def combine_kernel(parts_ref, out_ref):
    rows = out_ref.shape[0]
    lane = lax.broadcasted_iota(jnp.int32, (HD, HD), 1)
    line = lax.broadcasted_iota(jnp.int32, (HD, HD), 0)
    rest = rows - HD
    for h in range(2):
        numer = jnp.zeros((rows, HD), F32)
        packed = jnp.zeros((16, HD), F32)
        for g in range(GRID):
            numer = numer + parts_ref[2 * g + h, :rows, :].astype(F32)
            packed = packed + parts_ref[2 * g + h, rows:, :].astype(F32)
        first = packed[0:1] + packed[2:3]
        second = packed[1:2] + packed[3:4]
        first = jnp.sum(jnp.where(lane == line, first, 0.0), axis=1, keepdims=True)
        second = jnp.sum(
            jnp.where(lane[:rest] == line[:rest], second, 0.0), axis=1, keepdims=True
        )
        part = slice(h * HD, (h + 1) * HD)
        out_ref[:HD, part] = (numer[:HD] / first).astype(BF)
        out_ref[HD:, part] = (numer[HD:] / second).astype(BF)


def branch_kernel(a0, a1, a2, a3, w0, w1, w2, w3, out_ref):
    total = jnp.dot(a0[...], w0[0], preferred_element_type=F32)
    for a, w in ((a1, w1), (a2, w2), (a3, w3)):
        total = total + jnp.dot(a[...], w[0], preferred_element_type=F32)
    out_ref[0] = total.astype(BF)


def per_device(latents, train_qkv, ema_qkv, q_gain, k_gain, out_weight, modulation, timestep, step):
    rows, width = latents.shape
    channels = ema_qkv.shape[2]
    blocks = GRID * GRID
    stepped = step[0].astype(F32)
    decay = (1.0 + stepped) / (10.0 + stepped)
    ema_weights = (decay * ema_qkv.astype(F32) + (1.0 - decay) * train_qkv.astype(F32)).astype(BF)
    full_weights = lax.all_gather(ema_weights, TOKENS, axis=1, tiled=True)

    seq_here = lax.axis_index("seq").astype(jnp.int32).reshape(1)
    core_here = lax.axis_index("core").astype(jnp.int32).reshape(1)

    def column(k):
        return lambda i, seq: (0, i * GRID + lax.rem(seq[0] + k, GRID))

    out_parts = pl.pallas_call(
        pick_kernel,
        grid_spec=pltpu.PrefetchScalarGridSpec(
            num_scalar_prefetch=1,
            grid=(GRID,),
            in_specs=[pl.BlockSpec((channels, width), column(k)) for k in range(GRID)],
            out_specs=[pl.BlockSpec((1, channels, width), lambda i, seq: (i, 0, 0))] * GRID,
        ),
        out_shape=[jax.ShapeDtypeStruct((GRID, channels, width), BF)] * GRID,
        name="pick",
    )(seq_here, *([out_weight] * GRID))
    out_parts = [out_parts[0]] + [lax.ppermute(out_parts[k], "seq", shift(k)) for k in (1, 2, 3)]

    mod_row = lax.dynamic_index_in_dim(modulation, timestep[0], 0, keepdims=False)
    raw = gather_small(latents, "head")
    raw, *out_parts = lax.optimization_barrier((raw, *out_parts))
    raw = gather_small(raw, "seq").reshape(GRID, GRID, rows, width)
    hidden = pl.pallas_call(
        norm_kernel,
        out_shape=jax.ShapeDtypeStruct((rows, blocks * width), BF),
        name="norm",
    )(raw, mod_row.reshape(3, blocks, width))

    depth = D // GRID
    own, other = pl.pallas_call(
        project_kernel,
        grid_spec=pltpu.PrefetchScalarGridSpec(
            num_scalar_prefetch=1,
            grid=(GRID,),
            in_specs=[
                pl.BlockSpec((rows, depth), lambda i, core: (0, i)),
                pl.BlockSpec((3, depth, channels), lambda i, core: (0, i, 0)),
                pl.BlockSpec((1, HD), lambda i, core: (0, 0)),
                pl.BlockSpec((1, HD), lambda i, core: (0, 0)),
            ],
            out_specs=[pl.BlockSpec((3, rows, HD), lambda i, core: (0, 0, 0))] * 2,
            scratch_shapes=[pltpu.VMEM((3, rows, channels), F32)],
        ),
        out_shape=[jax.ShapeDtypeStruct((3, rows, HD), BF)] * 2,
        name="project",
    )(core_here, hidden, full_weights, q_gain.reshape(1, HD), k_gain.reshape(1, HD))

    both = jnp.stack([own, lax.ppermute(other, "core", [(0, 1), (1, 0)])])
    queries = gather_small(both[:, 0], "zl").reshape(GRID, 2, rows, HD)
    pairs = gather_small(both[:, 1:], "y").reshape(GRID, 2, 2, rows, HD)

    sent = rows + 16
    parts = pl.pallas_call(
        attend_kernel,
        grid_spec=pltpu.PrefetchScalarGridSpec(
            num_scalar_prefetch=1,
            grid=(2 * GRID,),
            in_specs=[
                pl.BlockSpec(
                    (1, 1, rows, HD), lambda i, core: (i // 2, lax.rem(i + core[0], 2), 0, 0)
                ),
                pl.BlockSpec((GRID, 2, 2, rows, HD), lambda i, core: (0, 0, 0, 0, 0)),
            ],
            out_specs=pl.BlockSpec((1, sent, HD), lambda i, core: (i, 0, 0)),
            scratch_shapes=[
                pltpu.VMEM((2 * GRID * rows, HD), BF),
                pltpu.VMEM((2 * GRID * rows, 2 * HD), BF),
            ],
        ),
        out_shape=jax.ShapeDtypeStruct((2 * GRID, sent, HD), BF),
        name="attend",
    )(core_here, queries, pairs)
    parts = lax.all_to_all(parts, ("zl", "core"), 0, 0, tiled=True)
    attended = pl.pallas_call(
        combine_kernel,
        out_shape=jax.ShapeDtypeStruct((rows, channels), BF),
        name="combine",
    )(parts)

    around = [attended] + [lax.ppermute(attended, "seq", shift(k)) for k in (1, 2, 3)]
    branch = pl.pallas_call(
        branch_kernel,
        grid=(GRID,),
        in_specs=[pl.BlockSpec((rows, channels), lambda i: (0, 0))] * GRID
        + [pl.BlockSpec((1, channels, width), lambda i: (i, 0, 0))] * GRID,
        out_specs=pl.BlockSpec((1, rows, width), lambda i: (i, 0, 0)),
        out_shape=jax.ShapeDtypeStruct((GRID, rows, width), BF),
        name="branch",
    )(*around, *out_parts)
    branch = lax.all_to_all(branch, "head", 0, 0, tiled=True)
    summed = jnp.sum(branch.astype(F32), axis=0)
    position = lax.axis_index(("head", "seq")) * width
    gate = lax.dynamic_slice_in_dim(mod_row[2], position, width, 0)
    return (latents.astype(F32) + gate[None, :] * summed).astype(BF)


def solution(mesh):
    fine = Mesh(
        mesh.devices.reshape(GRID, GRID, 2, GRID, GRID), ("y", "zl", "core", "head", "seq")
    )
    in_specs = (
        P(TOKENS, ("head", "seq")),
        P(None, TOKENS, ("head", "seq")),
        P(None, TOKENS, ("head", "seq")),
        P(),
        P(),
        P(("head", "seq"), None),
        P(),
        P(),
        P(),
    )
    out_specs = P(TOKENS, ("head", "seq"))
    return jax.shard_map(
        per_device, mesh=fine, in_specs=in_specs, out_specs=out_specs, check_vma=False
    )
```

```python
import math

import jax
import jax.numpy as jnp
from jax import lax
from jax.experimental import pallas as pl
from jax.experimental.pallas import tpu as pltpu
from jax.sharding import Mesh
from jax.sharding import PartitionSpec as P

D = 6144
HD = 128
GRID = 4
BF = jnp.bfloat16
F32 = jnp.float32
LOG2E = 1.4426950408889634
TOKENS = ("y", "zl", "core")


def shift(amount):
    return [(i, (i + amount) % GRID) for i in range(GRID)]


def gather_small(shard, axis_name):
    spread = jnp.broadcast_to(shard[None], (GRID,) + shard.shape)
    return lax.all_to_all(spread, axis_name, 0, 0, tiled=True)


def average_kernel(step_ref, ema_ref, train_ref, out_ref):
    stepped = jnp.full((1, HD), step_ref[0], jnp.int32).astype(F32)
    decay = (1.0 + stepped) / (10.0 + stepped)
    for h in range(2):
        for j in range(3):
            part = slice(h * HD, (h + 1) * HD)
            ema = ema_ref[j, :, part].astype(F32)
            train = train_ref[j, :, part].astype(F32)
            out_ref[h, :, j * HD : (j + 1) * HD] = (decay * ema + (1.0 - decay) * train).astype(BF)


def norm_kernel(order_ref, raw_ref, mod_ref, out_ref):
    blocks = [(s, k) for s in range(GRID) for k in range(GRID)]
    rows, width = raw_ref.shape[2], raw_ref.shape[3]
    total = jnp.zeros((rows, width), F32)
    for s, k in blocks:
        total = total + raw_ref[s, k].astype(F32)
    average = jnp.sum(total, axis=1, keepdims=True) * (1.0 / D)
    squares = jnp.zeros((rows, width), F32)
    for s, k in blocks:
        centred = raw_ref[s, k].astype(F32) - average
        squares = squares + centred * centred
    variance = jnp.sum(squares, axis=1, keepdims=True) * (1.0 / D)
    inverse = lax.rsqrt(variance + 1e-06)
    for s, k in blocks:
        h = order_ref[k]
        centred = raw_ref[s, k].astype(F32) - average
        scale = mod_ref[1, h, s : s + 1, :]
        move = mod_ref[0, h, s : s + 1, :]
        start = pl.multiple_of((h * GRID + s) * width, HD)
        out_ref[:, pl.ds(start, width)] = (
            centred * inverse * (1.0 + scale) + move
        ).astype(BF)


def pick_kernel(place_ref, *refs):
    for source, target in zip(refs[:GRID], refs[GRID:]):
        target[0] = source[...]


def project_kernel(core_ref, own_ref, other_ref, weight_ref, q_gain_ref, k_gain_ref, q_ref, kv_ref, acc_ref):
    step = pl.program_id(0)

    @pl.when(step == 0)
    def _():
        acc_ref[...] = jnp.zeros_like(acc_ref)

    for t, hidden_ref in enumerate((own_ref, other_ref)):
        acc_ref[t] += jnp.dot(hidden_ref[...], weight_ref[0], preferred_element_type=F32)

    @pl.when(step == pl.num_programs(0) - 1)
    def _():
        for t in range(2):
            for j, gain_ref in ((0, q_gain_ref), (1, k_gain_ref)):
                values = acc_ref[t, :, j * HD : (j + 1) * HD]
                squares = jnp.mean(values * values, axis=1, keepdims=True)
                normed = (values * lax.rsqrt(squares + 1e-06) * gain_ref[...]).astype(BF)
                if j == 0:
                    q_ref[t] = normed
                else:
                    kv_ref[0, t] = normed
            kv_ref[1, t] = acc_ref[t, :, 2 * HD :].astype(BF)


def attend_kernel(place_ref, q_ref, kv0, kv1, kv2, kv3, out_ref, k_all, v_all):
    rows = q_ref.shape[2]
    blocks = 2 * GRID

    @pl.when(pl.program_id(0) == 0)
    def _():
        for g, kv_ref in enumerate((kv0, kv1, kv2, kv3)):
            for t in range(2):
                part = slice((2 * g + t) * rows, (2 * g + t + 1) * rows)
                k_all[part, :] = kv_ref[0, t]
                v_all[part, :HD] = kv_ref[1, t]
        v_all[:, HD:] = jnp.ones((blocks * rows, HD), BF)

    chunk = 512
    both = jnp.zeros((rows, 2 * HD), F32)
    for c in range(blocks * rows // chunk):
        part = slice(c * chunk, (c + 1) * chunk)
        scores = lax.dot_general(
            q_ref[0, 0], k_all[part, :], (((1,), (1,)), ((), ())), preferred_element_type=F32
        )
        weights = jnp.exp2(scores * (LOG2E / math.sqrt(HD))).astype(BF)
        both = both + jnp.dot(weights, v_all[part, :], preferred_element_type=F32)
    out_ref[0, :rows, :] = both[:, :HD].astype(BF)
    totals = both[:, HD:]
    lane = lax.broadcasted_iota(jnp.int32, (HD, HD), 1)
    line = lax.broadcasted_iota(jnp.int32, (HD, HD), 0)
    first = jnp.sum(jnp.where(lane == line, totals[:HD], 0.0), axis=0, keepdims=True)
    rest = rows - HD
    second = jnp.sum(
        jnp.where(lane[:rest] == line[:rest], totals[HD:], 0.0), axis=0, keepdims=True
    )
    sub = lax.broadcasted_iota(jnp.int32, (16, HD), 0)
    first_high = first.astype(BF).astype(F32)
    second_high = second.astype(BF).astype(F32)
    packed = jnp.where(sub == 0, first_high, 0.0)
    packed = jnp.where(sub == 1, second_high, packed)
    packed = jnp.where(sub == 2, first - first_high, packed)
    packed = jnp.where(sub == 3, second - second_high, packed)
    out_ref[0, rows:, :] = packed.astype(BF)


def combine_kernel(parts_ref, out_ref):
    rows = out_ref.shape[0]
    lane = lax.broadcasted_iota(jnp.int32, (HD, HD), 1)
    line = lax.broadcasted_iota(jnp.int32, (HD, HD), 0)
    rest = rows - HD
    for h in range(2):
        numer = jnp.zeros((rows, HD), F32)
        packed = jnp.zeros((16, HD), F32)
        for g in range(GRID):
            numer = numer + parts_ref[2 * g + h, :rows, :].astype(F32)
            packed = packed + parts_ref[2 * g + h, rows:, :].astype(F32)
        first = packed[0:1] + packed[2:3]
        second = packed[1:2] + packed[3:4]
        first = jnp.sum(jnp.where(lane == line, first, 0.0), axis=1, keepdims=True)
        second = jnp.sum(
            jnp.where(lane[:rest] == line[:rest], second, 0.0), axis=1, keepdims=True
        )
        part = slice(h * HD, (h + 1) * HD)
        out_ref[:HD, part] = (numer[:HD] / first).astype(BF)
        out_ref[HD:, part] = (numer[HD:] / second).astype(BF)


def branch_kernel(place_ref, a0, a1, a2, a3, w0, w1, w2, w3, out_ref):
    total = jnp.dot(a0[...], w0[0], preferred_element_type=F32)
    for a, w in ((a1, w1), (a2, w2), (a3, w3)):
        total = total + jnp.dot(a[...], w[0], preferred_element_type=F32)
    out_ref[...] = total.astype(BF)


def per_device(latents, train_qkv, ema_qkv, q_gain, k_gain, out_weight, modulation, timestep, step):
    rows, width = latents.shape
    channels = ema_qkv.shape[2]
    blocks = GRID * GRID
    by_head = pl.pallas_call(
        average_kernel,
        in_specs=[
            pl.BlockSpec(memory_space=pltpu.SMEM),
            pl.BlockSpec(memory_space=pltpu.VMEM),
            pl.BlockSpec(memory_space=pltpu.VMEM),
        ],
        out_specs=pl.BlockSpec(memory_space=pltpu.VMEM),
        out_shape=jax.ShapeDtypeStruct((2, rows, 3 * HD), BF),
        name="average",
    )(step, ema_qkv, train_qkv)
    full_weights = lax.all_gather(by_head, TOKENS, axis=1, tiled=True)

    place = jnp.stack(
        [lax.axis_index(name).astype(jnp.int32) for name in ("core", "zl", "head", "seq")]
    )

    def column(k):
        return lambda i, place: (0, i * GRID + lax.rem(place[3] + k, GRID))

    out_parts = pl.pallas_call(
        pick_kernel,
        grid_spec=pltpu.PrefetchScalarGridSpec(
            num_scalar_prefetch=1,
            grid=(GRID,),
            in_specs=[pl.BlockSpec((channels, width), column(k)) for k in range(GRID)],
            out_specs=[pl.BlockSpec((1, channels, width), lambda i, place: (i, 0, 0))] * GRID,
        ),
        out_shape=[jax.ShapeDtypeStruct((GRID, channels, width), BF)] * GRID,
        name="pick",
    )(place, *([out_weight] * GRID))

    mod_row = lax.dynamic_index_in_dim(modulation, timestep[0], 0, keepdims=False)
    half = rows // 2
    before = lax.ppermute(latents, "head", shift(1))
    after = lax.ppermute(latents, "head", shift(3))
    far = jnp.concatenate(
        [
            lax.ppermute(before[:half], "head", shift(1)),
            lax.ppermute(after[half:], "head", shift(3)),
        ]
    )
    raw = jnp.stack([latents, before, far, after])
    raw = gather_small(raw, "seq").reshape(GRID, GRID, rows, width)
    raw, *out_parts = lax.optimization_barrier((raw, *out_parts))
    out_parts = [out_parts[0]] + [lax.ppermute(out_parts[k], "seq", shift(k)) for k in (1, 2, 3)]
    head_order = lax.rem(place[2] + GRID - jnp.arange(GRID, dtype=jnp.int32), GRID)
    by_place = mod_row.reshape(3, GRID, GRID, width)
    hidden = pl.pallas_call(
        norm_kernel,
        grid_spec=pltpu.PrefetchScalarGridSpec(
            num_scalar_prefetch=1,
            grid=(1,),
            in_specs=[
                pl.BlockSpec((GRID, GRID, rows, width), lambda i, order: (0, 0, 0, 0)),
                pl.BlockSpec((3, GRID, GRID, width), lambda i, order: (0, 0, 0, 0)),
            ],
            out_specs=pl.BlockSpec((rows, blocks * width), lambda i, order: (0, 0)),
        ),
        out_shape=jax.ShapeDtypeStruct((rows, blocks * width), BF),
        name="norm",
    )(head_order, raw, by_place)
    sibling = lax.ppermute(hidden, "core", [(0, 1), (1, 0)])

    depth = D // GRID
    queries, pairs = pl.pallas_call(
        project_kernel,
        grid_spec=pltpu.PrefetchScalarGridSpec(
            num_scalar_prefetch=1,
            grid=(GRID,),
            in_specs=[
                pl.BlockSpec((rows, depth), lambda i, place: (0, i)),
                pl.BlockSpec((rows, depth), lambda i, place: (0, i)),
                pl.BlockSpec((1, depth, 3 * HD), lambda i, place: (place[0], i, 0)),
                pl.BlockSpec((1, HD), lambda i, place: (0, 0)),
                pl.BlockSpec((1, HD), lambda i, place: (0, 0)),
            ],
            out_specs=[
                pl.BlockSpec((2, rows, HD), lambda i, place: (0, 0, 0)),
                pl.BlockSpec((2, 2, rows, HD), lambda i, place: (0, 0, 0, 0)),
            ],
            scratch_shapes=[pltpu.VMEM((2, rows, 3 * HD), F32)],
        ),
        out_shape=[
            jax.ShapeDtypeStruct((2, rows, HD), BF),
            jax.ShapeDtypeStruct((2, 2, rows, HD), BF),
        ],
        name="project",
    )(place, hidden, sibling, full_weights, q_gain.reshape(1, HD), k_gain.reshape(1, HD))

    all_pairs = [pairs] + [lax.ppermute(pairs, "y", shift(k)) for k in (1, 3, 2)]
    queries = jnp.stack([queries] + [lax.ppermute(queries, "zl", shift(k)) for k in (1, 2, 3)])

    sent = rows + 16
    parts = pl.pallas_call(
        attend_kernel,
        grid_spec=pltpu.PrefetchScalarGridSpec(
            num_scalar_prefetch=1,
            grid=(2 * GRID,),
            in_specs=[
                pl.BlockSpec(
                    (1, 1, rows, HD),
                    lambda i, place: (
                        lax.rem(place[1] + GRID - i // 2, GRID),
                        lax.rem(i + place[0], 2),
                        0,
                        0,
                    ),
                ),
            ]
            + [pl.BlockSpec((2, 2, rows, HD), lambda i, place: (0, 0, 0, 0))] * GRID,
            out_specs=pl.BlockSpec((1, sent, HD), lambda i, place: (i, 0, 0)),
            scratch_shapes=[
                pltpu.VMEM((2 * GRID * rows, HD), BF),
                pltpu.VMEM((2 * GRID * rows, 2 * HD), BF),
            ],
        ),
        out_shape=jax.ShapeDtypeStruct((2 * GRID, sent, HD), BF),
        name="attend",
    )(place, queries, *all_pairs)
    parts, *out_parts = lax.optimization_barrier((parts, *out_parts))
    parts = lax.all_to_all(parts, ("zl", "core"), 0, 0, tiled=True)
    attended = pl.pallas_call(
        combine_kernel,
        out_shape=jax.ShapeDtypeStruct((rows, channels), BF),
        name="combine",
    )(parts)

    around = [attended] + [lax.ppermute(attended, "seq", shift(k)) for k in (1, 2, 3)]

    def branch_for(k):
        return pl.pallas_call(
            branch_kernel,
            grid_spec=pltpu.PrefetchScalarGridSpec(
                num_scalar_prefetch=1,
                grid=(1,),
                in_specs=[pl.BlockSpec((rows, channels), lambda i, place: (0, 0))] * GRID
                + [
                    pl.BlockSpec(
                        (1, channels, width), lambda i, place: (lax.rem(place[2] + k, GRID), 0, 0)
                    )
                ]
                * GRID,
                out_specs=pl.BlockSpec((rows, width), lambda i, place: (0, 0)),
            ),
            out_shape=jax.ShapeDtypeStruct((rows, width), BF),
            name="branch",
        )(place, *around, *out_parts)

    shares = [lax.ppermute(branch_for(k), "head", shift(k)) for k in (2, 1, 3)]
    summed = branch_for(0).astype(F32)
    for share in shares:
        summed = summed + share.astype(F32)
    position = lax.axis_index(("head", "seq")) * width
    gate = lax.dynamic_slice_in_dim(mod_row[2], position, width, 0)
    return (latents.astype(F32) + gate[None, :] * summed).astype(BF)


def solution(mesh):
    fine = Mesh(
        mesh.devices.reshape(GRID, GRID, 2, GRID, GRID), ("y", "zl", "core", "head", "seq")
    )
    in_specs = (
        P(TOKENS, ("head", "seq")),
        P(None, TOKENS, ("head", "seq")),
        P(None, TOKENS, ("head", "seq")),
        P(),
        P(),
        P(("head", "seq"), None),
        P(),
        P(),
        P(),
    )
    out_specs = P(TOKENS, ("head", "seq"))
    return jax.shard_map(
        per_device, mesh=fine, in_specs=in_specs, out_specs=out_specs, check_vma=False
    )
```

```python
import math

import jax
import jax.numpy as jnp
from jax import lax
from jax.experimental import pallas as pl
from jax.experimental.pallas import tpu as pltpu
from jax.sharding import Mesh
from jax.sharding import PartitionSpec as P

D = 6144
HD = 128
GRID = 4
BF = jnp.bfloat16
F32 = jnp.float32
LOG2E = 1.4426950408889634
TOKENS = ("y", "zl", "core")


def shift(amount):
    return [(i, (i + amount) % GRID) for i in range(GRID)]


def gather_small(shard, axis_name):
    spread = jnp.broadcast_to(shard[None], (GRID,) + shard.shape)
    return lax.all_to_all(spread, axis_name, 0, 0, tiled=True)


def average_kernel(step_ref, ema_ref, train_ref, out_ref):
    stepped = jnp.full((1, HD), step_ref[0], jnp.int32).astype(F32)
    decay = (1.0 + stepped) / (10.0 + stepped)
    for h in range(2):
        for j in range(3):
            part = slice(h * HD, (h + 1) * HD)
            ema = ema_ref[j, :, part].astype(F32)
            train = train_ref[j, :, part].astype(F32)
            out_ref[h, :, j * HD : (j + 1) * HD] = (decay * ema + (1.0 - decay) * train).astype(BF)


def norm_kernel(place_ref, raw_ref, mod_ref, out_ref):
    blocks = [(s, k) for s in range(GRID) for k in range(GRID)]
    rows, width = raw_ref.shape[2], raw_ref.shape[3]
    some = 32

    def one_piece(i, carry):
        part = pl.ds(pl.multiple_of(i * some, some), some)
        total = jnp.zeros((some, width), F32)
        for s, k in blocks:
            total = total + raw_ref[s, k, part, :].astype(F32)
        average = jnp.sum(total, axis=1, keepdims=True) * (1.0 / D)
        squares = jnp.zeros((some, width), F32)
        for s, k in blocks:
            centred = raw_ref[s, k, part, :].astype(F32) - average
            squares = squares + centred * centred
        variance = jnp.sum(squares, axis=1, keepdims=True) * (1.0 / D)
        inverse = lax.rsqrt(variance + 1e-06)
        for s, k in blocks:
            h = lax.rem(place_ref[2] + GRID - k, GRID)
            centred = raw_ref[s, k, part, :].astype(F32) - average
            scale = mod_ref[1, h, s : s + 1, :]
            move = mod_ref[0, h, s : s + 1, :]
            start = pl.multiple_of((h * GRID + s) * width, HD)
            out_ref[part, pl.ds(start, width)] = (
                centred * inverse * (1.0 + scale) + move
            ).astype(BF)
        return carry

    lax.fori_loop(0, rows // some, one_piece, 0)


def pick_kernel(place_ref, *refs):
    for source, target in zip(refs[:GRID], refs[GRID:]):
        target[0] = source[...]


def project_kernel(core_ref, own_ref, other_ref, weight_ref, q_gain_ref, k_gain_ref, q_ref, kv_ref, acc_ref):
    step = pl.program_id(0)

    @pl.when(step == 0)
    def _():
        acc_ref[...] = jnp.zeros_like(acc_ref)

    rows = own_ref.shape[0]
    hidden = jnp.concatenate([own_ref[...], other_ref[...]], axis=0)
    acc_ref[...] += jnp.dot(hidden, weight_ref[0], preferred_element_type=F32)

    @pl.when(step == pl.num_programs(0) - 1)
    def _():
        for t in range(2):
            for j, gain_ref in ((0, q_gain_ref), (1, k_gain_ref)):
                values = acc_ref[t * rows : (t + 1) * rows, j * HD : (j + 1) * HD]
                squares = jnp.mean(values * values, axis=1, keepdims=True)
                normed = (values * lax.rsqrt(squares + 1e-06) * gain_ref[...]).astype(BF)
                if j == 0:
                    q_ref[t] = normed
                else:
                    kv_ref[0, t] = normed
            kv_ref[1, t] = acc_ref[t * rows : (t + 1) * rows, 2 * HD :].astype(BF)


def attend_kernel(place_ref, q_ref, kv_ref, out_ref, k_all, v_all):
    rows = q_ref.shape[2]
    blocks = 2 * GRID

    @pl.when(pl.program_id(0) == 0)
    def _():
        for g in range(GRID):
            for t in range(2):
                part = slice((2 * g + t) * rows, (2 * g + t + 1) * rows)
                k_all[part, :] = kv_ref[g, 0, t]
                v_all[part, :HD] = kv_ref[g, 1, t]
        v_all[:, HD:] = jnp.ones((blocks * rows, HD), BF)

    chunk = 512
    queries = jnp.concatenate([q_ref[0, 0], q_ref[0, 1]], axis=0)
    both = jnp.zeros((2 * rows, 2 * HD), F32)
    for c in range(blocks * rows // chunk):
        part = slice(c * chunk, (c + 1) * chunk)
        scores = lax.dot_general(
            queries, k_all[part, :], (((1,), (1,)), ((), ())), preferred_element_type=F32
        )
        weights = jnp.exp2(scores * (LOG2E / math.sqrt(HD))).astype(BF)
        both = both + jnp.dot(weights, v_all[part, :], preferred_element_type=F32)
    lane = lax.broadcasted_iota(jnp.int32, (HD, HD), 1)
    line = lax.broadcasted_iota(jnp.int32, (HD, HD), 0)
    sub = lax.broadcasted_iota(jnp.int32, (16, HD), 0)
    rest = rows - HD
    for t in range(2):
        target = lax.rem(place_ref[0] + t, 2)
        out_ref[target, :rows, :] = both[t * rows : (t + 1) * rows, :HD].astype(BF)
        totals = both[t * rows : (t + 1) * rows, HD:]
        first = jnp.sum(jnp.where(lane == line, totals[:HD], 0.0), axis=0, keepdims=True)
        second = jnp.sum(
            jnp.where(lane[:rest] == line[:rest], totals[HD:], 0.0), axis=0, keepdims=True
        )
        first_high = first.astype(BF).astype(F32)
        second_high = second.astype(BF).astype(F32)
        packed = jnp.where(sub == 0, first_high, 0.0)
        packed = jnp.where(sub == 1, second_high, packed)
        packed = jnp.where(sub == 2, first - first_high, packed)
        packed = jnp.where(sub == 3, second - second_high, packed)
        out_ref[target, rows:, :] = packed.astype(BF)


def combine_kernel(parts_ref, out_ref):
    rows = out_ref.shape[0]
    lane = lax.broadcasted_iota(jnp.int32, (HD, HD), 1)
    line = lax.broadcasted_iota(jnp.int32, (HD, HD), 0)
    rest = rows - HD
    for h in range(2):
        numer = jnp.zeros((rows, HD), F32)
        packed = jnp.zeros((16, HD), F32)
        for g in range(GRID):
            numer = numer + parts_ref[2 * g + h, :rows, :].astype(F32)
            packed = packed + parts_ref[2 * g + h, rows:, :].astype(F32)
        first = packed[0:1] + packed[2:3]
        second = packed[1:2] + packed[3:4]
        first = jnp.sum(jnp.where(lane == line, first, 0.0), axis=1, keepdims=True)
        second = jnp.sum(
            jnp.where(lane[:rest] == line[:rest], second, 0.0), axis=1, keepdims=True
        )
        part = slice(h * HD, (h + 1) * HD)
        out_ref[:HD, part] = (numer[:HD] / first).astype(BF)
        out_ref[HD:, part] = (numer[HD:] / second).astype(BF)


def branch_kernel(place_ref, a_ref, w0, w1, w2, w3, *out_refs):
    for k, out_ref in enumerate(out_refs):
        total = jnp.zeros(out_ref.shape, F32)
        for away, w_ref in enumerate((w0, w1, w2, w3)):
            total = total + jnp.dot(
                a_ref[lax.rem(place_ref[3] + GRID - away, GRID)],
                w_ref[lax.rem(place_ref[2] + k, GRID)],
                preferred_element_type=F32,
            )
        out_ref[...] = total.astype(BF)


def per_device(latents, train_qkv, ema_qkv, q_gain, k_gain, out_weight, modulation, timestep, step):
    rows, width = latents.shape
    channels = ema_qkv.shape[2]
    blocks = GRID * GRID
    by_head = pl.pallas_call(
        average_kernel,
        in_specs=[
            pl.BlockSpec(memory_space=pltpu.SMEM),
            pl.BlockSpec(memory_space=pltpu.VMEM),
            pl.BlockSpec(memory_space=pltpu.VMEM),
        ],
        out_specs=pl.BlockSpec(memory_space=pltpu.VMEM),
        out_shape=jax.ShapeDtypeStruct((2, rows, 3 * HD), BF),
        name="average",
    )(step, ema_qkv, train_qkv)
    full_weights = lax.all_gather(by_head, TOKENS, axis=1, tiled=True)

    place = jnp.stack(
        [lax.axis_index(name).astype(jnp.int32) for name in ("core", "y", "head", "seq")]
    )

    def column(k):
        return lambda i, place: (0, i * GRID + lax.rem(place[3] + k, GRID))

    out_parts = pl.pallas_call(
        pick_kernel,
        grid_spec=pltpu.PrefetchScalarGridSpec(
            num_scalar_prefetch=1,
            grid=(GRID,),
            in_specs=[pl.BlockSpec((channels, width), column(k)) for k in range(GRID)],
            out_specs=[pl.BlockSpec((1, channels, width), lambda i, place: (i, 0, 0))] * GRID,
        ),
        out_shape=[jax.ShapeDtypeStruct((GRID, channels, width), BF)] * GRID,
        name="pick",
    )(place, *([out_weight] * GRID))

    mod_row = lax.dynamic_index_in_dim(modulation, timestep[0], 0, keepdims=False)
    half = rows // 2
    before = lax.ppermute(latents, "head", shift(1))
    after = lax.ppermute(latents, "head", shift(3))
    far = jnp.concatenate(
        [
            lax.ppermute(before[:half], "head", shift(1)),
            lax.ppermute(after[half:], "head", shift(3)),
        ]
    )
    raw = jnp.stack([latents, before, far, after])
    raw = gather_small(raw, "seq").reshape(GRID, GRID, rows, width)
    raw, *out_parts = lax.optimization_barrier((raw, *out_parts))
    out_parts = [out_parts[0]] + [lax.ppermute(out_parts[k], "seq", shift(k)) for k in (1, 2, 3)]
    in_smem = pl.BlockSpec(memory_space=pltpu.SMEM)
    in_vmem = pl.BlockSpec(memory_space=pltpu.VMEM)
    hidden = pl.pallas_call(
        norm_kernel,
        in_specs=[in_smem, in_vmem, in_vmem],
        out_specs=in_vmem,
        out_shape=jax.ShapeDtypeStruct((rows, blocks * width), BF),
        name="norm",
    )(place, raw, mod_row.reshape(3, GRID, GRID, width))
    sibling = lax.ppermute(hidden, "core", [(0, 1), (1, 0)])

    depth = D // GRID
    queries, pairs = pl.pallas_call(
        project_kernel,
        grid_spec=pltpu.PrefetchScalarGridSpec(
            num_scalar_prefetch=1,
            grid=(GRID,),
            in_specs=[
                pl.BlockSpec((rows, depth), lambda i, place: (0, i)),
                pl.BlockSpec((rows, depth), lambda i, place: (0, i)),
                pl.BlockSpec((1, depth, 3 * HD), lambda i, place: (place[0], i, 0)),
                pl.BlockSpec((1, HD), lambda i, place: (0, 0)),
                pl.BlockSpec((1, HD), lambda i, place: (0, 0)),
            ],
            out_specs=[
                pl.BlockSpec((2, rows, HD), lambda i, place: (0, 0, 0)),
                pl.BlockSpec((2, 2, rows, HD), lambda i, place: (0, 0, 0, 0)),
            ],
            scratch_shapes=[pltpu.VMEM((2 * rows, 3 * HD), F32)],
        ),
        out_shape=[
            jax.ShapeDtypeStruct((2, rows, HD), BF),
            jax.ShapeDtypeStruct((2, 2, rows, HD), BF),
        ],
        name="project",
    )(place, hidden, sibling, full_weights, q_gain.reshape(1, HD), k_gain.reshape(1, HD))

    pairs = gather_small(pairs, "zl").reshape(GRID, 2, 2, rows, HD)
    queries = jnp.stack([queries] + [lax.ppermute(queries, "y", shift(k)) for k in (1, 2, 3)])

    sent = rows + 16
    parts = pl.pallas_call(
        attend_kernel,
        grid_spec=pltpu.PrefetchScalarGridSpec(
            num_scalar_prefetch=1,
            grid=(GRID,),
            in_specs=[
                pl.BlockSpec(
                    (1, 2, rows, HD), lambda i, place: (lax.rem(place[1] + GRID - i, GRID), 0, 0, 0)
                ),
                pl.BlockSpec((GRID, 2, 2, rows, HD), lambda i, place: (0, 0, 0, 0, 0)),
            ],
            out_specs=pl.BlockSpec((2, sent, HD), lambda i, place: (i, 0, 0)),
            scratch_shapes=[
                pltpu.VMEM((2 * GRID * rows, HD), BF),
                pltpu.VMEM((2 * GRID * rows, 2 * HD), BF),
            ],
        ),
        out_shape=jax.ShapeDtypeStruct((2 * GRID, sent, HD), BF),
        name="attend",
    )(place, queries, pairs)
    parts, *out_parts = lax.optimization_barrier((parts, *out_parts))
    parts = lax.all_to_all(parts, ("y", "core"), 0, 0, tiled=True)
    attended = pl.pallas_call(
        combine_kernel,
        out_shape=jax.ShapeDtypeStruct((rows, channels), BF),
        name="combine",
    )(parts)

    around = gather_small(attended, "seq")
    outs = pl.pallas_call(
        branch_kernel,
        in_specs=[in_smem] + [in_vmem] * (GRID + 1),
        out_specs=[in_vmem] * GRID,
        out_shape=[jax.ShapeDtypeStruct((rows, width), BF)] * GRID,
        name="branch",
    )(place, around, *out_parts)
    shares = [lax.ppermute(outs[k], "head", shift(k)) for k in (2, 1, 3)]
    summed = outs[0].astype(F32)
    for share in shares:
        summed = summed + share.astype(F32)
    position = lax.axis_index(("head", "seq")) * width
    gate = lax.dynamic_slice_in_dim(mod_row[2], position, width, 0)
    return (latents.astype(F32) + gate[None, :] * summed).astype(BF)


def solution(mesh):
    fine = Mesh(
        mesh.devices.reshape(GRID, GRID, 2, GRID, GRID), ("y", "zl", "core", "head", "seq")
    )
    in_specs = (
        P(TOKENS, ("head", "seq")),
        P(None, TOKENS, ("head", "seq")),
        P(None, TOKENS, ("head", "seq")),
        P(),
        P(),
        P(("head", "seq"), None),
        P(),
        P(),
        P(),
    )
    out_specs = P(TOKENS, ("head", "seq"))
    return jax.shard_map(
        per_device, mesh=fine, in_specs=in_specs, out_specs=out_specs, check_vma=False
    )
```

```python
import math

import jax
import jax.numpy as jnp
from jax import lax
from jax.experimental import pallas as pl
from jax.experimental.pallas import tpu as pltpu
from jax.sharding import Mesh
from jax.sharding import PartitionSpec as P

D = 6144
HD = 128
GRID = 4
BF = jnp.bfloat16
F32 = jnp.float32
LOG2E = 1.4426950408889634
TOKENS = ("y", "zl", "core")
PARAMS = pltpu.CompilerParams(vmem_limit_bytes=24 << 20)


def shift(amount):
    return [(i, (i + amount) % GRID) for i in range(GRID)]


def average_kernel(step_ref, ema_ref, train_ref, out_ref):
    stepped = jnp.full((1, HD), step_ref[0], jnp.int32).astype(F32)
    decay = (1.0 + stepped) / (10.0 + stepped)
    for h in range(2):
        for j in range(3):
            part = slice(h * HD, (h + 1) * HD)
            ema = ema_ref[j, :, part].astype(F32)
            train = train_ref[j, :, part].astype(F32)
            out_ref[h, :, j * HD : (j + 1) * HD] = (decay * ema + (1.0 - decay) * train).astype(BF)


def spread_kernel(own_ref, before_ref, low_ref, high_ref, after_ref, out_ref):
    half = low_ref.shape[0]
    for copy in range(GRID):
        out_ref[copy, 0] = own_ref[...]
        out_ref[copy, 1] = before_ref[...]
        out_ref[copy, 2, :half] = low_ref[...]
        out_ref[copy, 2, half:] = high_ref[...]
        out_ref[copy, 3] = after_ref[...]


def norm_kernel(place_ref, raw_ref, mod_ref, sent_ref, out_ref, sems):
    blocks = [(s, k) for s in range(GRID) for k in range(GRID)]
    rows, width = raw_ref.shape[2], raw_ref.shape[3]
    some = 32

    def one_piece(i, carry):
        part = pl.ds(pl.multiple_of(i * some, some), some)
        total = jnp.zeros((some, width), F32)
        for s, k in blocks:
            total = total + raw_ref[s, k, part, :].astype(F32)
        average = jnp.sum(total, axis=1, keepdims=True) * (1.0 / D)
        squares = jnp.zeros((some, width), F32)
        for s, k in blocks:
            centred = raw_ref[s, k, part, :].astype(F32) - average
            squares = squares + centred * centred
        variance = jnp.sum(squares, axis=1, keepdims=True) * (1.0 / D)
        inverse = lax.rsqrt(variance + 1e-06)
        for s, k in blocks:
            h = lax.rem(place_ref[2] + GRID - k, GRID)
            centred = raw_ref[s, k, part, :].astype(F32) - average
            scale = mod_ref[1, h, s : s + 1, :]
            move = mod_ref[0, h, s : s + 1, :]
            start = pl.multiple_of((h * GRID + s) * width, HD)
            out_ref[part, pl.ds(start, width)] = (
                centred * inverse * (1.0 + scale) + move
            ).astype(BF)
        pltpu.make_async_copy(out_ref.at[part], sent_ref.at[part], sems.at[i]).start()
        return carry

    lax.fori_loop(0, rows // some, one_piece, 0)
    for i in range(rows // some):
        part = pl.ds(i * some, some)
        pltpu.make_async_copy(out_ref.at[part], sent_ref.at[part], sems.at[i]).wait()


def pick_kernel(place_ref, *refs):
    for source, target in zip(refs[:GRID], refs[GRID:]):
        target[0] = source[...]


def project_kernel(place_ref, own_ref, other_ref, weight_ref, q_gain_ref, k_gain_ref, q_ref, kv_ref, held, sems):
    rows = own_ref.shape[0]
    depth = held.shape[1]
    copies = [
        pltpu.make_async_copy(
            weight_ref.at[place_ref[0], pl.ds(i * depth, depth), :], held.at[i], sems.at[i]
        )
        for i in range(held.shape[0])
    ]
    for copy in copies:
        copy.start()
    total = None
    for i, copy in enumerate(copies):
        part = slice(i * depth, (i + 1) * depth)
        hidden = jnp.concatenate([own_ref[:, part], other_ref[:, part]], axis=0)
        copy.wait()
        product = jnp.dot(hidden, held[i], preferred_element_type=F32)
        total = product if total is None else total + product
    for t in range(2):
        here = slice(t * rows, (t + 1) * rows)
        for j, gain_ref in ((0, q_gain_ref), (1, k_gain_ref)):
            values = total[here, j * HD : (j + 1) * HD]
            squares = jnp.mean(values * values, axis=1, keepdims=True)
            normed = (values * lax.rsqrt(squares + 1e-06) * gain_ref[...]).astype(BF)
            if j == 0:
                q_ref[t] = normed
            else:
                for copy in range(GRID):
                    kv_ref[copy, 0, t] = normed
        values = total[here, 2 * HD :].astype(BF)
        for copy in range(GRID):
            kv_ref[copy, 1, t] = values


def attend_kernel(place_ref, q0, q1, q2, q3, kv_ref, out_ref, k_all, v_all):
    rows = q0.shape[1]
    blocks = 2 * GRID
    for g in range(GRID):
        for t in range(2):
            part = slice((2 * g + t) * rows, (2 * g + t + 1) * rows)
            k_all[part, :] = kv_ref[g, 0, t]
            v_all[part, :HD] = kv_ref[g, 1, t]
    v_all[:, HD:] = jnp.ones((blocks * rows, HD), BF)

    chunk = 512
    lane = lax.broadcasted_iota(jnp.int32, (HD, HD), 1)
    line = lax.broadcasted_iota(jnp.int32, (HD, HD), 0)
    sub = lax.broadcasted_iota(jnp.int32, (16, HD), 0)
    rest = rows - HD
    for k, q_ref in enumerate((q0, q1, q2, q3)):
        queries = jnp.concatenate([q_ref[0], q_ref[1]], axis=0)
        both = jnp.zeros((2 * rows, 2 * HD), F32)
        for c in range(blocks * rows // chunk):
            part = slice(c * chunk, (c + 1) * chunk)
            scores = lax.dot_general(
                queries, k_all[part, :], (((1,), (1,)), ((), ())), preferred_element_type=F32
            )
            weights = jnp.exp2(scores * (LOG2E / math.sqrt(HD))).astype(BF)
            both = both + jnp.dot(weights, v_all[part, :], preferred_element_type=F32)
        for t in range(2):
            target = 2 * lax.rem(place_ref[1] + GRID - k, GRID) + lax.rem(place_ref[0] + t, 2)
            out_ref[target, :rows, :] = both[t * rows : (t + 1) * rows, :HD].astype(BF)
            totals = both[t * rows : (t + 1) * rows, HD:]
            first = jnp.sum(jnp.where(lane == line, totals[:HD], 0.0), axis=0, keepdims=True)
            second = jnp.sum(
                jnp.where(lane[:rest] == line[:rest], totals[HD:], 0.0), axis=0, keepdims=True
            )
            first_high = first.astype(BF).astype(F32)
            second_high = second.astype(BF).astype(F32)
            packed = jnp.where(sub == 0, first_high, 0.0)
            packed = jnp.where(sub == 1, second_high, packed)
            packed = jnp.where(sub == 2, first - first_high, packed)
            packed = jnp.where(sub == 3, second - second_high, packed)
            out_ref[target, rows:, :] = packed.astype(BF)


def combine_kernel(parts_ref, out_ref):
    rows = out_ref.shape[1]
    lane = lax.broadcasted_iota(jnp.int32, (HD, HD), 1)
    line = lax.broadcasted_iota(jnp.int32, (HD, HD), 0)
    rest = rows - HD
    for h in range(2):
        numer = jnp.zeros((rows, HD), F32)
        packed = jnp.zeros((16, HD), F32)
        for g in range(GRID):
            numer = numer + parts_ref[2 * g + h, :rows, :].astype(F32)
            packed = packed + parts_ref[2 * g + h, rows:, :].astype(F32)
        first = packed[0:1] + packed[2:3]
        second = packed[1:2] + packed[3:4]
        first = jnp.sum(jnp.where(lane == line, first, 0.0), axis=1, keepdims=True)
        second = jnp.sum(
            jnp.where(lane[:rest] == line[:rest], second, 0.0), axis=1, keepdims=True
        )
        part = slice(h * HD, (h + 1) * HD)
        upper = (numer[:HD] / first).astype(BF)
        lower = (numer[HD:] / second).astype(BF)
        for copy in range(GRID):
            out_ref[copy, :HD, part] = upper
            out_ref[copy, HD:, part] = lower


def branch_kernel(place_ref, a_ref, w0, w1, w2, w3, *out_refs):
    for k, out_ref in enumerate(out_refs):
        total = jnp.zeros(out_ref.shape, F32)
        for away, w_ref in enumerate((w0, w1, w2, w3)):
            total = total + jnp.dot(
                a_ref[lax.rem(place_ref[3] + GRID - away, GRID)],
                w_ref[lax.rem(place_ref[2] + k, GRID)],
                preferred_element_type=F32,
            )
        out_ref[...] = total.astype(BF)


def per_device(latents, train_qkv, ema_qkv, q_gain, k_gain, out_weight, modulation, timestep, step):
    rows, width = latents.shape
    channels = ema_qkv.shape[2]
    blocks = GRID * GRID
    by_head = pl.pallas_call(
        average_kernel,
        in_specs=[
            pl.BlockSpec(memory_space=pltpu.SMEM),
            pl.BlockSpec(memory_space=pltpu.VMEM),
            pl.BlockSpec(memory_space=pltpu.VMEM),
        ],
        out_specs=pl.BlockSpec(memory_space=pltpu.VMEM),
        out_shape=jax.ShapeDtypeStruct((2, rows, 3 * HD), BF),
        name="average",
    )(step, ema_qkv, train_qkv)
    full_weights = lax.all_gather(by_head, TOKENS, axis=1, tiled=True)

    place = jnp.stack(
        [lax.axis_index(name).astype(jnp.int32) for name in ("core", "y", "head", "seq")]
    )

    def column(k):
        return lambda i, place: (0, i * GRID + lax.rem(place[3] + k, GRID))

    out_parts = pl.pallas_call(
        pick_kernel,
        grid_spec=pltpu.PrefetchScalarGridSpec(
            num_scalar_prefetch=1,
            grid=(GRID,),
            in_specs=[pl.BlockSpec((channels, width), column(k)) for k in range(GRID)],
            out_specs=[pl.BlockSpec((1, channels, width), lambda i, place: (i, 0, 0))] * GRID,
        ),
        out_shape=[jax.ShapeDtypeStruct((GRID, channels, width), BF)] * GRID,
        name="pick",
    )(place, *([out_weight] * GRID))

    mod_row = lax.dynamic_index_in_dim(modulation, timestep[0], 0, keepdims=False)
    half = rows // 2
    before = lax.ppermute(latents, "head", shift(1))
    after = lax.ppermute(latents, "head", shift(3))
    far_low = lax.ppermute(before[:half], "head", shift(1))
    far_high = lax.ppermute(after[half:], "head", shift(3))
    in_smem = pl.BlockSpec(memory_space=pltpu.SMEM)
    in_vmem = pl.BlockSpec(memory_space=pltpu.VMEM)
    raw = pl.pallas_call(
        spread_kernel,
        in_specs=[in_vmem] * (GRID + 1),
        out_specs=in_vmem,
        out_shape=jax.ShapeDtypeStruct((GRID, GRID, rows, width), BF),
        name="spread",
    )(latents, before, far_low, far_high, after)
    raw = lax.all_to_all(raw, "seq", 0, 0, tiled=True)
    out0, out1, out2, out3 = out_parts
    raw, out2 = lax.optimization_barrier((raw, out2))
    out2 = lax.ppermute(out2, "seq", shift(2))
    hidden = pl.pallas_call(
        norm_kernel,
        in_specs=[in_smem, in_vmem, in_vmem],
        out_specs=pl.BlockSpec(memory_space=pltpu.HBM),
        out_shape=jax.ShapeDtypeStruct((rows, blocks * width), BF),
        scratch_shapes=[
            pltpu.VMEM((rows, blocks * width), BF),
            pltpu.SemaphoreType.DMA((rows // 32,)),
        ],
        compiler_params=PARAMS,
        name="norm",
    )(place, raw, mod_row.reshape(3, GRID, GRID, width))
    sibling = lax.ppermute(hidden, "core", [(0, 1), (1, 0)])

    depth = D // GRID
    queries, pairs = pl.pallas_call(
        project_kernel,
        in_specs=[in_smem, in_vmem, in_vmem, pl.BlockSpec(memory_space=pltpu.HBM), in_vmem, in_vmem],
        out_specs=[in_vmem, in_vmem],
        out_shape=[
            jax.ShapeDtypeStruct((2, rows, HD), BF),
            jax.ShapeDtypeStruct((GRID, 2, 2, rows, HD), BF),
        ],
        scratch_shapes=[
            pltpu.VMEM((GRID, depth, 3 * HD), BF),
            pltpu.SemaphoreType.DMA((GRID,)),
        ],
        compiler_params=PARAMS,
        name="project",
    )(place, hidden, sibling, pltpu.with_memory_space_constraint(full_weights, pltpu.HBM), q_gain.reshape(1, HD), k_gain.reshape(1, HD))

    pairs = lax.all_to_all(pairs, "zl", 0, 0, tiled=True)
    queries = [queries] + [lax.ppermute(queries, "y", shift(k)) for k in (1, 2, 3)]

    sent = rows + 16
    parts = pl.pallas_call(
        attend_kernel,
        in_specs=[in_smem] + [in_vmem] * (GRID + 1),
        out_specs=in_vmem,
        out_shape=jax.ShapeDtypeStruct((2 * GRID, sent, HD), BF),
        scratch_shapes=[
            pltpu.VMEM((2 * GRID * rows, HD), BF),
            pltpu.VMEM((2 * GRID * rows, 2 * HD), BF),
        ],
        compiler_params=PARAMS,
        name="attend",
    )(place, *queries, pairs)
    parts, out1, out2, out3 = lax.optimization_barrier((parts, out1, out2, out3))
    parts = lax.all_to_all(parts, ("y", "core"), 0, 0, tiled=True)
    out1 = lax.ppermute(out1, "seq", shift(1))
    out3 = lax.ppermute(out3, "seq", shift(3))
    around = pl.pallas_call(
        combine_kernel,
        in_specs=[in_vmem],
        out_specs=in_vmem,
        out_shape=jax.ShapeDtypeStruct((GRID, rows, channels), BF),
        name="combine",
    )(parts)
    around, out1, out3 = lax.optimization_barrier((around, out1, out3))
    around = lax.all_to_all(around, "seq", 0, 0, tiled=True)
    outs = pl.pallas_call(
        branch_kernel,
        in_specs=[in_smem] + [in_vmem] * (GRID + 1),
        out_specs=[in_vmem] * GRID,
        out_shape=[jax.ShapeDtypeStruct((rows, width), BF)] * GRID,
        compiler_params=PARAMS,
        name="branch",
    )(place, around, out0, out1, out2, out3)
    shares = [lax.ppermute(outs[k], "head", shift(k)) for k in (2, 1, 3)]
    summed = outs[0].astype(F32)
    for share in shares:
        summed = summed + share.astype(F32)
    position = lax.axis_index(("head", "seq")) * width
    gate = lax.dynamic_slice_in_dim(mod_row[2], position, width, 0)
    return (latents.astype(F32) + gate[None, :] * summed).astype(BF)


def solution(mesh):
    fine = Mesh(
        mesh.devices.reshape(GRID, GRID, 2, GRID, GRID), ("y", "zl", "core", "head", "seq")
    )
    in_specs = (
        P(TOKENS, ("head", "seq")),
        P(None, TOKENS, ("head", "seq")),
        P(None, TOKENS, ("head", "seq")),
        P(),
        P(),
        P(("head", "seq"), None),
        P(),
        P(),
        P(),
    )
    out_specs = P(TOKENS, ("head", "seq"))
    return jax.shard_map(
        per_device, mesh=fine, in_specs=in_specs, out_specs=out_specs, check_vma=False
    )
```

```python
import math

import jax
import jax.numpy as jnp
from jax import lax
from jax.experimental import pallas as pl
from jax.experimental.pallas import tpu as pltpu
from jax.sharding import Mesh
from jax.sharding import PartitionSpec as P

D = 6144
HD = 128
GRID = 4
BF = jnp.bfloat16
F32 = jnp.float32
LOG2E = 1.4426950408889634
TOKENS = ("y", "zl", "core")
PARAMS = pltpu.CompilerParams(vmem_limit_bytes=24 << 20)


def shift(amount):
    return [(i, (i + amount) % GRID) for i in range(GRID)]


def average_kernel(step_ref, ema_ref, train_ref, out_ref):
    stepped = jnp.full((1, HD), step_ref[0], jnp.int32).astype(F32)
    decay = (1.0 + stepped) / (10.0 + stepped)
    for h in range(2):
        for j in range(3):
            part = slice(h * HD, (h + 1) * HD)
            ema = ema_ref[j, :, part].astype(F32)
            train = train_ref[j, :, part].astype(F32)
            out_ref[h, :, j * HD : (j + 1) * HD] = (decay * ema + (1.0 - decay) * train).astype(BF)


def spread_kernel(r0, r1, r2, r3, out_ref, sems):
    copies = [
        pltpu.make_async_copy(ref, out_ref.at[i, k], sems.at[GRID * i + k])
        for i in range(GRID)
        for k, ref in enumerate((r0, r1, r2, r3))
    ]
    for copy in copies:
        copy.start()
    for copy in copies:
        copy.wait()


def norm_kernel(place_ref, raw_ref, mod_ref, sent_ref, out_ref, sems):
    blocks = [(s, k) for s in range(GRID) for k in range(GRID)]
    rows, width = raw_ref.shape[2], raw_ref.shape[3]
    some = 32

    def one_piece(i, carry):
        part = pl.ds(pl.multiple_of(i * some, some), some)
        total = jnp.zeros((some, width), F32)
        for s, k in blocks:
            total = total + raw_ref[s, k, part, :].astype(F32)
        average = jnp.sum(total, axis=1, keepdims=True) * (1.0 / D)
        squares = jnp.zeros((some, width), F32)
        for s, k in blocks:
            centred = raw_ref[s, k, part, :].astype(F32) - average
            squares = squares + centred * centred
        variance = jnp.sum(squares, axis=1, keepdims=True) * (1.0 / D)
        inverse = lax.rsqrt(variance + 1e-06)
        for s, k in blocks:
            h = lax.rem(place_ref[2] + GRID - k, GRID)
            centred = raw_ref[s, k, part, :].astype(F32) - average
            scale = mod_ref[1, h, s : s + 1, :]
            move = mod_ref[0, h, s : s + 1, :]
            start = pl.multiple_of((h * GRID + s) * width, HD)
            out_ref[part, pl.ds(start, width)] = (
                centred * inverse * (1.0 + scale) + move
            ).astype(BF)
        pltpu.make_async_copy(out_ref.at[part], sent_ref.at[part], sems.at[i]).start()
        return carry

    lax.fori_loop(0, rows // some, one_piece, 0)
    for i in range(rows // some):
        part = pl.ds(i * some, some)
        pltpu.make_async_copy(out_ref.at[part], sent_ref.at[part], sems.at[i]).wait()


def pick_kernel(place_ref, *refs):
    for source, target in zip(refs[:GRID], refs[GRID:]):
        target[0] = source[...]


def project_kernel(place_ref, own_ref, other_ref, weight_ref, q_gain_ref, k_gain_ref, q_ref, kv_ref, held, sems):
    rows = own_ref.shape[0]
    depth = held.shape[1]
    copies = [
        pltpu.make_async_copy(
            weight_ref.at[place_ref[0], pl.ds(i * depth, depth), :], held.at[i], sems.at[i]
        )
        for i in range(held.shape[0])
    ]
    for copy in copies:
        copy.start()
    total = None
    for i, copy in enumerate(copies):
        part = slice(i * depth, (i + 1) * depth)
        hidden = jnp.concatenate([own_ref[:, part], other_ref[:, part]], axis=0)
        copy.wait()
        product = jnp.dot(hidden, held[i], preferred_element_type=F32)
        total = product if total is None else total + product
    for t in range(2):
        here = slice(t * rows, (t + 1) * rows)
        for j, gain_ref in ((0, q_gain_ref), (1, k_gain_ref)):
            values = total[here, j * HD : (j + 1) * HD]
            squares = jnp.mean(values * values, axis=1, keepdims=True)
            normed = (values * lax.rsqrt(squares + 1e-06) * gain_ref[...]).astype(BF)
            if j == 0:
                q_ref[t] = normed
            else:
                for copy in range(GRID):
                    kv_ref[copy, 0, t] = normed
        values = total[here, 2 * HD :].astype(BF)
        for copy in range(GRID):
            kv_ref[copy, 1, t] = values


def attend_kernel(place_ref, q0, q1, q2, q3, kv_ref, out_ref, k_all, v_all):
    rows = q0.shape[1]
    blocks = 2 * GRID
    for g in range(GRID):
        for t in range(2):
            part = slice((2 * g + t) * rows, (2 * g + t + 1) * rows)
            k_all[part, :] = kv_ref[g, 0, t]
            v_all[part, :HD] = kv_ref[g, 1, t]
    v_all[:, HD:] = jnp.ones((blocks * rows, HD), BF)

    chunk = 512
    lane = lax.broadcasted_iota(jnp.int32, (HD, HD), 1)
    line = lax.broadcasted_iota(jnp.int32, (HD, HD), 0)
    sub = lax.broadcasted_iota(jnp.int32, (16, HD), 0)
    rest = rows - HD
    for k, q_ref in enumerate((q0, q1, q2, q3)):
        queries = jnp.concatenate([q_ref[0], q_ref[1]], axis=0)
        both = jnp.zeros((2 * rows, 2 * HD), F32)
        for c in range(blocks * rows // chunk):
            part = slice(c * chunk, (c + 1) * chunk)
            scores = lax.dot_general(
                queries, k_all[part, :], (((1,), (1,)), ((), ())), preferred_element_type=F32
            )
            weights = jnp.exp2(scores * (LOG2E / math.sqrt(HD))).astype(BF)
            both = both + jnp.dot(weights, v_all[part, :], preferred_element_type=F32)
        for t in range(2):
            target = 2 * lax.rem(place_ref[1] + GRID - k, GRID) + lax.rem(place_ref[0] + t, 2)
            out_ref[target, :rows, :] = both[t * rows : (t + 1) * rows, :HD].astype(BF)
            totals = both[t * rows : (t + 1) * rows, HD:]
            first = jnp.sum(jnp.where(lane == line, totals[:HD], 0.0), axis=0, keepdims=True)
            second = jnp.sum(
                jnp.where(lane[:rest] == line[:rest], totals[HD:], 0.0), axis=0, keepdims=True
            )
            first_high = first.astype(BF).astype(F32)
            second_high = second.astype(BF).astype(F32)
            packed = jnp.where(sub == 0, first_high, 0.0)
            packed = jnp.where(sub == 1, second_high, packed)
            packed = jnp.where(sub == 2, first - first_high, packed)
            packed = jnp.where(sub == 3, second - second_high, packed)
            out_ref[target, rows:, :] = packed.astype(BF)


def combine_kernel(parts_ref, out_ref):
    rows = out_ref.shape[1]
    lane = lax.broadcasted_iota(jnp.int32, (HD, HD), 1)
    line = lax.broadcasted_iota(jnp.int32, (HD, HD), 0)
    rest = rows - HD
    for h in range(2):
        numer = jnp.zeros((rows, HD), F32)
        packed = jnp.zeros((16, HD), F32)
        for g in range(GRID):
            numer = numer + parts_ref[2 * g + h, :rows, :].astype(F32)
            packed = packed + parts_ref[2 * g + h, rows:, :].astype(F32)
        first = packed[0:1] + packed[2:3]
        second = packed[1:2] + packed[3:4]
        first = jnp.sum(jnp.where(lane == line, first, 0.0), axis=1, keepdims=True)
        second = jnp.sum(
            jnp.where(lane[:rest] == line[:rest], second, 0.0), axis=1, keepdims=True
        )
        part = slice(h * HD, (h + 1) * HD)
        upper = (numer[:HD] / first).astype(BF)
        lower = (numer[HD:] / second).astype(BF)
        for copy in range(GRID):
            out_ref[copy, :HD, part] = upper
            out_ref[copy, HD:, part] = lower


def branch_kernel(place_ref, a_ref, w0, w1, w2, w3, *out_refs):
    for k, out_ref in enumerate(out_refs):
        total = jnp.zeros(out_ref.shape, F32)
        for away, w_ref in enumerate((w0, w1, w2, w3)):
            total = total + jnp.dot(
                a_ref[lax.rem(place_ref[3] + GRID - away, GRID)],
                w_ref[lax.rem(place_ref[2] + k, GRID)],
                preferred_element_type=F32,
            )
        out_ref[...] = total.astype(BF)


def per_device(latents, train_qkv, ema_qkv, q_gain, k_gain, out_weight, modulation, timestep, step):
    rows, width = latents.shape
    channels = ema_qkv.shape[2]
    blocks = GRID * GRID
    by_head = pl.pallas_call(
        average_kernel,
        in_specs=[
            pl.BlockSpec(memory_space=pltpu.SMEM),
            pl.BlockSpec(memory_space=pltpu.VMEM),
            pl.BlockSpec(memory_space=pltpu.VMEM),
        ],
        out_specs=pl.BlockSpec(memory_space=pltpu.VMEM),
        out_shape=jax.ShapeDtypeStruct((2, rows, 3 * HD), BF),
        name="average",
    )(step, ema_qkv, train_qkv)
    full_weights = lax.all_gather(by_head, TOKENS, axis=1, tiled=True)

    place = jnp.stack(
        [lax.axis_index(name).astype(jnp.int32) for name in ("core", "y", "head", "seq")]
    )

    def column(k):
        return lambda i, place: (0, i * GRID + lax.rem(place[3] + k, GRID))

    out_parts = pl.pallas_call(
        pick_kernel,
        grid_spec=pltpu.PrefetchScalarGridSpec(
            num_scalar_prefetch=1,
            grid=(GRID,),
            in_specs=[pl.BlockSpec((channels, width), column(k)) for k in range(GRID)],
            out_specs=[pl.BlockSpec((1, channels, width), lambda i, place: (i, 0, 0))] * GRID,
        ),
        out_shape=[jax.ShapeDtypeStruct((GRID, channels, width), BF)] * GRID,
        name="pick",
    )(place, *([out_weight] * GRID))

    mod_row = lax.dynamic_index_in_dim(modulation, timestep[0], 0, keepdims=False)
    far = lax.ppermute(latents, "head", shift(2))
    before = lax.ppermute(latents, "head", shift(1))
    after = lax.ppermute(latents, "head", shift(3))
    in_smem = pl.BlockSpec(memory_space=pltpu.SMEM)
    in_vmem = pl.BlockSpec(memory_space=pltpu.VMEM)
    in_place = pl.BlockSpec(memory_space=pl.ANY)
    raw = pl.pallas_call(
        spread_kernel,
        in_specs=[in_place] * GRID,
        out_specs=in_place,
        out_shape=jax.ShapeDtypeStruct((GRID, GRID, rows, width), BF),
        scratch_shapes=[pltpu.SemaphoreType.DMA((blocks,))],
        name="spread",
    )(latents, before, far, after)
    raw = lax.all_to_all(raw, "seq", 0, 0, tiled=True)
    out0, out1, out2, out3 = out_parts
    raw, out2 = lax.optimization_barrier((raw, out2))
    out2 = lax.ppermute(out2, "seq", shift(2))
    hidden = pl.pallas_call(
        norm_kernel,
        in_specs=[in_smem, in_vmem, in_vmem],
        out_specs=pl.BlockSpec(memory_space=pltpu.HBM),
        out_shape=jax.ShapeDtypeStruct((rows, blocks * width), BF),
        scratch_shapes=[
            pltpu.VMEM((rows, blocks * width), BF),
            pltpu.SemaphoreType.DMA((rows // 32,)),
        ],
        compiler_params=PARAMS,
        name="norm",
    )(place, raw, mod_row.reshape(3, GRID, GRID, width))
    sibling = lax.ppermute(hidden, "core", [(0, 1), (1, 0)])

    depth = D // GRID
    queries, pairs = pl.pallas_call(
        project_kernel,
        in_specs=[in_smem, in_vmem, in_vmem, pl.BlockSpec(memory_space=pltpu.HBM), in_vmem, in_vmem],
        out_specs=[in_vmem, in_vmem],
        out_shape=[
            jax.ShapeDtypeStruct((2, rows, HD), BF),
            jax.ShapeDtypeStruct((GRID, 2, 2, rows, HD), BF),
        ],
        scratch_shapes=[
            pltpu.VMEM((GRID, depth, 3 * HD), BF),
            pltpu.SemaphoreType.DMA((GRID,)),
        ],
        compiler_params=PARAMS,
        name="project",
    )(place, hidden, sibling, pltpu.with_memory_space_constraint(full_weights, pltpu.HBM), q_gain.reshape(1, HD), k_gain.reshape(1, HD))

    pairs = lax.all_to_all(pairs, "zl", 0, 0, tiled=True)
    queries = [queries] + [lax.ppermute(queries, "y", shift(k)) for k in (1, 2, 3)]

    sent = rows + 16
    parts = pl.pallas_call(
        attend_kernel,
        in_specs=[in_smem] + [in_vmem] * (GRID + 1),
        out_specs=in_vmem,
        out_shape=jax.ShapeDtypeStruct((2 * GRID, sent, HD), BF),
        scratch_shapes=[
            pltpu.VMEM((2 * GRID * rows, HD), BF),
            pltpu.VMEM((2 * GRID * rows, 2 * HD), BF),
        ],
        compiler_params=PARAMS,
        name="attend",
    )(place, *queries, pairs)
    parts, out1, out2, out3 = lax.optimization_barrier((parts, out1, out2, out3))
    parts = lax.all_to_all(parts, ("y", "core"), 0, 0, tiled=True)
    out1 = lax.ppermute(out1, "seq", shift(1))
    out3 = lax.ppermute(out3, "seq", shift(3))
    around = pl.pallas_call(
        combine_kernel,
        in_specs=[in_vmem],
        out_specs=in_vmem,
        out_shape=jax.ShapeDtypeStruct((GRID, rows, channels), BF),
        name="combine",
    )(parts)
    around, out1, out3 = lax.optimization_barrier((around, out1, out3))
    around = lax.all_to_all(around, "seq", 0, 0, tiled=True)
    outs = pl.pallas_call(
        branch_kernel,
        in_specs=[in_smem] + [in_vmem] * (GRID + 1),
        out_specs=[in_vmem] * GRID,
        out_shape=[jax.ShapeDtypeStruct((rows, width), BF)] * GRID,
        compiler_params=PARAMS,
        name="branch",
    )(place, around, out0, out1, out2, out3)
    shares = [lax.ppermute(outs[k], "head", shift(k)) for k in (2, 1, 3)]
    summed = outs[0].astype(F32)
    for share in shares:
        summed = summed + share.astype(F32)
    position = lax.axis_index(("head", "seq")) * width
    gate = lax.dynamic_slice_in_dim(mod_row[2], position, width, 0)
    return (latents.astype(F32) + gate[None, :] * summed).astype(BF)


def solution(mesh):
    fine = Mesh(
        mesh.devices.reshape(GRID, GRID, 2, GRID, GRID), ("y", "zl", "core", "head", "seq")
    )
    in_specs = (
        P(TOKENS, ("head", "seq")),
        P(None, TOKENS, ("head", "seq")),
        P(None, TOKENS, ("head", "seq")),
        P(),
        P(),
        P(("head", "seq"), None),
        P(),
        P(),
        P(),
    )
    out_specs = P(TOKENS, ("head", "seq"))
    return jax.shard_map(
        per_device, mesh=fine, in_specs=in_specs, out_specs=out_specs, check_vma=False
    )
```

```python
import math

import jax
import jax.numpy as jnp
from jax import lax
from jax.experimental import pallas as pl
from jax.experimental.pallas import tpu as pltpu
from jax.sharding import Mesh
from jax.sharding import PartitionSpec as P

D = 6144
HD = 128
GRID = 4
BF = jnp.bfloat16
F32 = jnp.float32
LOG2E = 1.4426950408889634
TOKENS = ("y", "zl", "core")
PARAMS = pltpu.CompilerParams(vmem_limit_bytes=24 << 20)


def shift(amount):
    return [(i, (i + amount) % GRID) for i in range(GRID)]


def average_kernel(step_ref, ema_ref, train_ref, out_ref):
    stepped = jnp.full((1, HD), step_ref[0], jnp.int32).astype(F32)
    decay = (1.0 + stepped) / (10.0 + stepped)
    for h in range(2):
        part = slice(h * HD, (h + 1) * HD)
        ema = ema_ref[0, :, part].astype(F32)
        train = train_ref[0, :, part].astype(F32)
        out_ref[h] = (decay * ema + (1.0 - decay) * train).astype(BF)


def spread_kernel(own_ref, before_ref, low_ref, high_ref, after_ref, out_ref):
    half = low_ref.shape[0]
    out_ref[0, 0] = own_ref[...]
    out_ref[0, 1] = before_ref[...]
    out_ref[0, 2, :half] = low_ref[...]
    out_ref[0, 2, half:] = high_ref[...]
    out_ref[0, 3] = after_ref[...]


def norm_kernel(place_ref, raw_ref, mod_ref, sent_ref, out_ref, sems):
    blocks = [(s, k) for s in range(GRID) for k in range(GRID)]
    rows, width = raw_ref.shape[2], raw_ref.shape[3]
    some = 32

    def one_piece(i, carry):
        part = pl.ds(pl.multiple_of(i * some, some), some)
        total = jnp.zeros((some, width), F32)
        for s, k in blocks:
            total = total + raw_ref[s, k, part, :].astype(F32)
        average = jnp.sum(total, axis=1, keepdims=True) * (1.0 / D)
        squares = jnp.zeros((some, width), F32)
        for s, k in blocks:
            centred = raw_ref[s, k, part, :].astype(F32) - average
            squares = squares + centred * centred
        variance = jnp.sum(squares, axis=1, keepdims=True) * (1.0 / D)
        inverse = lax.rsqrt(variance + 1e-06)
        for s, k in blocks:
            h = lax.rem(place_ref[2] + GRID - k, GRID)
            centred = raw_ref[s, k, part, :].astype(F32) - average
            scale = mod_ref[1, h, s : s + 1, :]
            move = mod_ref[0, h, s : s + 1, :]
            start = pl.multiple_of((h * GRID + s) * width, HD)
            out_ref[part, pl.ds(start, width)] = (
                centred * inverse * (1.0 + scale) + move
            ).astype(BF)
        pltpu.make_async_copy(out_ref.at[part], sent_ref.at[part], sems.at[i]).start()
        return carry

    lax.fori_loop(0, rows // some, one_piece, 0)
    for i in range(rows // some):
        part = pl.ds(i * some, some)
        pltpu.make_async_copy(out_ref.at[part], sent_ref.at[part], sems.at[i]).wait()


def pick_kernel(place_ref, *refs):
    for source, target in zip(refs[:GRID], refs[GRID:]):
        target[0] = source[...]


def project_kernel(place_ref, own_ref, other_ref, weight_ref, q_gain_ref, k_gain_ref, q_ref, kv_ref, held, sems):
    rows = own_ref.shape[0]
    depth = held.shape[1]
    copies = [
        pltpu.make_async_copy(
            weight_ref.at[place_ref[0], pl.ds(i * depth, depth), :], held.at[i], sems.at[i]
        )
        for i in range(held.shape[0])
    ]
    for copy in copies:
        copy.start()
    total = None
    for i, copy in enumerate(copies):
        part = slice(i * depth, (i + 1) * depth)
        hidden = jnp.concatenate([own_ref[:, part], other_ref[:, part]], axis=0)
        copy.wait()
        product = jnp.dot(hidden, held[i], preferred_element_type=F32)
        total = product if total is None else total + product
    for t in range(2):
        here = slice(t * rows, (t + 1) * rows)
        for j, gain_ref in ((0, q_gain_ref), (1, k_gain_ref)):
            values = total[here, j * HD : (j + 1) * HD]
            squares = jnp.mean(values * values, axis=1, keepdims=True)
            normed = (values * lax.rsqrt(squares + 1e-06) * gain_ref[...]).astype(BF)
            if j == 0:
                q_ref[t] = normed
            else:
                for copy in range(GRID):
                    kv_ref[copy, 0, t] = normed
        values = total[here, 2 * HD :].astype(BF)
        for copy in range(GRID):
            kv_ref[copy, 1, t] = values


def attend_kernel(place_ref, q0, q1, q2, q3, kv_ref, out_ref, k_all, v_all):
    rows = q0.shape[1]
    blocks = 2 * GRID
    for g in range(GRID):
        for t in range(2):
            part = slice((2 * g + t) * rows, (2 * g + t + 1) * rows)
            k_all[part, :] = kv_ref[g, 0, t]
            v_all[part, :HD] = kv_ref[g, 1, t]
    v_all[:, HD:] = jnp.ones((blocks * rows, HD), BF)

    chunk = 512
    lane = lax.broadcasted_iota(jnp.int32, (HD, HD), 1)
    line = lax.broadcasted_iota(jnp.int32, (HD, HD), 0)
    sub = lax.broadcasted_iota(jnp.int32, (16, HD), 0)
    rest = rows - HD
    for k, q_ref in enumerate((q0, q1, q2, q3)):
        queries = jnp.concatenate([q_ref[0], q_ref[1]], axis=0)
        both = jnp.zeros((2 * rows, 2 * HD), F32)
        for c in range(blocks * rows // chunk):
            part = slice(c * chunk, (c + 1) * chunk)
            scores = lax.dot_general(
                queries, k_all[part, :], (((1,), (1,)), ((), ())), preferred_element_type=F32
            )
            weights = jnp.exp2(scores * (LOG2E / math.sqrt(HD))).astype(BF)
            both = both + jnp.dot(weights, v_all[part, :], preferred_element_type=F32)
        for t in range(2):
            target = 2 * lax.rem(place_ref[1] + GRID - k, GRID) + lax.rem(place_ref[0] + t, 2)
            out_ref[target, :rows, :] = both[t * rows : (t + 1) * rows, :HD].astype(BF)
            totals = both[t * rows : (t + 1) * rows, HD:]
            first = jnp.sum(jnp.where(lane == line, totals[:HD], 0.0), axis=0, keepdims=True)
            second = jnp.sum(
                jnp.where(lane[:rest] == line[:rest], totals[HD:], 0.0), axis=0, keepdims=True
            )
            first_high = first.astype(BF).astype(F32)
            second_high = second.astype(BF).astype(F32)
            packed = jnp.where(sub == 0, first_high, 0.0)
            packed = jnp.where(sub == 1, second_high, packed)
            packed = jnp.where(sub == 2, first - first_high, packed)
            packed = jnp.where(sub == 3, second - second_high, packed)
            out_ref[target, rows:, :] = packed.astype(BF)


def combine_kernel(parts_ref, out_ref):
    rows = out_ref.shape[1]
    lane = lax.broadcasted_iota(jnp.int32, (HD, HD), 1)
    line = lax.broadcasted_iota(jnp.int32, (HD, HD), 0)
    rest = rows - HD
    for h in range(2):
        numer = jnp.zeros((rows, HD), F32)
        packed = jnp.zeros((16, HD), F32)
        for g in range(GRID):
            numer = numer + parts_ref[2 * g + h, :rows, :].astype(F32)
            packed = packed + parts_ref[2 * g + h, rows:, :].astype(F32)
        first = packed[0:1] + packed[2:3]
        second = packed[1:2] + packed[3:4]
        first = jnp.sum(jnp.where(lane == line, first, 0.0), axis=1, keepdims=True)
        second = jnp.sum(
            jnp.where(lane[:rest] == line[:rest], second, 0.0), axis=1, keepdims=True
        )
        part = slice(h * HD, (h + 1) * HD)
        upper = (numer[:HD] / first).astype(BF)
        lower = (numer[HD:] / second).astype(BF)
        for copy in range(GRID):
            out_ref[copy, :HD, part] = upper
            out_ref[copy, HD:, part] = lower


def branch_kernel(place_ref, a_ref, w0, w1, w2, w3, *out_refs):
    for k, out_ref in enumerate(out_refs):
        total = jnp.zeros(out_ref.shape, F32)
        for away, w_ref in enumerate((w0, w1, w2, w3)):
            total = total + jnp.dot(
                a_ref[lax.rem(place_ref[3] + GRID - away, GRID)],
                w_ref[lax.rem(place_ref[2] + k, GRID)],
                preferred_element_type=F32,
            )
        out_ref[...] = total.astype(BF)


def per_device(latents, train_qkv, ema_qkv, q_gain, k_gain, out_weight, modulation, timestep, step):
    rows, width = latents.shape
    channels = ema_qkv.shape[2]
    blocks = GRID * GRID
    by_head = pl.pallas_call(
        average_kernel,
        grid=(3,),
        in_specs=[
            pl.BlockSpec(memory_space=pltpu.SMEM),
            pl.BlockSpec((1, rows, channels), lambda j: (j, 0, 0)),
            pl.BlockSpec((1, rows, channels), lambda j: (j, 0, 0)),
        ],
        out_specs=pl.BlockSpec((2, rows, HD), lambda j: (0, 0, j)),
        out_shape=jax.ShapeDtypeStruct((2, rows, 3 * HD), BF),
        name="average",
    )(step, ema_qkv, train_qkv)
    full_weights = lax.all_gather(by_head, TOKENS, axis=1, tiled=True)

    place = jnp.stack(
        [lax.axis_index(name).astype(jnp.int32) for name in ("core", "y", "head", "seq")]
    )

    def column(k):
        return lambda i, place: (0, i * GRID + lax.rem(place[3] + k, GRID))

    out_parts = pl.pallas_call(
        pick_kernel,
        grid_spec=pltpu.PrefetchScalarGridSpec(
            num_scalar_prefetch=1,
            grid=(GRID,),
            in_specs=[pl.BlockSpec((channels, width), column(k)) for k in range(GRID)],
            out_specs=[pl.BlockSpec((1, channels, width), lambda i, place: (i, 0, 0))] * GRID,
        ),
        out_shape=[jax.ShapeDtypeStruct((GRID, channels, width), BF)] * GRID,
        name="pick",
    )(place, *([out_weight] * GRID))

    mod_row = lax.dynamic_index_in_dim(modulation, timestep[0], 0, keepdims=False)
    half = rows // 2
    before = lax.ppermute(latents, "head", shift(1))
    after = lax.ppermute(latents, "head", shift(3))
    far_low = lax.ppermute(before[:half], "head", shift(1))
    far_high = lax.ppermute(after[half:], "head", shift(3))
    in_smem = pl.BlockSpec(memory_space=pltpu.SMEM)
    in_vmem = pl.BlockSpec(memory_space=pltpu.VMEM)
    raw = pl.pallas_call(
        spread_kernel,
        grid=(GRID,),
        in_specs=[
            pl.BlockSpec(part.shape, lambda i: (0, 0))
            for part in (latents, before, far_low, far_high, after)
        ],
        out_specs=pl.BlockSpec((1, GRID, rows, width), lambda i: (i, 0, 0, 0)),
        out_shape=jax.ShapeDtypeStruct((GRID, GRID, rows, width), BF),
        name="spread",
    )(latents, before, far_low, far_high, after)
    raw = lax.all_to_all(raw, "seq", 0, 0, tiled=True)
    out0, out1, out2, out3 = out_parts
    raw, out2 = lax.optimization_barrier((raw, out2))
    out2 = lax.ppermute(out2, "seq", shift(2))
    hidden = pl.pallas_call(
        norm_kernel,
        in_specs=[in_smem, in_vmem, in_vmem],
        out_specs=pl.BlockSpec(memory_space=pltpu.HBM),
        out_shape=jax.ShapeDtypeStruct((rows, blocks * width), BF),
        scratch_shapes=[
            pltpu.VMEM((rows, blocks * width), BF),
            pltpu.SemaphoreType.DMA((rows // 32,)),
        ],
        compiler_params=PARAMS,
        name="norm",
    )(place, raw, mod_row.reshape(3, GRID, GRID, width))
    sibling = lax.ppermute(hidden, "core", [(0, 1), (1, 0)])

    depth = D // GRID
    queries, pairs = pl.pallas_call(
        project_kernel,
        in_specs=[in_smem, in_vmem, in_vmem, pl.BlockSpec(memory_space=pltpu.HBM), in_vmem, in_vmem],
        out_specs=[in_vmem, in_vmem],
        out_shape=[
            jax.ShapeDtypeStruct((2, rows, HD), BF),
            jax.ShapeDtypeStruct((GRID, 2, 2, rows, HD), BF),
        ],
        scratch_shapes=[
            pltpu.VMEM((GRID, depth, 3 * HD), BF),
            pltpu.SemaphoreType.DMA((GRID,)),
        ],
        compiler_params=PARAMS,
        name="project",
    )(place, hidden, sibling, pltpu.with_memory_space_constraint(full_weights, pltpu.HBM), q_gain.reshape(1, HD), k_gain.reshape(1, HD))

    pairs = lax.all_to_all(pairs, "zl", 0, 0, tiled=True)
    queries = [queries] + [lax.ppermute(queries, "y", shift(k)) for k in (1, 2, 3)]

    sent = rows + 16
    parts = pl.pallas_call(
        attend_kernel,
        in_specs=[in_smem] + [in_vmem] * (GRID + 1),
        out_specs=in_vmem,
        out_shape=jax.ShapeDtypeStruct((2 * GRID, sent, HD), BF),
        scratch_shapes=[
            pltpu.VMEM((2 * GRID * rows, HD), BF),
            pltpu.VMEM((2 * GRID * rows, 2 * HD), BF),
        ],
        compiler_params=PARAMS,
        name="attend",
    )(place, *queries, pairs)
    parts, out1, out2, out3 = lax.optimization_barrier((parts, out1, out2, out3))
    parts = lax.all_to_all(parts, ("y", "core"), 0, 0, tiled=True)
    out1 = lax.ppermute(out1, "seq", shift(1))
    out3 = lax.ppermute(out3, "seq", shift(3))
    around = pl.pallas_call(
        combine_kernel,
        in_specs=[in_vmem],
        out_specs=in_vmem,
        out_shape=jax.ShapeDtypeStruct((GRID, rows, channels), BF),
        name="combine",
    )(parts)
    around = lax.all_to_all(around, "seq", 0, 0, tiled=True)
    outs = pl.pallas_call(
        branch_kernel,
        in_specs=[in_smem] + [in_vmem] * (GRID + 1),
        out_specs=[in_vmem] * GRID,
        out_shape=[jax.ShapeDtypeStruct((rows, width), BF)] * GRID,
        compiler_params=PARAMS,
        name="branch",
    )(place, around, out0, out1, out2, out3)
    shares = [lax.ppermute(outs[k], "head", shift(k)) for k in (2, 1, 3)]
    summed = outs[0].astype(F32)
    for share in shares:
        summed = summed + share.astype(F32)
    position = lax.axis_index(("head", "seq")) * width
    gate = lax.dynamic_slice_in_dim(mod_row[2], position, width, 0)
    return (latents.astype(F32) + gate[None, :] * summed).astype(BF)


def solution(mesh):
    fine = Mesh(
        mesh.devices.reshape(GRID, GRID, 2, GRID, GRID), ("y", "zl", "core", "head", "seq")
    )
    in_specs = (
        P(TOKENS, ("head", "seq")),
        P(None, TOKENS, ("head", "seq")),
        P(None, TOKENS, ("head", "seq")),
        P(),
        P(),
        P(("head", "seq"), None),
        P(),
        P(),
        P(),
    )
    out_specs = P(TOKENS, ("head", "seq"))
    return jax.shard_map(
        per_device, mesh=fine, in_specs=in_specs, out_specs=out_specs, check_vma=False
    )
```

```python
import math

import jax
import jax.numpy as jnp
from jax import lax
from jax.experimental import pallas as pl
from jax.experimental.pallas import tpu as pltpu
from jax.sharding import Mesh
from jax.sharding import PartitionSpec as P

D = 6144
HD = 128
GRID = 4
BF = jnp.bfloat16
F32 = jnp.float32
LOG2E = 1.4426950408889634
TOKENS = ("y", "zl", "core")
PARAMS = pltpu.CompilerParams(vmem_limit_bytes=24 << 20)


def shift(amount):
    return [(i, (i + amount) % GRID) for i in range(GRID)]


def average_kernel(step_ref, ema_ref, train_ref, out_ref):
    stepped = jnp.full((1, HD), step_ref[0], jnp.int32).astype(F32)
    decay = (1.0 + stepped) / (10.0 + stepped)
    for h in range(2):
        for j in range(3):
            part = slice(h * HD, (h + 1) * HD)
            ema = ema_ref[j, :, part].astype(F32)
            train = train_ref[j, :, part].astype(F32)
            out_ref[h, :, j * HD : (j + 1) * HD] = (decay * ema + (1.0 - decay) * train).astype(BF)


def spread_kernel(own_ref, before_ref, low_ref, high_ref, after_ref, out_ref):
    half = low_ref.shape[0]
    for copy in range(GRID):
        out_ref[copy, 0] = own_ref[...]
        out_ref[copy, 1] = before_ref[...]
        out_ref[copy, 2, :half] = low_ref[...]
        out_ref[copy, 2, half:] = high_ref[...]
        out_ref[copy, 3] = after_ref[...]


def norm_kernel(place_ref, raw_ref, mod_ref, sent_ref, out_ref, sems):
    blocks = [(s, k) for s in range(GRID) for k in range(GRID)]
    rows, width = raw_ref.shape[2], raw_ref.shape[3]
    some = 32

    def one_piece(i, carry):
        part = pl.ds(pl.multiple_of(i * some, some), some)
        total = jnp.zeros((some, width), F32)
        for s, k in blocks:
            total = total + raw_ref[s, k, part, :].astype(F32)
        average = jnp.sum(total, axis=1, keepdims=True) * (1.0 / D)
        squares = jnp.zeros((some, width), F32)
        for s, k in blocks:
            centred = raw_ref[s, k, part, :].astype(F32) - average
            squares = squares + centred * centred
        variance = jnp.sum(squares, axis=1, keepdims=True) * (1.0 / D)
        inverse = lax.rsqrt(variance + 1e-06)
        for s, k in blocks:
            h = lax.rem(place_ref[2] + GRID - k, GRID)
            centred = raw_ref[s, k, part, :].astype(F32) - average
            scale = mod_ref[1, h, s : s + 1, :]
            move = mod_ref[0, h, s : s + 1, :]
            start = pl.multiple_of((h * GRID + s) * width, HD)
            out_ref[part, pl.ds(start, width)] = (
                centred * inverse * (1.0 + scale) + move
            ).astype(BF)
        pltpu.make_async_copy(out_ref.at[part], sent_ref.at[part], sems.at[i]).start()
        return carry

    lax.fori_loop(0, rows // some, one_piece, 0)
    for i in range(rows // some):
        part = pl.ds(i * some, some)
        pltpu.make_async_copy(out_ref.at[part], sent_ref.at[part], sems.at[i]).wait()


def pick_kernel(place_ref, *refs):
    for source, target in zip(refs[:GRID], refs[GRID:]):
        target[0] = source[...]


def project_kernel(place_ref, own_ref, other_ref, weight_ref, q_gain_ref, k_gain_ref, q_ref, kv_ref, held, own, sems):
    rows = own_ref.shape[0]
    depth = held.shape[1]
    copies = [
        pltpu.make_async_copy(
            weight_ref.at[place_ref[0], pl.ds(i * depth, depth), :], held.at[i], sems.at[i]
        )
        for i in range(held.shape[0])
    ]
    more = [
        pltpu.make_async_copy(
            own_ref.at[:, pl.ds(i * depth, depth)], own.at[i], sems.at[held.shape[0] + i]
        )
        for i in range(held.shape[0])
    ]
    for first, second in zip(copies, more):
        first.start()
        second.start()
    total = None
    for i, copy in enumerate(copies):
        part = slice(i * depth, (i + 1) * depth)
        more[i].wait()
        hidden = jnp.concatenate([own[i], other_ref[:, part]], axis=0)
        copy.wait()
        product = jnp.dot(hidden, held[i], preferred_element_type=F32)
        total = product if total is None else total + product
    for t in range(2):
        here = slice(t * rows, (t + 1) * rows)
        for j, gain_ref in ((0, q_gain_ref), (1, k_gain_ref)):
            values = total[here, j * HD : (j + 1) * HD]
            squares = jnp.mean(values * values, axis=1, keepdims=True)
            normed = (values * lax.rsqrt(squares + 1e-06) * gain_ref[...]).astype(BF)
            if j == 0:
                q_ref[t] = normed
            else:
                for copy in range(GRID):
                    kv_ref[copy, 0, t] = normed
        values = total[here, 2 * HD :].astype(BF)
        for copy in range(GRID):
            kv_ref[copy, 1, t] = values


def attend_kernel(place_ref, q0, q1, q2, q3, kv_ref, out_ref, k_all, v_all):
    rows = q0.shape[1]
    blocks = 2 * GRID
    for g in range(GRID):
        for t in range(2):
            part = slice((2 * g + t) * rows, (2 * g + t + 1) * rows)
            k_all[part, :] = kv_ref[g, 0, t]
            v_all[part, :HD] = kv_ref[g, 1, t]
    v_all[:, HD:] = jnp.ones((blocks * rows, HD), BF)

    chunk = 512
    lane = lax.broadcasted_iota(jnp.int32, (HD, HD), 1)
    line = lax.broadcasted_iota(jnp.int32, (HD, HD), 0)
    sub = lax.broadcasted_iota(jnp.int32, (16, HD), 0)
    rest = rows - HD
    for k, q_ref in enumerate((q0, q1, q2, q3)):
        queries = jnp.concatenate([q_ref[0], q_ref[1]], axis=0)
        both = jnp.zeros((2 * rows, 2 * HD), F32)
        for c in range(blocks * rows // chunk):
            part = slice(c * chunk, (c + 1) * chunk)
            scores = lax.dot_general(
                queries, k_all[part, :], (((1,), (1,)), ((), ())), preferred_element_type=F32
            )
            weights = jnp.exp2(scores * (LOG2E / math.sqrt(HD))).astype(BF)
            both = both + jnp.dot(weights, v_all[part, :], preferred_element_type=F32)
        for t in range(2):
            target = 2 * lax.rem(place_ref[1] + GRID - k, GRID) + lax.rem(place_ref[0] + t, 2)
            out_ref[target, :rows, :] = both[t * rows : (t + 1) * rows, :HD].astype(BF)
            totals = both[t * rows : (t + 1) * rows, HD:]
            first = jnp.sum(jnp.where(lane == line, totals[:HD], 0.0), axis=0, keepdims=True)
            second = jnp.sum(
                jnp.where(lane[:rest] == line[:rest], totals[HD:], 0.0), axis=0, keepdims=True
            )
            first_high = first.astype(BF).astype(F32)
            second_high = second.astype(BF).astype(F32)
            packed = jnp.where(sub == 0, first_high, 0.0)
            packed = jnp.where(sub == 1, second_high, packed)
            packed = jnp.where(sub == 2, first - first_high, packed)
            packed = jnp.where(sub == 3, second - second_high, packed)
            out_ref[target, rows:, :] = packed.astype(BF)


def combine_kernel(parts_ref, out_ref):
    rows = out_ref.shape[1]
    lane = lax.broadcasted_iota(jnp.int32, (HD, HD), 1)
    line = lax.broadcasted_iota(jnp.int32, (HD, HD), 0)
    rest = rows - HD
    for h in range(2):
        numer = jnp.zeros((rows, HD), F32)
        packed = jnp.zeros((16, HD), F32)
        for g in range(GRID):
            numer = numer + parts_ref[2 * g + h, :rows, :].astype(F32)
            packed = packed + parts_ref[2 * g + h, rows:, :].astype(F32)
        first = packed[0:1] + packed[2:3]
        second = packed[1:2] + packed[3:4]
        first = jnp.sum(jnp.where(lane == line, first, 0.0), axis=1, keepdims=True)
        second = jnp.sum(
            jnp.where(lane[:rest] == line[:rest], second, 0.0), axis=1, keepdims=True
        )
        part = slice(h * HD, (h + 1) * HD)
        upper = (numer[:HD] / first).astype(BF)
        lower = (numer[HD:] / second).astype(BF)
        for copy in range(GRID):
            out_ref[copy, :HD, part] = upper
            out_ref[copy, HD:, part] = lower


def branch_kernel(place_ref, a_ref, w0, w1, w2, w3, *out_refs):
    for k, out_ref in enumerate(out_refs):
        total = jnp.zeros(out_ref.shape, F32)
        for away, w_ref in enumerate((w0, w1, w2, w3)):
            total = total + jnp.dot(
                a_ref[lax.rem(place_ref[3] + GRID - away, GRID)],
                w_ref[lax.rem(place_ref[2] + k, GRID)],
                preferred_element_type=F32,
            )
        out_ref[...] = total.astype(BF)


def per_device(latents, train_qkv, ema_qkv, q_gain, k_gain, out_weight, modulation, timestep, step):
    rows, width = latents.shape
    channels = ema_qkv.shape[2]
    blocks = GRID * GRID
    by_head = pl.pallas_call(
        average_kernel,
        in_specs=[
            pl.BlockSpec(memory_space=pltpu.SMEM),
            pl.BlockSpec(memory_space=pltpu.VMEM),
            pl.BlockSpec(memory_space=pltpu.VMEM),
        ],
        out_specs=pl.BlockSpec(memory_space=pltpu.VMEM),
        out_shape=jax.ShapeDtypeStruct((2, rows, 3 * HD), BF),
        name="average",
    )(step, ema_qkv, train_qkv)
    full_weights = lax.all_gather(by_head, TOKENS, axis=1, tiled=True)

    place = jnp.stack(
        [lax.axis_index(name).astype(jnp.int32) for name in ("core", "y", "head", "seq")]
    )

    def column(k):
        return lambda i, place: (0, i * GRID + lax.rem(place[3] + k, GRID))

    out_parts = pl.pallas_call(
        pick_kernel,
        grid_spec=pltpu.PrefetchScalarGridSpec(
            num_scalar_prefetch=1,
            grid=(GRID,),
            in_specs=[pl.BlockSpec((channels, width), column(k)) for k in range(GRID)],
            out_specs=[pl.BlockSpec((1, channels, width), lambda i, place: (i, 0, 0))] * GRID,
        ),
        out_shape=[jax.ShapeDtypeStruct((GRID, channels, width), BF)] * GRID,
        name="pick",
    )(place, *([out_weight] * GRID))

    mod_row = lax.dynamic_index_in_dim(modulation, timestep[0], 0, keepdims=False)
    half = rows // 2
    before = lax.ppermute(latents, "head", shift(1))
    after = lax.ppermute(latents, "head", shift(3))
    far_low = lax.ppermute(before[:half], "head", shift(1))
    far_high = lax.ppermute(after[half:], "head", shift(3))
    in_smem = pl.BlockSpec(memory_space=pltpu.SMEM)
    in_vmem = pl.BlockSpec(memory_space=pltpu.VMEM)
    raw = pl.pallas_call(
        spread_kernel,
        in_specs=[in_vmem] * (GRID + 1),
        out_specs=in_vmem,
        out_shape=jax.ShapeDtypeStruct((GRID, GRID, rows, width), BF),
        name="spread",
    )(latents, before, far_low, far_high, after)
    raw = lax.all_to_all(raw, "seq", 0, 0, tiled=True)
    out0, out1, out2, out3 = out_parts
    raw, out2 = lax.optimization_barrier((raw, out2))
    out2 = lax.ppermute(out2, "seq", shift(2))
    hidden = pl.pallas_call(
        norm_kernel,
        in_specs=[in_smem, in_vmem, in_vmem],
        out_specs=pl.BlockSpec(memory_space=pltpu.HBM),
        out_shape=jax.ShapeDtypeStruct((rows, blocks * width), BF),
        scratch_shapes=[
            pltpu.VMEM((rows, blocks * width), BF),
            pltpu.SemaphoreType.DMA((rows // 32,)),
        ],
        compiler_params=PARAMS,
        name="norm",
    )(place, raw, mod_row.reshape(3, GRID, GRID, width))
    sibling = lax.ppermute(hidden, "core", [(0, 1), (1, 0)])

    depth = D // GRID
    in_hbm = pl.BlockSpec(memory_space=pltpu.HBM)
    queries, pairs = pl.pallas_call(
        project_kernel,
        in_specs=[in_smem, in_hbm, in_vmem, in_hbm, in_vmem, in_vmem],
        out_specs=[in_vmem, in_vmem],
        out_shape=[
            jax.ShapeDtypeStruct((2, rows, HD), BF),
            jax.ShapeDtypeStruct((GRID, 2, 2, rows, HD), BF),
        ],
        scratch_shapes=[
            pltpu.VMEM((GRID, depth, 3 * HD), BF),
            pltpu.VMEM((GRID, rows, depth), BF),
            pltpu.SemaphoreType.DMA((2 * GRID,)),
        ],
        compiler_params=PARAMS,
        name="project",
    )(
        place,
        pltpu.with_memory_space_constraint(hidden, pltpu.HBM),
        sibling,
        pltpu.with_memory_space_constraint(full_weights, pltpu.HBM),
        q_gain.reshape(1, HD),
        k_gain.reshape(1, HD),
    )

    pairs = lax.all_to_all(pairs, "zl", 0, 0, tiled=True)
    queries = [queries] + [lax.ppermute(queries, "y", shift(k)) for k in (1, 2, 3)]

    sent = rows + 16
    parts = pl.pallas_call(
        attend_kernel,
        in_specs=[in_smem] + [in_vmem] * (GRID + 1),
        out_specs=in_vmem,
        out_shape=jax.ShapeDtypeStruct((2 * GRID, sent, HD), BF),
        scratch_shapes=[
            pltpu.VMEM((2 * GRID * rows, HD), BF),
            pltpu.VMEM((2 * GRID * rows, 2 * HD), BF),
        ],
        compiler_params=PARAMS,
        name="attend",
    )(place, *queries, pairs)
    parts, out1, out2, out3 = lax.optimization_barrier((parts, out1, out2, out3))
    parts = lax.all_to_all(parts, ("y", "core"), 0, 0, tiled=True)
    out1 = lax.ppermute(out1, "seq", shift(1))
    out3 = lax.ppermute(out3, "seq", shift(3))
    around = pl.pallas_call(
        combine_kernel,
        in_specs=[in_vmem],
        out_specs=in_vmem,
        out_shape=jax.ShapeDtypeStruct((GRID, rows, channels), BF),
        compiler_params=PARAMS,
        name="combine",
    )(parts)
    around = lax.all_to_all(around, "seq", 0, 0, tiled=True)
    outs = pl.pallas_call(
        branch_kernel,
        in_specs=[in_smem] + [in_vmem] * (GRID + 1),
        out_specs=[in_vmem] * GRID,
        out_shape=[jax.ShapeDtypeStruct((rows, width), BF)] * GRID,
        compiler_params=PARAMS,
        name="branch",
    )(place, around, out0, out1, out2, out3)
    shares = [lax.ppermute(outs[k], "head", shift(k)) for k in (2, 1, 3)]
    summed = outs[0].astype(F32)
    for share in shares:
        summed = summed + share.astype(F32)
    position = lax.axis_index(("head", "seq")) * width
    gate = lax.dynamic_slice_in_dim(mod_row[2], position, width, 0)
    return (latents.astype(F32) + gate[None, :] * summed).astype(BF)


def solution(mesh):
    fine = Mesh(
        mesh.devices.reshape(GRID, GRID, 2, GRID, GRID), ("y", "zl", "core", "head", "seq")
    )
    in_specs = (
        P(TOKENS, ("head", "seq")),
        P(None, TOKENS, ("head", "seq")),
        P(None, TOKENS, ("head", "seq")),
        P(),
        P(),
        P(("head", "seq"), None),
        P(),
        P(),
        P(),
    )
    out_specs = P(TOKENS, ("head", "seq"))
    return jax.shard_map(
        per_device, mesh=fine, in_specs=in_specs, out_specs=out_specs, check_vma=False
    )
```

```python
import math

import jax
import jax.numpy as jnp
from jax import lax
from jax.experimental import pallas as pl
from jax.experimental.pallas import tpu as pltpu
from jax.sharding import Mesh
from jax.sharding import PartitionSpec as P

D = 6144
HD = 128
GRID = 4
BF = jnp.bfloat16
F32 = jnp.float32
LOG2E = 1.4426950408889634
TOKENS = ("y", "zl", "core")
PARAMS = pltpu.CompilerParams(vmem_limit_bytes=24 << 20)


def shift(amount):
    return [(i, (i + amount) % GRID) for i in range(GRID)]


def average_kernel(step_ref, ema_ref, train_ref, out_ref):
    stepped = jnp.full((1, HD), step_ref[0], jnp.int32).astype(F32)
    decay = (1.0 + stepped) / (10.0 + stepped)
    for h in range(2):
        for j in range(3):
            part = slice(h * HD, (h + 1) * HD)
            ema = ema_ref[j, :, part].astype(F32)
            train = train_ref[j, :, part].astype(F32)
            out_ref[h, :, j * HD : (j + 1) * HD] = (decay * ema + (1.0 - decay) * train).astype(BF)


def spread_kernel(own_ref, before_ref, low_ref, high_ref, after_ref, out_ref):
    half = low_ref.shape[0]
    for copy in range(GRID):
        out_ref[copy, 0] = own_ref[...]
        out_ref[copy, 1] = before_ref[...]
        out_ref[copy, 2, :half] = low_ref[...]
        out_ref[copy, 2, half:] = high_ref[...]
        out_ref[copy, 3] = after_ref[...]


def norm_kernel(place_ref, raw_ref, mod_ref, sent_ref, out_ref, sems):
    blocks = [(s, k) for s in range(GRID) for k in range(GRID)]
    rows, width = raw_ref.shape[2], raw_ref.shape[3]
    some = 32

    def one_piece(i, carry):
        part = pl.ds(pl.multiple_of(i * some, some), some)
        total = jnp.zeros((some, width), F32)
        for s, k in blocks:
            total = total + raw_ref[s, k, part, :].astype(F32)
        average = jnp.sum(total, axis=1, keepdims=True) * (1.0 / D)
        squares = jnp.zeros((some, width), F32)
        for s, k in blocks:
            centred = raw_ref[s, k, part, :].astype(F32) - average
            squares = squares + centred * centred
        variance = jnp.sum(squares, axis=1, keepdims=True) * (1.0 / D)
        inverse = lax.rsqrt(variance + 1e-06)
        for s, k in blocks:
            h = lax.rem(place_ref[2] + GRID - k, GRID)
            centred = raw_ref[s, k, part, :].astype(F32) - average
            scale = mod_ref[1, h, s : s + 1, :]
            move = mod_ref[0, h, s : s + 1, :]
            start = pl.multiple_of((h * GRID + s) * width, HD)
            out_ref[part, pl.ds(start, width)] = (
                centred * inverse * (1.0 + scale) + move
            ).astype(BF)
        pltpu.make_async_copy(out_ref.at[part], sent_ref.at[part], sems.at[i]).start()
        return carry

    lax.fori_loop(0, rows // some, one_piece, 0)
    for i in range(rows // some):
        part = pl.ds(i * some, some)
        pltpu.make_async_copy(out_ref.at[part], sent_ref.at[part], sems.at[i]).wait()


def pick_kernel(place_ref, *refs):
    for source, target in zip(refs[:GRID], refs[GRID:]):
        target[0] = source[...]


def project_kernel(place_ref, own_ref, other_ref, weight_ref, q_gain_ref, k_gain_ref, q_ref, kv_ref, held, own, sems):
    rows = own_ref.shape[0]
    depth = held.shape[1]
    copies = [
        pltpu.make_async_copy(
            weight_ref.at[place_ref[0], pl.ds(i * depth, depth), :], held.at[i], sems.at[i]
        )
        for i in range(held.shape[0])
    ]
    more = [
        pltpu.make_async_copy(
            own_ref.at[:, pl.ds(i * depth, depth)], own.at[i], sems.at[held.shape[0] + i]
        )
        for i in range(held.shape[0])
    ]
    for first, second in zip(copies, more):
        first.start()
        second.start()
    total = None
    for i, copy in enumerate(copies):
        part = slice(i * depth, (i + 1) * depth)
        more[i].wait()
        hidden = jnp.concatenate([own[i], other_ref[:, part]], axis=0)
        copy.wait()
        product = jnp.dot(hidden, held[i], preferred_element_type=F32)
        total = product if total is None else total + product
    for t in range(2):
        here = slice(t * rows, (t + 1) * rows)
        for j, gain_ref in ((0, q_gain_ref), (1, k_gain_ref)):
            values = total[here, j * HD : (j + 1) * HD]
            squares = jnp.mean(values * values, axis=1, keepdims=True)
            normed = (values * lax.rsqrt(squares + 1e-06) * gain_ref[...]).astype(BF)
            if j == 0:
                q_ref[t] = normed
            else:
                for copy in range(GRID):
                    kv_ref[copy, 0, t] = normed
        values = total[here, 2 * HD :].astype(BF)
        for copy in range(GRID):
            kv_ref[copy, 1, t] = values


def attend_kernel(place_ref, q0, q1, q2, q3, kv_ref, out_ref, k_all, v_all):
    rows = q0.shape[1]
    blocks = 2 * GRID
    for g in range(GRID):
        for t in range(2):
            part = slice((2 * g + t) * rows, (2 * g + t + 1) * rows)
            k_all[part, :] = kv_ref[g, 0, t]
            v_all[part, :HD] = kv_ref[g, 1, t]
    v_all[:, HD:] = jnp.ones((blocks * rows, HD), BF)

    chunk = 512
    lane = lax.broadcasted_iota(jnp.int32, (HD, HD), 1)
    line = lax.broadcasted_iota(jnp.int32, (HD, HD), 0)
    sub = lax.broadcasted_iota(jnp.int32, (16, HD), 0)
    rest = rows - HD
    for k, q_ref in enumerate((q0, q1, q2, q3)):
        queries = jnp.concatenate([q_ref[0], q_ref[1]], axis=0)
        both = jnp.zeros((2 * rows, 2 * HD), F32)
        for c in range(blocks * rows // chunk):
            part = slice(c * chunk, (c + 1) * chunk)
            scores = lax.dot_general(
                queries, k_all[part, :], (((1,), (1,)), ((), ())), preferred_element_type=F32
            )
            weights = jnp.exp2(scores * (LOG2E / math.sqrt(HD))).astype(BF)
            both = both + jnp.dot(weights, v_all[part, :], preferred_element_type=F32)
        for t in range(2):
            target = 2 * lax.rem(place_ref[1] + GRID - k, GRID) + lax.rem(place_ref[0] + t, 2)
            out_ref[target, :rows, :] = both[t * rows : (t + 1) * rows, :HD].astype(BF)
            totals = both[t * rows : (t + 1) * rows, HD:]
            first = jnp.sum(jnp.where(lane == line, totals[:HD], 0.0), axis=0, keepdims=True)
            second = jnp.sum(
                jnp.where(lane[:rest] == line[:rest], totals[HD:], 0.0), axis=0, keepdims=True
            )
            first_high = first.astype(BF).astype(F32)
            second_high = second.astype(BF).astype(F32)
            packed = jnp.where(sub == 0, first_high, 0.0)
            packed = jnp.where(sub == 1, second_high, packed)
            packed = jnp.where(sub == 2, first - first_high, packed)
            packed = jnp.where(sub == 3, second - second_high, packed)
            out_ref[target, rows:, :] = packed.astype(BF)


def combine_kernel(parts_ref, out_ref):
    rows = out_ref.shape[1]
    lane = lax.broadcasted_iota(jnp.int32, (HD, HD), 1)
    line = lax.broadcasted_iota(jnp.int32, (HD, HD), 0)
    rest = rows - HD
    for h in range(2):
        numer = jnp.zeros((rows, HD), F32)
        packed = jnp.zeros((16, HD), F32)
        for g in range(GRID):
            numer = numer + parts_ref[2 * g + h, :rows, :].astype(F32)
            packed = packed + parts_ref[2 * g + h, rows:, :].astype(F32)
        first = packed[0:1] + packed[2:3]
        second = packed[1:2] + packed[3:4]
        first = jnp.sum(jnp.where(lane == line, first, 0.0), axis=1, keepdims=True)
        second = jnp.sum(
            jnp.where(lane[:rest] == line[:rest], second, 0.0), axis=1, keepdims=True
        )
        part = slice(h * HD, (h + 1) * HD)
        upper = (numer[:HD] / first).astype(BF)
        lower = (numer[HD:] / second).astype(BF)
        for copy in range(GRID):
            out_ref[copy, :HD, part] = upper
            out_ref[copy, HD:, part] = lower


def branch_kernel(place_ref, a_ref, w0, w1, w2, w3, *out_refs):
    for k, out_ref in enumerate(out_refs):
        total = jnp.zeros(out_ref.shape, F32)
        for away, w_ref in enumerate((w0, w1, w2, w3)):
            total = total + jnp.dot(
                a_ref[lax.rem(place_ref[3] + GRID - away, GRID)],
                w_ref[lax.rem(place_ref[2] + k, GRID)],
                preferred_element_type=F32,
            )
        out_ref[...] = total.astype(BF)


def per_device(latents, train_qkv, ema_qkv, q_gain, k_gain, out_weight, modulation, timestep, step):
    rows, width = latents.shape
    channels = ema_qkv.shape[2]
    blocks = GRID * GRID
    by_head = pl.pallas_call(
        average_kernel,
        in_specs=[
            pl.BlockSpec(memory_space=pltpu.SMEM),
            pl.BlockSpec(memory_space=pltpu.VMEM),
            pl.BlockSpec(memory_space=pltpu.VMEM),
        ],
        out_specs=pl.BlockSpec(memory_space=pltpu.VMEM),
        out_shape=jax.ShapeDtypeStruct((2, rows, 3 * HD), BF),
        name="average",
    )(step, ema_qkv, train_qkv)
    full_weights = lax.all_gather(by_head, TOKENS, axis=1, tiled=True)

    place = jnp.stack(
        [lax.axis_index(name).astype(jnp.int32) for name in ("core", "y", "head", "seq")]
    )

    def column(k):
        return lambda i, place: (0, i * GRID + lax.rem(place[3] + k, GRID))

    out_parts = pl.pallas_call(
        pick_kernel,
        grid_spec=pltpu.PrefetchScalarGridSpec(
            num_scalar_prefetch=1,
            grid=(GRID,),
            in_specs=[pl.BlockSpec((channels, width), column(k)) for k in range(GRID)],
            out_specs=[pl.BlockSpec((1, channels, width), lambda i, place: (i, 0, 0))] * GRID,
        ),
        out_shape=[jax.ShapeDtypeStruct((GRID, channels, width), BF)] * GRID,
        name="pick",
    )(place, *([out_weight] * GRID))

    mod_row = lax.dynamic_index_in_dim(modulation, timestep[0], 0, keepdims=False)
    half = rows // 2
    before = lax.ppermute(latents, "head", shift(1))
    after = lax.ppermute(latents, "head", shift(3))
    far_low = lax.ppermute(before[:half], "head", shift(1))
    far_high = lax.ppermute(after[half:], "head", shift(3))
    in_smem = pl.BlockSpec(memory_space=pltpu.SMEM)
    in_vmem = pl.BlockSpec(memory_space=pltpu.VMEM)
    raw = pl.pallas_call(
        spread_kernel,
        in_specs=[in_vmem] * (GRID + 1),
        out_specs=in_vmem,
        out_shape=jax.ShapeDtypeStruct((GRID, GRID, rows, width), BF),
        compiler_params=PARAMS,
        name="spread",
    )(latents, before, far_low, far_high, after)
    raw = lax.all_to_all(raw, "seq", 0, 0, tiled=True)
    out0, out1, out2, out3 = out_parts
    raw, out1, out2, out3 = lax.optimization_barrier((raw, out1, out2, out3))
    out2 = lax.ppermute(out2, "seq", shift(2))
    hidden = pl.pallas_call(
        norm_kernel,
        in_specs=[in_smem, in_vmem, in_vmem],
        out_specs=pl.BlockSpec(memory_space=pltpu.HBM),
        out_shape=jax.ShapeDtypeStruct((rows, blocks * width), BF),
        scratch_shapes=[
            pltpu.VMEM((rows, blocks * width), BF),
            pltpu.SemaphoreType.DMA((rows // 32,)),
        ],
        compiler_params=PARAMS,
        name="norm",
    )(place, raw, mod_row.reshape(3, GRID, GRID, width))
    sibling = lax.ppermute(hidden, "core", [(0, 1), (1, 0)])

    depth = D // GRID
    in_hbm = pl.BlockSpec(memory_space=pltpu.HBM)
    queries, pairs = pl.pallas_call(
        project_kernel,
        in_specs=[in_smem, in_hbm, in_vmem, in_hbm, in_vmem, in_vmem],
        out_specs=[in_vmem, in_vmem],
        out_shape=[
            jax.ShapeDtypeStruct((2, rows, HD), BF),
            jax.ShapeDtypeStruct((GRID, 2, 2, rows, HD), BF),
        ],
        scratch_shapes=[
            pltpu.VMEM((GRID, depth, 3 * HD), BF),
            pltpu.VMEM((GRID, rows, depth), BF),
            pltpu.SemaphoreType.DMA((2 * GRID,)),
        ],
        compiler_params=PARAMS,
        name="project",
    )(
        place,
        pltpu.with_memory_space_constraint(hidden, pltpu.HBM),
        sibling,
        pltpu.with_memory_space_constraint(full_weights, pltpu.HBM),
        q_gain.reshape(1, HD),
        k_gain.reshape(1, HD),
    )

    pairs = lax.all_to_all(pairs, "zl", 0, 0, tiled=True)
    queries = [queries] + [lax.ppermute(queries, "y", shift(k)) for k in (1, 2, 3)]
    *queries, out1, out3 = lax.optimization_barrier((*queries, out1, out3))
    out1 = lax.ppermute(out1, "seq", shift(1))
    out3 = lax.ppermute(out3, "seq", shift(3))

    sent = rows + 16
    parts = pl.pallas_call(
        attend_kernel,
        in_specs=[in_smem] + [in_vmem] * (GRID + 1),
        out_specs=in_vmem,
        out_shape=jax.ShapeDtypeStruct((2 * GRID, sent, HD), BF),
        scratch_shapes=[
            pltpu.VMEM((2 * GRID * rows, HD), BF),
            pltpu.VMEM((2 * GRID * rows, 2 * HD), BF),
        ],
        compiler_params=PARAMS,
        name="attend",
    )(place, *queries, pairs)
    parts, out2 = lax.optimization_barrier((parts, out2))
    parts = lax.all_to_all(parts, ("y", "core"), 0, 0, tiled=True)
    around = pl.pallas_call(
        combine_kernel,
        in_specs=[in_vmem],
        out_specs=in_vmem,
        out_shape=jax.ShapeDtypeStruct((GRID, rows, channels), BF),
        compiler_params=PARAMS,
        name="combine",
    )(parts)
    around = lax.all_to_all(around, "seq", 0, 0, tiled=True)
    outs = pl.pallas_call(
        branch_kernel,
        in_specs=[in_smem] + [in_vmem] * (GRID + 1),
        out_specs=[in_vmem] * GRID,
        out_shape=[jax.ShapeDtypeStruct((rows, width), BF)] * GRID,
        compiler_params=PARAMS,
        name="branch",
    )(place, around, out0, out1, out2, out3)
    shares = [lax.ppermute(outs[k], "head", shift(k)) for k in (1, 3, 2)]
    summed = outs[0].astype(F32)
    for share in shares:
        summed = summed + share.astype(F32)
    position = lax.axis_index(("head", "seq")) * width
    gate = lax.dynamic_slice_in_dim(mod_row[2], position, width, 0)
    return (latents.astype(F32) + gate[None, :] * summed).astype(BF)


def solution(mesh):
    fine = Mesh(
        mesh.devices.reshape(GRID, GRID, 2, GRID, GRID), ("y", "zl", "core", "head", "seq")
    )
    in_specs = (
        P(TOKENS, ("head", "seq")),
        P(None, TOKENS, ("head", "seq")),
        P(None, TOKENS, ("head", "seq")),
        P(),
        P(),
        P(("head", "seq"), None),
        P(),
        P(),
        P(),
    )
    out_specs = P(TOKENS, ("head", "seq"))
    return jax.shard_map(
        per_device, mesh=fine, in_specs=in_specs, out_specs=out_specs, check_vma=False
    )
```

```python
import math

import jax
import jax.numpy as jnp
from jax import lax
from jax.experimental import pallas as pl
from jax.experimental.pallas import tpu as pltpu
from jax.sharding import Mesh
from jax.sharding import PartitionSpec as P

D = 6144
HD = 128
GRID = 4
BF = jnp.bfloat16
F32 = jnp.float32
LOG2E = 1.4426950408889634
TOKENS = ("y", "zl", "core")
PARAMS = pltpu.CompilerParams(vmem_limit_bytes=24 << 20)
SPREAD_PARAMS = pltpu.CompilerParams(vmem_limit_bytes=53 << 20)


def shift(amount):
    return [(i, (i + amount) % GRID) for i in range(GRID)]


def average_kernel(step_ref, ema_ref, train_ref, out_ref):
    stepped = jnp.full((1, HD), step_ref[0], jnp.int32).astype(F32)
    decay = (1.0 + stepped) / (10.0 + stepped)
    for h in range(2):
        for j in range(3):
            part = slice(h * HD, (h + 1) * HD)
            ema = ema_ref[j, :, part].astype(F32)
            train = train_ref[j, :, part].astype(F32)
            out_ref[h, :, j * HD : (j + 1) * HD] = (decay * ema + (1.0 - decay) * train).astype(BF)


def spread_kernel(own_ref, before_ref, low_ref, high_ref, after_ref, out_ref):
    half = low_ref.shape[0]
    for copy in range(GRID):
        out_ref[copy, 0] = own_ref[...]
        out_ref[copy, 1] = before_ref[...]
        out_ref[copy, 2, :half] = low_ref[...]
        out_ref[copy, 2, half:] = high_ref[...]
        out_ref[copy, 3] = after_ref[...]


def norm_kernel(place_ref, raw_ref, mod_ref, sent_ref, out_ref, sems):
    blocks = [(s, k) for s in range(GRID) for k in range(GRID)]
    rows, width = raw_ref.shape[2], raw_ref.shape[3]
    some = 32

    def one_piece(i, carry):
        part = pl.ds(pl.multiple_of(i * some, some), some)
        total = jnp.zeros((some, width), F32)
        for s, k in blocks:
            total = total + raw_ref[s, k, part, :].astype(F32)
        average = jnp.sum(total, axis=1, keepdims=True) * (1.0 / D)
        squares = jnp.zeros((some, width), F32)
        for s, k in blocks:
            centred = raw_ref[s, k, part, :].astype(F32) - average
            squares = squares + centred * centred
        variance = jnp.sum(squares, axis=1, keepdims=True) * (1.0 / D)
        inverse = lax.rsqrt(variance + 1e-06)
        for s, k in blocks:
            h = lax.rem(place_ref[2] + GRID - k, GRID)
            centred = raw_ref[s, k, part, :].astype(F32) - average
            scale = mod_ref[1, h, s : s + 1, :]
            move = mod_ref[0, h, s : s + 1, :]
            start = pl.multiple_of((h * GRID + s) * width, HD)
            out_ref[part, pl.ds(start, width)] = (
                centred * inverse * (1.0 + scale) + move
            ).astype(BF)
        pltpu.make_async_copy(out_ref.at[part], sent_ref.at[part], sems.at[i]).start()
        return carry

    lax.fori_loop(0, rows // some, one_piece, 0)
    for i in range(rows // some):
        part = pl.ds(i * some, some)
        pltpu.make_async_copy(out_ref.at[part], sent_ref.at[part], sems.at[i]).wait()


def pick_kernel(place_ref, *refs):
    for source, target in zip(refs[:GRID], refs[GRID:]):
        target[0] = source[...]


def project_kernel(place_ref, own_ref, other_ref, weight_ref, q_gain_ref, k_gain_ref, q_ref, kv_ref, held, own, sems):
    rows = own_ref.shape[0]
    depth = held.shape[1]
    copies = [
        pltpu.make_async_copy(
            weight_ref.at[place_ref[0], pl.ds(i * depth, depth), :], held.at[i], sems.at[i]
        )
        for i in range(held.shape[0])
    ]
    more = [
        pltpu.make_async_copy(
            own_ref.at[:, pl.ds(i * depth, depth)], own.at[i], sems.at[held.shape[0] + i]
        )
        for i in range(held.shape[0])
    ]
    for first, second in zip(copies, more):
        first.start()
        second.start()
    total = None
    for i, copy in enumerate(copies):
        part = slice(i * depth, (i + 1) * depth)
        more[i].wait()
        hidden = jnp.concatenate([own[i], other_ref[:, part]], axis=0)
        copy.wait()
        product = jnp.dot(hidden, held[i], preferred_element_type=F32)
        total = product if total is None else total + product
    for t in range(2):
        here = slice(t * rows, (t + 1) * rows)
        for j, gain_ref in ((0, q_gain_ref), (1, k_gain_ref)):
            values = total[here, j * HD : (j + 1) * HD]
            squares = jnp.mean(values * values, axis=1, keepdims=True)
            normed = (values * lax.rsqrt(squares + 1e-06) * gain_ref[...]).astype(BF)
            if j == 0:
                q_ref[t] = normed
            else:
                for copy in range(GRID):
                    kv_ref[copy, 0, t] = normed
        values = total[here, 2 * HD :].astype(BF)
        for copy in range(GRID):
            kv_ref[copy, 1, t] = values


def attend_kernel(place_ref, q0, q1, q2, q3, kv_ref, out_ref, k_all, v_all):
    rows = q0.shape[1]
    blocks = 2 * GRID
    for g in range(GRID):
        for t in range(2):
            part = slice((2 * g + t) * rows, (2 * g + t + 1) * rows)
            k_all[part, :] = kv_ref[g, 0, t]
            v_all[part, :HD] = kv_ref[g, 1, t]
    v_all[:, HD:] = jnp.ones((blocks * rows, HD), BF)

    chunk = 512
    lane = lax.broadcasted_iota(jnp.int32, (HD, HD), 1)
    line = lax.broadcasted_iota(jnp.int32, (HD, HD), 0)
    sub = lax.broadcasted_iota(jnp.int32, (16, HD), 0)
    rest = rows - HD
    for k, q_ref in enumerate((q0, q1, q2, q3)):
        queries = jnp.concatenate([q_ref[0], q_ref[1]], axis=0)
        both = jnp.zeros((2 * rows, 2 * HD), F32)
        for c in range(blocks * rows // chunk):
            part = slice(c * chunk, (c + 1) * chunk)
            scores = lax.dot_general(
                queries, k_all[part, :], (((1,), (1,)), ((), ())), preferred_element_type=F32
            )
            weights = jnp.exp2(scores * (LOG2E / math.sqrt(HD))).astype(BF)
            both = both + jnp.dot(weights, v_all[part, :], preferred_element_type=F32)
        for t in range(2):
            target = 2 * lax.rem(place_ref[1] + GRID - k, GRID) + lax.rem(place_ref[0] + t, 2)
            out_ref[target, :rows, :] = both[t * rows : (t + 1) * rows, :HD].astype(BF)
            totals = both[t * rows : (t + 1) * rows, HD:]
            first = jnp.sum(jnp.where(lane == line, totals[:HD], 0.0), axis=0, keepdims=True)
            second = jnp.sum(
                jnp.where(lane[:rest] == line[:rest], totals[HD:], 0.0), axis=0, keepdims=True
            )
            first_high = first.astype(BF).astype(F32)
            second_high = second.astype(BF).astype(F32)
            packed = jnp.where(sub == 0, first_high, 0.0)
            packed = jnp.where(sub == 1, second_high, packed)
            packed = jnp.where(sub == 2, first - first_high, packed)
            packed = jnp.where(sub == 3, second - second_high, packed)
            out_ref[target, rows:, :] = packed.astype(BF)


def combine_kernel(parts_ref, out_ref):
    rows = out_ref.shape[1]
    lane = lax.broadcasted_iota(jnp.int32, (HD, HD), 1)
    line = lax.broadcasted_iota(jnp.int32, (HD, HD), 0)
    rest = rows - HD
    for h in range(2):
        numer = jnp.zeros((rows, HD), F32)
        packed = jnp.zeros((16, HD), F32)
        for g in range(GRID):
            numer = numer + parts_ref[2 * g + h, :rows, :].astype(F32)
            packed = packed + parts_ref[2 * g + h, rows:, :].astype(F32)
        first = packed[0:1] + packed[2:3]
        second = packed[1:2] + packed[3:4]
        first = jnp.sum(jnp.where(lane == line, first, 0.0), axis=1, keepdims=True)
        second = jnp.sum(
            jnp.where(lane[:rest] == line[:rest], second, 0.0), axis=1, keepdims=True
        )
        part = slice(h * HD, (h + 1) * HD)
        upper = (numer[:HD] / first).astype(BF)
        lower = (numer[HD:] / second).astype(BF)
        for copy in range(GRID):
            out_ref[copy, :HD, part] = upper
            out_ref[copy, HD:, part] = lower


def branch_kernel(place_ref, a_ref, w0, w1, w2, w3, *out_refs):
    for k, out_ref in enumerate(out_refs):
        total = jnp.zeros(out_ref.shape, F32)
        for away, w_ref in enumerate((w0, w1, w2, w3)):
            total = total + jnp.dot(
                a_ref[lax.rem(place_ref[3] + GRID - away, GRID)],
                w_ref[lax.rem(place_ref[2] + k, GRID)],
                preferred_element_type=F32,
            )
        out_ref[...] = total.astype(BF)


def per_device(latents, train_qkv, ema_qkv, q_gain, k_gain, out_weight, modulation, timestep, step):
    rows, width = latents.shape
    channels = ema_qkv.shape[2]
    blocks = GRID * GRID
    by_head = pl.pallas_call(
        average_kernel,
        in_specs=[
            pl.BlockSpec(memory_space=pltpu.SMEM),
            pl.BlockSpec(memory_space=pltpu.VMEM),
            pl.BlockSpec(memory_space=pltpu.VMEM),
        ],
        out_specs=pl.BlockSpec(memory_space=pltpu.VMEM),
        out_shape=jax.ShapeDtypeStruct((2, rows, 3 * HD), BF),
        name="average",
    )(step, ema_qkv, train_qkv)
    full_weights = lax.all_gather(by_head, TOKENS, axis=1, tiled=True)

    place = jnp.stack(
        [lax.axis_index(name).astype(jnp.int32) for name in ("core", "y", "head", "seq")]
    )

    def column(k):
        return lambda i, place: (0, i * GRID + lax.rem(place[3] + k, GRID))

    out_parts = pl.pallas_call(
        pick_kernel,
        grid_spec=pltpu.PrefetchScalarGridSpec(
            num_scalar_prefetch=1,
            grid=(GRID,),
            in_specs=[pl.BlockSpec((channels, width), column(k)) for k in range(GRID)],
            out_specs=[pl.BlockSpec((1, channels, width), lambda i, place: (i, 0, 0))] * GRID,
        ),
        out_shape=[jax.ShapeDtypeStruct((GRID, channels, width), BF)] * GRID,
        name="pick",
    )(place, *([out_weight] * GRID))

    mod_row = lax.dynamic_index_in_dim(modulation, timestep[0], 0, keepdims=False)
    half = rows // 2
    before = lax.ppermute(latents, "head", shift(1))
    after = lax.ppermute(latents, "head", shift(3))
    far_low = lax.ppermute(before[:half], "head", shift(1))
    far_high = lax.ppermute(after[half:], "head", shift(3))
    in_smem = pl.BlockSpec(memory_space=pltpu.SMEM)
    in_vmem = pl.BlockSpec(memory_space=pltpu.VMEM)
    raw = pl.pallas_call(
        spread_kernel,
        in_specs=[in_vmem] * (GRID + 1),
        out_specs=in_vmem,
        out_shape=jax.ShapeDtypeStruct((GRID, GRID, rows, width), BF),
        compiler_params=SPREAD_PARAMS,
        name="spread",
    )(latents, before, far_low, far_high, after)
    raw = lax.all_to_all(raw, "seq", 0, 0, tiled=True)
    out0, out1, out2, out3 = out_parts
    raw, out1, out2, out3 = lax.optimization_barrier((raw, out1, out2, out3))
    out2 = lax.ppermute(out2, "seq", shift(2))
    hidden = pl.pallas_call(
        norm_kernel,
        in_specs=[in_smem, in_vmem, in_vmem],
        out_specs=pl.BlockSpec(memory_space=pltpu.HBM),
        out_shape=jax.ShapeDtypeStruct((rows, blocks * width), BF),
        scratch_shapes=[
            pltpu.VMEM((rows, blocks * width), BF),
            pltpu.SemaphoreType.DMA((rows // 32,)),
        ],
        compiler_params=PARAMS,
        name="norm",
    )(place, raw, mod_row.reshape(3, GRID, GRID, width))
    sibling = lax.ppermute(hidden, "core", [(0, 1), (1, 0)])

    depth = D // GRID
    in_hbm = pl.BlockSpec(memory_space=pltpu.HBM)
    queries, pairs = pl.pallas_call(
        project_kernel,
        in_specs=[in_smem, in_hbm, in_vmem, in_hbm, in_vmem, in_vmem],
        out_specs=[in_vmem, in_vmem],
        out_shape=[
            jax.ShapeDtypeStruct((2, rows, HD), BF),
            jax.ShapeDtypeStruct((GRID, 2, 2, rows, HD), BF),
        ],
        scratch_shapes=[
            pltpu.VMEM((GRID, depth, 3 * HD), BF),
            pltpu.VMEM((GRID, rows, depth), BF),
            pltpu.SemaphoreType.DMA((2 * GRID,)),
        ],
        compiler_params=PARAMS,
        name="project",
    )(
        place,
        pltpu.with_memory_space_constraint(hidden, pltpu.HBM),
        sibling,
        pltpu.with_memory_space_constraint(full_weights, pltpu.HBM),
        q_gain.reshape(1, HD),
        k_gain.reshape(1, HD),
    )

    pairs = lax.all_to_all(pairs, "zl", 0, 0, tiled=True)
    queries = [queries] + [lax.ppermute(queries, "y", shift(k)) for k in (1, 2, 3)]
    *queries, out1, out3 = lax.optimization_barrier((*queries, out1, out3))
    out1 = lax.ppermute(out1, "seq", shift(1))
    out3 = lax.ppermute(out3, "seq", shift(3))

    sent = rows + 16
    parts = pl.pallas_call(
        attend_kernel,
        in_specs=[in_smem] + [in_vmem] * (GRID + 1),
        out_specs=in_vmem,
        out_shape=jax.ShapeDtypeStruct((2 * GRID, sent, HD), BF),
        scratch_shapes=[
            pltpu.VMEM((2 * GRID * rows, HD), BF),
            pltpu.VMEM((2 * GRID * rows, 2 * HD), BF),
        ],
        compiler_params=PARAMS,
        name="attend",
    )(place, *queries, pairs)
    parts, out2 = lax.optimization_barrier((parts, out2))
    parts = lax.all_to_all(parts, ("y", "core"), 0, 0, tiled=True)
    around = pl.pallas_call(
        combine_kernel,
        in_specs=[in_vmem],
        out_specs=in_vmem,
        out_shape=jax.ShapeDtypeStruct((GRID, rows, channels), BF),
        compiler_params=PARAMS,
        name="combine",
    )(parts)
    around = lax.all_to_all(around, "seq", 0, 0, tiled=True)
    outs = pl.pallas_call(
        branch_kernel,
        in_specs=[in_smem] + [in_vmem] * (GRID + 1),
        out_specs=[in_vmem] * GRID,
        out_shape=[jax.ShapeDtypeStruct((rows, width), BF)] * GRID,
        compiler_params=PARAMS,
        name="branch",
    )(place, around, out0, out1, out2, out3)
    shares = [lax.ppermute(outs[k], "head", shift(k)) for k in (1, 3, 2)]
    summed = outs[0].astype(F32)
    for share in shares:
        summed = summed + share.astype(F32)
    position = lax.axis_index(("head", "seq")) * width
    gate = lax.dynamic_slice_in_dim(mod_row[2], position, width, 0)
    return (latents.astype(F32) + gate[None, :] * summed).astype(BF)


def solution(mesh):
    fine = Mesh(
        mesh.devices.reshape(GRID, GRID, 2, GRID, GRID), ("y", "zl", "core", "head", "seq")
    )
    in_specs = (
        P(TOKENS, ("head", "seq")),
        P(None, TOKENS, ("head", "seq")),
        P(None, TOKENS, ("head", "seq")),
        P(),
        P(),
        P(("head", "seq"), None),
        P(),
        P(),
        P(),
    )
    out_specs = P(TOKENS, ("head", "seq"))
    return jax.shard_map(
        per_device, mesh=fine, in_specs=in_specs, out_specs=out_specs, check_vma=False
    )
```

```python
import math

import jax
import jax.numpy as jnp
from jax import lax
from jax.experimental import pallas as pl
from jax.experimental.pallas import tpu as pltpu
from jax.sharding import Mesh
from jax.sharding import PartitionSpec as P

D = 6144
HD = 128
GRID = 4
BF = jnp.bfloat16
F32 = jnp.float32
LOG2E = 1.4426950408889634
TOKENS = ("y", "zl", "core")
PARAMS = pltpu.CompilerParams(vmem_limit_bytes=24 << 20)
SPREAD_PARAMS = pltpu.CompilerParams(vmem_limit_bytes=53 << 20)


def shift(amount):
    return [(i, (i + amount) % GRID) for i in range(GRID)]


def average_kernel(step_ref, ema_ref, train_ref, out_ref):
    stepped = jnp.full((1, HD), step_ref[0], jnp.int32).astype(F32)
    decay = (1.0 + stepped) / (10.0 + stepped)
    for h in range(2):
        for j in range(3):
            part = slice(h * HD, (h + 1) * HD)
            ema = ema_ref[j, :, part].astype(F32)
            train = train_ref[j, :, part].astype(F32)
            out_ref[h, :, j * HD : (j + 1) * HD] = (decay * ema + (1.0 - decay) * train).astype(BF)


def spread_kernel(own_ref, before_ref, low_ref, high_ref, after_ref, out_ref):
    half = low_ref.shape[0]
    for copy in range(GRID):
        out_ref[copy, 0] = own_ref[...]
        out_ref[copy, 1] = before_ref[...]
        out_ref[copy, 2, :half] = low_ref[...]
        out_ref[copy, 2, half:] = high_ref[...]
        out_ref[copy, 3] = after_ref[...]


def norm_kernel(place_ref, raw_ref, mod_ref, sent_ref, out_ref, sems):
    blocks = [(s, k) for s in range(GRID) for k in range(GRID)]
    rows, width = raw_ref.shape[2], raw_ref.shape[3]
    some = 32

    def one_piece(i, carry):
        part = pl.ds(pl.multiple_of(i * some, some), some)
        total = jnp.zeros((some, width), F32)
        for s, k in blocks:
            total = total + raw_ref[s, k, part, :].astype(F32)
        average = jnp.sum(total, axis=1, keepdims=True) * (1.0 / D)
        squares = jnp.zeros((some, width), F32)
        for s, k in blocks:
            centred = raw_ref[s, k, part, :].astype(F32) - average
            squares = squares + centred * centred
        variance = jnp.sum(squares, axis=1, keepdims=True) * (1.0 / D)
        inverse = lax.rsqrt(variance + 1e-06)
        for s, k in blocks:
            h = lax.rem(place_ref[2] + GRID - k, GRID)
            centred = raw_ref[s, k, part, :].astype(F32) - average
            scale = mod_ref[1, h, s : s + 1, :]
            move = mod_ref[0, h, s : s + 1, :]
            start = pl.multiple_of((h * GRID + s) * width, HD)
            out_ref[part, pl.ds(start, width)] = (
                centred * inverse * (1.0 + scale) + move
            ).astype(BF)
        pltpu.make_async_copy(out_ref.at[part], sent_ref.at[part], sems.at[i]).start()
        return carry

    lax.fori_loop(0, rows // some, one_piece, 0)
    for i in range(rows // some):
        part = pl.ds(i * some, some)
        pltpu.make_async_copy(out_ref.at[part], sent_ref.at[part], sems.at[i]).wait()


def pick_kernel(place_ref, *refs):
    for source, target in zip(refs[:GRID], refs[GRID:]):
        target[0] = source[...]


def project_kernel(place_ref, own_ref, other_ref, weight_ref, q_gain_ref, k_gain_ref, q_ref, kv_ref, held, own, sems):
    rows = own_ref.shape[0]
    depth = held.shape[1]
    copies = [
        pltpu.make_async_copy(
            weight_ref.at[place_ref[0], pl.ds(i * depth, depth), :], held.at[i], sems.at[i]
        )
        for i in range(held.shape[0])
    ]
    more = [
        pltpu.make_async_copy(
            own_ref.at[:, pl.ds(i * depth, depth)], own.at[i], sems.at[held.shape[0] + i]
        )
        for i in range(held.shape[0])
    ]
    for first, second in zip(copies, more):
        first.start()
        second.start()
    total = None
    for i, copy in enumerate(copies):
        part = slice(i * depth, (i + 1) * depth)
        more[i].wait()
        hidden = jnp.concatenate([own[i], other_ref[:, part]], axis=0)
        copy.wait()
        product = jnp.dot(hidden, held[i], preferred_element_type=F32)
        total = product if total is None else total + product
    for t in range(2):
        here = slice(t * rows, (t + 1) * rows)
        for j, gain_ref in ((0, q_gain_ref), (1, k_gain_ref)):
            values = total[here, j * HD : (j + 1) * HD]
            squares = jnp.mean(values * values, axis=1, keepdims=True)
            normed = (values * lax.rsqrt(squares + 1e-06) * gain_ref[...]).astype(BF)
            if j == 0:
                q_ref[t] = normed
            else:
                for copy in range(GRID):
                    kv_ref[copy, 0, t] = normed
        values = total[here, 2 * HD :].astype(BF)
        for copy in range(GRID):
            kv_ref[copy, 1, t] = values


def attend_kernel(place_ref, q0, q1, q2, q3, kv_ref, out_ref, k_all, v_all):
    rows = q0.shape[1]
    blocks = 2 * GRID
    for g in range(GRID):
        for t in range(2):
            part = slice((2 * g + t) * rows, (2 * g + t + 1) * rows)
            k_all[part, :] = kv_ref[g, 0, t]
            v_all[part, :HD] = kv_ref[g, 1, t]
    v_all[:, HD:] = jnp.ones((blocks * rows, HD), BF)

    chunk = 512
    lane = lax.broadcasted_iota(jnp.int32, (HD, HD), 1)
    line = lax.broadcasted_iota(jnp.int32, (HD, HD), 0)
    sub = lax.broadcasted_iota(jnp.int32, (16, HD), 0)
    rest = rows - HD
    for k, q_ref in enumerate((q0, q1, q2, q3)):
        queries = jnp.concatenate([q_ref[0], q_ref[1]], axis=0)
        both = jnp.zeros((2 * rows, 2 * HD), F32)
        for c in range(blocks * rows // chunk):
            part = slice(c * chunk, (c + 1) * chunk)
            scores = lax.dot_general(
                queries, k_all[part, :], (((1,), (1,)), ((), ())), preferred_element_type=F32
            )
            weights = jnp.exp2(scores * (LOG2E / math.sqrt(HD))).astype(BF)
            both = both + jnp.dot(weights, v_all[part, :], preferred_element_type=F32)
        for t in range(2):
            target = 2 * lax.rem(place_ref[1] + GRID - k, GRID) + lax.rem(place_ref[0] + t, 2)
            out_ref[target, :rows, :] = both[t * rows : (t + 1) * rows, :HD].astype(BF)
            totals = both[t * rows : (t + 1) * rows, HD:]
            first = jnp.sum(jnp.where(lane == line, totals[:HD], 0.0), axis=0, keepdims=True)
            second = jnp.sum(
                jnp.where(lane[:rest] == line[:rest], totals[HD:], 0.0), axis=0, keepdims=True
            )
            first_high = first.astype(BF).astype(F32)
            second_high = second.astype(BF).astype(F32)
            packed = jnp.where(sub == 0, first_high, 0.0)
            packed = jnp.where(sub == 1, second_high, packed)
            packed = jnp.where(sub == 2, first - first_high, packed)
            packed = jnp.where(sub == 3, second - second_high, packed)
            out_ref[target, rows:, :] = packed.astype(BF)


def combine_kernel(parts_ref, out_ref):
    rows = out_ref.shape[1]
    lane = lax.broadcasted_iota(jnp.int32, (HD, HD), 1)
    line = lax.broadcasted_iota(jnp.int32, (HD, HD), 0)
    rest = rows - HD
    for h in range(2):
        numer = jnp.zeros((rows, HD), F32)
        packed = jnp.zeros((16, HD), F32)
        for g in range(GRID):
            numer = numer + parts_ref[2 * g + h, :rows, :].astype(F32)
            packed = packed + parts_ref[2 * g + h, rows:, :].astype(F32)
        first = packed[0:1] + packed[2:3]
        second = packed[1:2] + packed[3:4]
        first = jnp.sum(jnp.where(lane == line, first, 0.0), axis=1, keepdims=True)
        second = jnp.sum(
            jnp.where(lane[:rest] == line[:rest], second, 0.0), axis=1, keepdims=True
        )
        part = slice(h * HD, (h + 1) * HD)
        upper = (numer[:HD] / first).astype(BF)
        lower = (numer[HD:] / second).astype(BF)
        for copy in range(GRID):
            out_ref[copy, :HD, part] = upper
            out_ref[copy, HD:, part] = lower


def branch_kernel(place_ref, a_ref, w0, w1, w2, w3, *out_refs):
    for k, out_ref in enumerate(out_refs):
        total = jnp.zeros(out_ref.shape, F32)
        for away, w_ref in enumerate((w0, w1, w2, w3)):
            total = total + jnp.dot(
                a_ref[lax.rem(place_ref[3] + GRID - away, GRID)],
                w_ref[lax.rem(place_ref[2] + k, GRID)],
                preferred_element_type=F32,
            )
        out_ref[...] = total.astype(BF)


def per_device(latents, train_qkv, ema_qkv, q_gain, k_gain, out_weight, modulation, timestep, step):
    rows, width = latents.shape
    channels = ema_qkv.shape[2]
    blocks = GRID * GRID
    by_head = pl.pallas_call(
        average_kernel,
        in_specs=[
            pl.BlockSpec(memory_space=pltpu.SMEM),
            pl.BlockSpec(memory_space=pltpu.VMEM),
            pl.BlockSpec(memory_space=pltpu.VMEM),
        ],
        out_specs=pl.BlockSpec(memory_space=pltpu.VMEM),
        out_shape=jax.ShapeDtypeStruct((2, rows, 3 * HD), BF),
        name="average",
    )(step, ema_qkv, train_qkv)
    full_weights = lax.all_gather(by_head, TOKENS, axis=1, tiled=True)

    place = jnp.stack(
        [lax.axis_index(name).astype(jnp.int32) for name in ("core", "y", "head", "seq")]
    )

    def column(k):
        return lambda i, place: (0, i * GRID + lax.rem(place[3] + k, GRID))

    out_parts = pl.pallas_call(
        pick_kernel,
        grid_spec=pltpu.PrefetchScalarGridSpec(
            num_scalar_prefetch=1,
            grid=(GRID,),
            in_specs=[pl.BlockSpec((channels, width), column(k)) for k in range(GRID)],
            out_specs=[pl.BlockSpec((1, channels, width), lambda i, place: (i, 0, 0))] * GRID,
        ),
        out_shape=[jax.ShapeDtypeStruct((GRID, channels, width), BF)] * GRID,
        name="pick",
    )(place, *([out_weight] * GRID))

    mod_row = lax.dynamic_index_in_dim(modulation, timestep[0], 0, keepdims=False)
    half = rows // 2
    before = lax.ppermute(latents, "head", shift(1))
    after = lax.ppermute(latents, "head", shift(3))
    far_low = lax.ppermute(before[:half], "head", shift(1))
    far_high = lax.ppermute(after[half:], "head", shift(3))
    in_smem = pl.BlockSpec(memory_space=pltpu.SMEM)
    in_vmem = pl.BlockSpec(memory_space=pltpu.VMEM)
    raw = pl.pallas_call(
        spread_kernel,
        in_specs=[in_vmem] * (GRID + 1),
        out_specs=in_vmem,
        out_shape=jax.ShapeDtypeStruct((GRID, GRID, rows, width), BF),
        compiler_params=SPREAD_PARAMS,
        name="spread",
    )(latents, before, far_low, far_high, after)
    raw = lax.all_to_all(raw, "seq", 0, 0, tiled=True)
    out0, out1, out2, out3 = out_parts
    raw, out1, out2, out3 = lax.optimization_barrier((raw, out1, out2, out3))
    out2 = lax.ppermute(out2, "seq", shift(2))
    hidden = pl.pallas_call(
        norm_kernel,
        in_specs=[in_smem, in_vmem, in_vmem],
        out_specs=pl.BlockSpec(memory_space=pltpu.HBM),
        out_shape=jax.ShapeDtypeStruct((rows, blocks * width), BF),
        scratch_shapes=[
            pltpu.VMEM((rows, blocks * width), BF),
            pltpu.SemaphoreType.DMA((rows // 32,)),
        ],
        compiler_params=PARAMS,
        name="norm",
    )(place, raw, mod_row.reshape(3, GRID, GRID, width))
    sibling = lax.ppermute(hidden, "core", [(0, 1), (1, 0)])

    depth = D // GRID
    in_hbm = pl.BlockSpec(memory_space=pltpu.HBM)
    queries, pairs = pl.pallas_call(
        project_kernel,
        in_specs=[in_smem, in_hbm, in_vmem, in_hbm, in_vmem, in_vmem],
        out_specs=[in_vmem, in_vmem],
        out_shape=[
            jax.ShapeDtypeStruct((2, rows, HD), BF),
            jax.ShapeDtypeStruct((GRID, 2, 2, rows, HD), BF),
        ],
        scratch_shapes=[
            pltpu.VMEM((GRID, depth, 3 * HD), BF),
            pltpu.VMEM((GRID, rows, depth), BF),
            pltpu.SemaphoreType.DMA((2 * GRID,)),
        ],
        compiler_params=PARAMS,
        name="project",
    )(
        place,
        pltpu.with_memory_space_constraint(hidden, pltpu.HBM),
        sibling,
        pltpu.with_memory_space_constraint(full_weights, pltpu.HBM),
        q_gain.reshape(1, HD),
        k_gain.reshape(1, HD),
    )

    pairs = lax.all_to_all(pairs, "zl", 0, 0, tiled=True)
    queries = [queries] + [lax.ppermute(queries, "y", shift(k)) for k in (1, 2, 3)]
    *queries, out1, out3 = lax.optimization_barrier((*queries, out1, out3))
    out1 = lax.ppermute(out1, "seq", shift(1))
    out3 = lax.ppermute(out3, "seq", shift(3))

    sent = rows + 16
    parts = pl.pallas_call(
        attend_kernel,
        in_specs=[in_smem] + [in_vmem] * (GRID + 1),
        out_specs=in_vmem,
        out_shape=jax.ShapeDtypeStruct((2 * GRID, sent, HD), BF),
        scratch_shapes=[
            pltpu.VMEM((2 * GRID * rows, HD), BF),
            pltpu.VMEM((2 * GRID * rows, 2 * HD), BF),
        ],
        compiler_params=PARAMS,
        name="attend",
    )(place, *queries, pairs)
    parts, out2 = lax.optimization_barrier((parts, out2))
    parts = lax.all_to_all(parts, ("y", "core"), 0, 0, tiled=True)
    around = pl.pallas_call(
        combine_kernel,
        in_specs=[in_vmem],
        out_specs=in_vmem,
        out_shape=jax.ShapeDtypeStruct((GRID, rows, channels), BF),
        compiler_params=PARAMS,
        name="combine",
    )(parts)
    around = lax.all_to_all(around, "seq", 0, 0, tiled=True)
    outs = pl.pallas_call(
        branch_kernel,
        in_specs=[in_smem] + [in_vmem] * (GRID + 1),
        out_specs=[in_vmem] * GRID,
        out_shape=[jax.ShapeDtypeStruct((rows, width), BF)] * GRID,
        compiler_params=PARAMS,
        name="branch",
    )(place, around, out0, out1, out2, out3)
    shares = [lax.ppermute(outs[k], "head", shift(k)) for k in (2, 1, 3)]
    summed = outs[0].astype(F32)
    for share in shares:
        summed = summed + share.astype(F32)
    position = lax.axis_index(("head", "seq")) * width
    gate = lax.dynamic_slice_in_dim(mod_row[2], position, width, 0)
    return (latents.astype(F32) + gate[None, :] * summed).astype(BF)


def solution(mesh):
    fine = Mesh(
        mesh.devices.reshape(GRID, GRID, 2, GRID, GRID), ("y", "zl", "core", "head", "seq")
    )
    in_specs = (
        P(TOKENS, ("head", "seq")),
        P(None, TOKENS, ("head", "seq")),
        P(None, TOKENS, ("head", "seq")),
        P(),
        P(),
        P(("head", "seq"), None),
        P(),
        P(),
        P(),
    )
    out_specs = P(TOKENS, ("head", "seq"))
    return jax.shard_map(
        per_device, mesh=fine, in_specs=in_specs, out_specs=out_specs, check_vma=False
    )
```

```python
import math

import jax
import jax.numpy as jnp
from jax import lax
from jax.experimental import pallas as pl
from jax.experimental.pallas import tpu as pltpu
from jax.sharding import Mesh
from jax.sharding import PartitionSpec as P

D = 6144
HD = 128
GRID = 4
BF = jnp.bfloat16
F32 = jnp.float32
LOG2E = 1.4426950408889634
TOKENS = ("y", "zl", "core")
PARAMS = pltpu.CompilerParams(vmem_limit_bytes=24 << 20)
SPREAD_PARAMS = pltpu.CompilerParams(vmem_limit_bytes=53 << 20)


def shift(amount):
    return [(i, (i + amount) % GRID) for i in range(GRID)]


def average_kernel(step_ref, ema_ref, train_ref, out_ref):
    stepped = jnp.full((1, HD), step_ref[0], jnp.int32).astype(F32)
    decay = (1.0 + stepped) / (10.0 + stepped)
    for h in range(2):
        for j in range(3):
            part = slice(h * HD, (h + 1) * HD)
            ema = ema_ref[j, :, part].astype(F32)
            train = train_ref[j, :, part].astype(F32)
            out_ref[h, :, j * HD : (j + 1) * HD] = (decay * ema + (1.0 - decay) * train).astype(BF)


def spread_kernel(own_ref, before_ref, low_ref, high_ref, after_ref, out_ref):
    half = low_ref.shape[0]
    for copy in range(GRID):
        out_ref[copy, 0] = own_ref[...]
        out_ref[copy, 1] = before_ref[...]
        out_ref[copy, 2, :half] = low_ref[...]
        out_ref[copy, 2, half:] = high_ref[...]
        out_ref[copy, 3] = after_ref[...]


def norm_kernel(place_ref, raw_ref, mod_ref, sent_ref, out_ref, sems):
    blocks = [(s, k) for s in range(GRID) for k in range(GRID)]
    rows, width = raw_ref.shape[2], raw_ref.shape[3]
    some = 32

    def one_piece(i, carry):
        part = pl.ds(pl.multiple_of(i * some, some), some)
        total = jnp.zeros((some, width), F32)
        for s, k in blocks:
            total = total + raw_ref[s, k, part, :].astype(F32)
        average = jnp.sum(total, axis=1, keepdims=True) * (1.0 / D)
        squares = jnp.zeros((some, width), F32)
        for s, k in blocks:
            centred = raw_ref[s, k, part, :].astype(F32) - average
            squares = squares + centred * centred
        variance = jnp.sum(squares, axis=1, keepdims=True) * (1.0 / D)
        inverse = lax.rsqrt(variance + 1e-06)
        for s, k in blocks:
            h = lax.rem(place_ref[2] + GRID - k, GRID)
            centred = raw_ref[s, k, part, :].astype(F32) - average
            scale = mod_ref[1, h, s : s + 1, :]
            move = mod_ref[0, h, s : s + 1, :]
            start = pl.multiple_of((h * GRID + s) * width, HD)
            out_ref[part, pl.ds(start, width)] = (
                centred * inverse * (1.0 + scale) + move
            ).astype(BF)
        pltpu.make_async_copy(out_ref.at[part], sent_ref.at[part], sems.at[i]).start()
        return carry

    lax.fori_loop(0, rows // some, one_piece, 0)
    for i in range(rows // some):
        part = pl.ds(i * some, some)
        pltpu.make_async_copy(out_ref.at[part], sent_ref.at[part], sems.at[i]).wait()


def pick_kernel(place_ref, *refs):
    for source, target in zip(refs[:GRID], refs[GRID:]):
        target[0] = source[...]


def project_kernel(place_ref, own_ref, other_ref, weight_ref, q_gain_ref, k_gain_ref, q_ref, kv_ref, held, own, sems):
    rows = own_ref.shape[0]
    depth = held.shape[1]
    copies = [
        pltpu.make_async_copy(
            weight_ref.at[place_ref[0], pl.ds(i * depth, depth), :], held.at[i], sems.at[i]
        )
        for i in range(held.shape[0])
    ]
    more = [
        pltpu.make_async_copy(
            own_ref.at[:, pl.ds(i * depth, depth)], own.at[i], sems.at[held.shape[0] + i]
        )
        for i in range(held.shape[0])
    ]
    for first, second in zip(copies, more):
        first.start()
        second.start()
    total = None
    for i, copy in enumerate(copies):
        part = slice(i * depth, (i + 1) * depth)
        more[i].wait()
        hidden = jnp.concatenate([own[i], other_ref[:, part]], axis=0)
        copy.wait()
        product = jnp.dot(hidden, held[i], preferred_element_type=F32)
        total = product if total is None else total + product
    for t in range(2):
        here = slice(t * rows, (t + 1) * rows)
        for j, gain_ref in ((0, q_gain_ref), (1, k_gain_ref)):
            values = total[here, j * HD : (j + 1) * HD]
            squares = jnp.mean(values * values, axis=1, keepdims=True)
            normed = (values * lax.rsqrt(squares + 1e-06) * gain_ref[...]).astype(BF)
            if j == 0:
                q_ref[t] = normed
            else:
                for copy in range(GRID):
                    kv_ref[copy, 0, t] = normed
        values = total[here, 2 * HD :].astype(BF)
        for copy in range(GRID):
            kv_ref[copy, 1, t] = values


def attend_kernel(place_ref, q0, q1, q2, q3, kv_ref, out_ref, k_all, v_all):
    rows = q0.shape[1]
    blocks = 2 * GRID
    for g in range(GRID):
        for t in range(2):
            part = slice((2 * g + t) * rows, (2 * g + t + 1) * rows)
            k_all[part, :] = kv_ref[g, 0, t]
            v_all[part, :HD] = kv_ref[g, 1, t]
    v_all[:, HD:] = jnp.ones((blocks * rows, HD), BF)

    chunk = 512
    lane = lax.broadcasted_iota(jnp.int32, (HD, HD), 1)
    line = lax.broadcasted_iota(jnp.int32, (HD, HD), 0)
    sub = lax.broadcasted_iota(jnp.int32, (16, HD), 0)
    rest = rows - HD
    for k, q_ref in enumerate((q0, q1, q2, q3)):
        queries = jnp.concatenate([q_ref[0], q_ref[1]], axis=0)
        both = jnp.zeros((2 * rows, 2 * HD), F32)
        for c in range(blocks * rows // chunk):
            part = slice(c * chunk, (c + 1) * chunk)
            scores = lax.dot_general(
                queries, k_all[part, :], (((1,), (1,)), ((), ())), preferred_element_type=F32
            )
            weights = jnp.exp2(scores * (LOG2E / math.sqrt(HD))).astype(BF)
            both = both + jnp.dot(weights, v_all[part, :], preferred_element_type=F32)
        for t in range(2):
            target = 2 * lax.rem(place_ref[1] + GRID - k, GRID) + lax.rem(place_ref[0] + t, 2)
            out_ref[target, :rows, :] = both[t * rows : (t + 1) * rows, :HD].astype(BF)
            totals = both[t * rows : (t + 1) * rows, HD:]
            first = jnp.sum(jnp.where(lane == line, totals[:HD], 0.0), axis=0, keepdims=True)
            second = jnp.sum(
                jnp.where(lane[:rest] == line[:rest], totals[HD:], 0.0), axis=0, keepdims=True
            )
            first_high = first.astype(BF).astype(F32)
            second_high = second.astype(BF).astype(F32)
            packed = jnp.where(sub == 0, first_high, 0.0)
            packed = jnp.where(sub == 1, second_high, packed)
            packed = jnp.where(sub == 2, first - first_high, packed)
            packed = jnp.where(sub == 3, second - second_high, packed)
            out_ref[target, rows:, :] = packed.astype(BF)


def combine_kernel(parts_ref, out_ref):
    rows = out_ref.shape[1]
    lane = lax.broadcasted_iota(jnp.int32, (HD, HD), 1)
    line = lax.broadcasted_iota(jnp.int32, (HD, HD), 0)
    rest = rows - HD
    for h in range(2):
        numer = jnp.zeros((rows, HD), F32)
        packed = jnp.zeros((16, HD), F32)
        for g in range(GRID):
            numer = numer + parts_ref[2 * g + h, :rows, :].astype(F32)
            packed = packed + parts_ref[2 * g + h, rows:, :].astype(F32)
        first = packed[0:1] + packed[2:3]
        second = packed[1:2] + packed[3:4]
        first = jnp.sum(jnp.where(lane == line, first, 0.0), axis=1, keepdims=True)
        second = jnp.sum(
            jnp.where(lane[:rest] == line[:rest], second, 0.0), axis=1, keepdims=True
        )
        part = slice(h * HD, (h + 1) * HD)
        upper = (numer[:HD] / first).astype(BF)
        lower = (numer[HD:] / second).astype(BF)
        for copy in range(GRID):
            out_ref[copy, :HD, part] = upper
            out_ref[copy, HD:, part] = lower


def branch_kernel(place_ref, a_ref, w0, w1, w2, w3, *out_refs):
    for k, out_ref in enumerate(out_refs):
        total = jnp.zeros(out_ref.shape, F32)
        for away, w_ref in enumerate((w0, w1, w2, w3)):
            total = total + jnp.dot(
                a_ref[lax.rem(place_ref[3] + GRID - away, GRID)],
                w_ref[lax.rem(place_ref[2] + k, GRID)],
                preferred_element_type=F32,
            )
        out_ref[...] = total.astype(BF)


def per_device(latents, train_qkv, ema_qkv, q_gain, k_gain, out_weight, modulation, timestep, step):
    rows, width = latents.shape
    channels = ema_qkv.shape[2]
    blocks = GRID * GRID
    by_head = pl.pallas_call(
        average_kernel,
        in_specs=[
            pl.BlockSpec(memory_space=pltpu.SMEM),
            pl.BlockSpec(memory_space=pltpu.VMEM),
            pl.BlockSpec(memory_space=pltpu.VMEM),
        ],
        out_specs=pl.BlockSpec(memory_space=pltpu.VMEM),
        out_shape=jax.ShapeDtypeStruct((2, rows, 3 * HD), BF),
        name="average",
    )(step, ema_qkv, train_qkv)
    full_weights = lax.all_gather(by_head, TOKENS, axis=1, tiled=True)

    place = jnp.stack(
        [lax.axis_index(name).astype(jnp.int32) for name in ("core", "y", "head", "seq")]
    )

    def column(k):
        return lambda i, place: (0, i * GRID + lax.rem(place[3] + k, GRID))

    out_parts = pl.pallas_call(
        pick_kernel,
        grid_spec=pltpu.PrefetchScalarGridSpec(
            num_scalar_prefetch=1,
            grid=(GRID,),
            in_specs=[pl.BlockSpec((channels, width), column(k)) for k in range(GRID)],
            out_specs=[pl.BlockSpec((1, channels, width), lambda i, place: (i, 0, 0))] * GRID,
        ),
        out_shape=[jax.ShapeDtypeStruct((GRID, channels, width), BF)] * GRID,
        name="pick",
    )(place, *([out_weight] * GRID))

    mod_row = lax.dynamic_index_in_dim(modulation, timestep[0], 0, keepdims=False)
    half = rows // 2
    before = lax.ppermute(latents, "head", shift(1))
    after = lax.ppermute(latents, "head", shift(3))
    far_low = lax.ppermute(before[:half], "head", shift(1))
    far_high = lax.ppermute(after[half:], "head", shift(3))
    in_smem = pl.BlockSpec(memory_space=pltpu.SMEM)
    in_vmem = pl.BlockSpec(memory_space=pltpu.VMEM)
    raw = pl.pallas_call(
        spread_kernel,
        in_specs=[in_vmem] * (GRID + 1),
        out_specs=in_vmem,
        out_shape=jax.ShapeDtypeStruct((GRID, GRID, rows, width), BF),
        compiler_params=SPREAD_PARAMS,
        name="spread",
    )(latents, before, far_low, far_high, after)
    raw = lax.all_to_all(raw, "seq", 0, 0, tiled=True)
    out0, out1, out2, out3 = out_parts
    raw, out1, out2, out3 = lax.optimization_barrier((raw, out1, out2, out3))
    hidden = pl.pallas_call(
        norm_kernel,
        in_specs=[in_smem, in_vmem, in_vmem],
        out_specs=pl.BlockSpec(memory_space=pltpu.HBM),
        out_shape=jax.ShapeDtypeStruct((rows, blocks * width), BF),
        scratch_shapes=[
            pltpu.VMEM((rows, blocks * width), BF),
            pltpu.SemaphoreType.DMA((rows // 32,)),
        ],
        compiler_params=PARAMS,
        name="norm",
    )(place, raw, mod_row.reshape(3, GRID, GRID, width))
    sibling = lax.ppermute(hidden, "core", [(0, 1), (1, 0)])

    depth = D // GRID
    in_hbm = pl.BlockSpec(memory_space=pltpu.HBM)
    queries, pairs = pl.pallas_call(
        project_kernel,
        in_specs=[in_smem, in_hbm, in_vmem, in_hbm, in_vmem, in_vmem],
        out_specs=[in_vmem, in_vmem],
        out_shape=[
            jax.ShapeDtypeStruct((2, rows, HD), BF),
            jax.ShapeDtypeStruct((GRID, 2, 2, rows, HD), BF),
        ],
        scratch_shapes=[
            pltpu.VMEM((GRID, depth, 3 * HD), BF),
            pltpu.VMEM((GRID, rows, depth), BF),
            pltpu.SemaphoreType.DMA((2 * GRID,)),
        ],
        compiler_params=PARAMS,
        name="project",
    )(
        place,
        pltpu.with_memory_space_constraint(hidden, pltpu.HBM),
        sibling,
        pltpu.with_memory_space_constraint(full_weights, pltpu.HBM),
        q_gain.reshape(1, HD),
        k_gain.reshape(1, HD),
    )

    pairs = lax.all_to_all(pairs, "zl", 0, 0, tiled=True)
    queries = [queries] + [lax.ppermute(queries, "y", shift(k)) for k in (1, 2, 3)]
    *queries, out1, out2, out3 = lax.optimization_barrier((*queries, out1, out2, out3))
    out2 = lax.ppermute(out2, "seq", shift(2))
    out1 = lax.ppermute(out1, "seq", shift(1))
    out3 = lax.ppermute(out3, "seq", shift(3))

    sent = rows + 16
    parts = pl.pallas_call(
        attend_kernel,
        in_specs=[in_smem] + [in_vmem] * (GRID + 1),
        out_specs=in_vmem,
        out_shape=jax.ShapeDtypeStruct((2 * GRID, sent, HD), BF),
        scratch_shapes=[
            pltpu.VMEM((2 * GRID * rows, HD), BF),
            pltpu.VMEM((2 * GRID * rows, 2 * HD), BF),
        ],
        compiler_params=PARAMS,
        name="attend",
    )(place, *queries, pairs)
    parts = lax.all_to_all(parts, ("y", "core"), 0, 0, tiled=True)
    around = pl.pallas_call(
        combine_kernel,
        in_specs=[in_vmem],
        out_specs=in_vmem,
        out_shape=jax.ShapeDtypeStruct((GRID, rows, channels), BF),
        compiler_params=PARAMS,
        name="combine",
    )(parts)
    around = lax.all_to_all(around, "seq", 0, 0, tiled=True)
    outs = pl.pallas_call(
        branch_kernel,
        in_specs=[in_smem] + [in_vmem] * (GRID + 1),
        out_specs=[in_vmem] * GRID,
        out_shape=[jax.ShapeDtypeStruct((rows, width), BF)] * GRID,
        compiler_params=PARAMS,
        name="branch",
    )(place, around, out0, out1, out2, out3)
    shares = [lax.ppermute(outs[k], "head", shift(k)) for k in (2, 1, 3)]
    summed = outs[0].astype(F32)
    for share in shares:
        summed = summed + share.astype(F32)
    position = lax.axis_index(("head", "seq")) * width
    gate = lax.dynamic_slice_in_dim(mod_row[2], position, width, 0)
    return (latents.astype(F32) + gate[None, :] * summed).astype(BF)


def solution(mesh):
    fine = Mesh(
        mesh.devices.reshape(GRID, GRID, 2, GRID, GRID), ("y", "zl", "core", "head", "seq")
    )
    in_specs = (
        P(TOKENS, ("head", "seq")),
        P(None, TOKENS, ("head", "seq")),
        P(None, TOKENS, ("head", "seq")),
        P(),
        P(),
        P(("head", "seq"), None),
        P(),
        P(),
        P(),
    )
    out_specs = P(TOKENS, ("head", "seq"))
    return jax.shard_map(
        per_device, mesh=fine, in_specs=in_specs, out_specs=out_specs, check_vma=False
    )
```
